256 devices in a mesh: dp: 16 (over x, z_hi), mp: 16 (over z_lo, y, core).
Axes of the slice: x: 4, y: 4, z: 8 (z_hi: 4, z_lo: 2; z = z_hi * 2 + z_lo), core: 2. Of those that a mesh axis runs over, the one named last changes fastest.
Arguments:
- features: bfloat16 [16, 320, 128, 128], P('dp', 'mp'), may hold values from -6 to 6
- w_out: bfloat16 [320, 36], P('mp'), may hold values from -0.109375 to 0.109375
- noisy_latent: float32 [16, 4, 128, 128], P('dp', None, 'mp'), may hold values from -6 to 6
- timestep: int32 [16], P('dp'), may hold values from 100 to 699
- w_in: bfloat16 [9, 512, 4], replicated, may hold values from -1 to 1
- b_in: float32 [512], replicated, may hold values from -3 to 3
- w_mid: bfloat16 [9, 512, 512], replicated, may hold values from -0.09375 to 0.09375
- b_mid: float32 [512], replicated, may hold values from -3 to 3
- reward_head: float32 [512], replicated, may hold values from -6 to 6
Outputs:
- feature_grads: bfloat16 [16, 320, 128, 128], P('dp', 'mp')
- weight_grad: float32 [320, 36], P('mp')
The draws below stay inside these ranges and needn't reach their ends.
All inputs are finite; a program needn't handle non-finite values.
Results may differ from the reference program's by a relative error of at most 0.012.
Values may be sent and summed in bfloat16 or wider, within the bound.
A program may use at most 128 MiB of HBM per device.

```python
import jax
import jax.numpy as jnp
from jax import lax

CU = 320
CD = 512
LAT = 4
CROP = 128
W = 128
IMAGES = 16


def with_ends(drawn, stream_key, least, top_value):
    shape = drawn.shape
    spot = [jax.random.randint(jax.random.fold_in(stream_key, axis), (), 0, shape[axis]) for axis in range(len(shape))]
    drawn = drawn.at[tuple(spot)].set(least)
    longest = shape.index(max(shape))
    spot[longest] = (spot[longest] + 1) % shape[longest]
    return drawn.at[tuple(spot)].set(top_value)


def shard_levels(rng, shape, shards, least, largest):
    def one(dim, blocks):
        steps = jax.random.uniform(jax.random.fold_in(jax.random.fold_in(rng, 6), dim), (blocks,), jnp.float32, least / len(shards), largest / len(shards))
        return jnp.repeat(jnp.exp(steps), shape[dim] // blocks).reshape((-1,) + (1,) * (len(shape) - dim - 1))

    gain = one(*shards[0])
    for cut in shards[1:]:
        gain = gain * one(*cut)
    return gain


def noise(rng, shape, spread, reach, split=(), kind=jnp.bfloat16):
    factor_of = shard_levels(rng, shape, split, -0.22, 0.18) if split else 1.0
    array = jax.random.normal(rng, shape, jnp.float32) * spread * factor_of
    return jnp.minimum(jnp.maximum(array, -reach), reach).astype(kind)


def setup_inputs(seed: int = 0) -> dict:
    key_of = jax.random.split(jax.random.key(seed), 10)
    return {
        "features": noise(key_of[0], (IMAGES, CU, CROP, W), 1.0, 6.0, ((0, 16), (1, 16))),
        "w_out": noise(key_of[1], (CU, 9 * LAT), (9 * CU) ** -0.5, 0.109375, ((0, 16),)),
        "noisy_latent": noise(key_of[2], (IMAGES, LAT, CROP, W), 1.0, 6.0, ((0, 16), (2, 16)), jnp.float32),
        "timestep": with_ends(jax.random.randint(key_of[3], (IMAGES,), 100, 700), jax.random.fold_in(key_of[3], 1), 100, 699).astype(jnp.int32),
        "w_in": noise(key_of[4], (9, CD, LAT), (9 * LAT) ** -0.5, 1.0),
        "b_in": noise(key_of[5], (CD,), 0.5, 3.0, (), jnp.float32),
        "w_mid": noise(key_of[6], (9, CD, CD), (9 * CD) ** -0.5, 0.09375),
        "b_mid": noise(key_of[7], (CD,), 0.5, 3.0, (), jnp.float32),
        "reward_head": noise(key_of[8], (CD,), 1.0, 6.0, (), jnp.float32),
    }


def noise_levels(timestep):
    betas = jnp.linspace(0.00085 ** 0.5, 0.012 ** 0.5, 1000, dtype=jnp.float32) ** 2
    table = jnp.cumprod(1.0 - betas).astype(jnp.float32)
    hits = jnp.arange(1000, dtype=jnp.int32)[None, :] == timestep[:, None]
    return lax.optimization_barrier(jnp.sum(jnp.where(hits, table[None, :], jnp.float32(0.0)), axis=1))

def pad_both(source):
    return jnp.pad(source, ((0, 0), (1, 1), (1, 1)))

def slope(value):
    sig = jax.nn.sigmoid(value)
    return sig * (1.0 + value * (1.0 - sig))

def conv_taps(padded, kernel, out_rows, out_cols):
    summed = jnp.zeros((kernel.shape[1], out_rows * out_cols), jnp.float32)
    for tap in range(9):
        tap_row, tap_col = (tap // 3, tap % 3)
        window = padded[:, tap_row:tap_row + out_rows, tap_col:tap_col + out_cols].reshape(padded.shape[0], -1)
        summed = summed + jnp.dot(kernel[tap], window, preferred_element_type=jnp.float32)
    return summed.reshape(kernel.shape[1], out_rows, out_cols)

def conv_back(padded, kernel, out_rows, out_cols):
    summed = jnp.zeros((kernel.shape[2], out_rows * out_cols), jnp.float32)
    for tap in range(9):
        tap_row, tap_col = (tap // 3, tap % 3)
        window = padded[:, 2 - tap_row:2 - tap_row + out_rows, 2 - tap_col:2 - tap_col + out_cols].reshape(padded.shape[0], -1)
        summed = summed + jnp.dot(kernel[tap].T, window, preferred_element_type=jnp.float32)
    return summed.reshape(kernel.shape[2], out_rows, out_cols)

def weight_taps(padded, noise_grad, out_rows, out_cols):
    flat = noise_grad.reshape(noise_grad.shape[0], -1)
    parts = []
    for tap in range(9):
        tap_row, tap_col = (tap // 3, tap % 3)
        window = padded[:, tap_row:tap_row + out_rows, tap_col:tap_col + out_cols].reshape(padded.shape[0], -1)
        parts.append(jnp.dot(window, flat.T, preferred_element_type=jnp.float32))
    return jnp.concatenate(parts, axis=1)

def reference(features, w_out, noisy_latent, timestep, w_in, b_in, w_mid, b_mid, reward_head):
    channels = features.shape[1]
    lat_chans = noisy_latent.shape[1]
    crop_rows, col_count = (features.shape[2], features.shape[3])
    eps_kernel = jnp.transpose(w_out.reshape(channels, 9, lat_chans), (1, 2, 0))
    noise_level = noise_levels(timestep)
    root_a = jnp.sqrt(noise_level)
    root_b = jnp.sqrt(1.0 - noise_level)

    def one_image(packed):
        feats, noisy, coef_a, coef_b = packed
        feat_pad = pad_both(feats)
        eps = conv_taps(feat_pad, eps_kernel, crop_rows, col_count)
        latent = ((noisy - coef_b * eps) / coef_a).astype(jnp.bfloat16)
        hidden_pre = conv_taps(pad_both(latent), w_in, crop_rows, col_count) + b_in[:, None, None]
        hidden_act = jax.nn.silu(hidden_pre).astype(jnp.bfloat16)
        mixed_pre = conv_taps(pad_both(hidden_act), w_mid, crop_rows, col_count) + b_mid[:, None, None]
        mixed_grad = (reward_head[:, None, None] * slope(mixed_pre)).astype(jnp.bfloat16)
        act_grad = conv_back(pad_both(mixed_grad), w_mid, crop_rows, col_count)
        hidden_grad = (act_grad * slope(hidden_pre)).astype(jnp.bfloat16)
        latent_grad = conv_back(pad_both(hidden_grad), w_in, crop_rows, col_count)
        noise_grad = (-(coef_b / coef_a) * latent_grad).astype(jnp.bfloat16)
        feat_grads = conv_back(pad_both(noise_grad), eps_kernel, crop_rows, col_count).astype(jnp.bfloat16)
        return (feat_grads, weight_taps(feat_pad, noise_grad, crop_rows, col_count))
    feature_grads, weight_parts = lax.map(one_image, (features, noisy_latent, root_a, root_b))
    weight_grad = lax.optimization_barrier(jnp.sum(weight_parts, axis=0)) / (crop_rows * col_count)
    return (feature_grads, weight_grad)
```

```python
import jax
import jax.numpy as jnp
import numpy as np
from jax import lax
from jax.experimental import pallas as pl
from jax.experimental.pallas import tpu as pltpu
from jax.sharding import PartitionSpec as P

F32 = jnp.float32
BF16 = jnp.bfloat16
MESH = pl.DeviceIdType.MESH
N = 16
STRIDE = 136
NT = (((1,), (1,)), ((), ()))
VM = pl.BlockSpec(memory_space=pltpu.VMEM)


def noise_table():
    betas = np.linspace(0.00085**0.5, 0.012**0.5, 1000, dtype=np.float32) ** 2
    table = np.cumprod((1.0 - betas).astype(np.float32), dtype=np.float32)
    return np.pad(table, (0, 24)).reshape(8, 128)


def dot(a, b):
    return jnp.dot(a, b, preferred_element_type=F32)


def dot_nt(a, b):
    return lax.dot_general(a, b, NT, preferred_element_type=F32)


def right(v):
    lane = lax.broadcasted_iota(jnp.int32, v.shape, 1)
    return jnp.where(lane == 0, 0.0, pltpu.roll(v, 1, 1))


def left(v):
    lane = lax.broadcasted_iota(jnp.int32, v.shape, 1)
    return jnp.where(lane == 127, 0.0, pltpu.roll(v, 127, 1))


def sigmoid(v):
    return 0.5 * jnp.tanh(0.5 * v) + 0.5


def latent_kernel(feat, e48, noisy, tstep, table, lat_out, f2, coef_out,
                  stage, rs, eacc, nz, eloc, recv, send_sem, recv_sem):
    me = lax.axis_index("mp")
    barrier = pltpu.get_barrier_semaphore()

    def greet(j, c):
        pl.semaphore_signal(barrier, inc=1, device_id={"mp": lax.rem(me + j, N)}, device_id_type=MESH)
        return c

    lax.fori_loop(1, N, greet, 0)

    idx = lax.broadcasted_iota(jnp.int32, (8, 128), 0) * 128 + lax.broadcasted_iota(jnp.int32, (8, 128), 1)
    level = jnp.sum(jnp.where(idx == tstep[0], table[...], 0.0), keepdims=True)
    ra = jnp.sqrt(level)
    rb = jnp.sqrt(1.0 - level)
    ratio = rb / ra
    coef_out[...] = jnp.broadcast_to(-ratio, (8, 128))

    for c in range(20):
        stage[c * STRIDE : c * STRIDE + 128, :] = feat[0, c].astype(F32)
    for c in range(20, 24):
        stage[c * STRIDE : c * STRIDE + 128, :] = jnp.zeros((128, 128), F32)
    zero8 = jnp.zeros((8, 128), F32)
    rs[0:16, :] = jnp.zeros((16, 128), F32)
    rs[129 * 16 : 130 * 16, :] = jnp.zeros((16, 128), F32)

    def rows(b, c):
        parts = []
        for i in range(8):
            v = stage[pl.ds(b * 8 + i, 24, stride=STRIDE), :]
            parts.append(jnp.concatenate([v, zero8], axis=0).astype(BF16))
        block = jnp.concatenate(parts, axis=1)
        f2[:, pl.ds(pl.multiple_of(b * 1024, 1024), 1024)] = block
        p = dot(e48[...], block)
        for i in range(8):
            q = p[:, i * 128 : (i + 1) * 128]
            r = q[16:32] + right(q[0:16]) + left(q[32:48])
            rs[pl.ds(pl.multiple_of((b * 8 + i + 1) * 16, 16), 16), :] = r
        return c

    lax.fori_loop(0, 16, rows, 0)

    for o in range(4):
        nz[pl.ds(o, 8, stride=4), :] = noisy[0, o]
    eacc[0:16, :] = jnp.zeros((16, 128), F32)
    eacc[528:544, :] = jnp.zeros((16, 128), F32)
    low = lax.broadcasted_iota(jnp.int32, (8, 128), 0) < 4

    def pairs(b, c):
        def at(y, half):
            return rs[pl.ds(pl.multiple_of((y + 1) * 16 + 8 * half, 8), 8), :]

        y = 2 * b
        e = at(y + 1, 0)
        e += jnp.where(low, pltpu.roll(at(y, 0), 4, 0), pltpu.roll(at(y, 1), 4, 0))
        e += jnp.where(low, at(y - 1, 1), pltpu.roll(at(y + 2, 0), 4, 0))
        eacc[pl.ds(pl.multiple_of(16 + 8 * b, 8), 8), :] = -ratio * e
        return c

    lax.fori_loop(0, 64, pairs, 0, unroll=4)
    mine = pl.ds(pl.multiple_of(16 + 32 * me, 16), 32)
    eacc[mine, :] = eacc[mine, :] + nz[...] / ra
    eloc[...] = eacc[...].astype(BF16)

    pl.semaphore_wait(barrier, N - 1)

    def copy(dest, sem, slot):
        return pltpu.make_async_remote_copy(
            src_ref=eloc.at[pl.ds(pl.multiple_of(32 * dest, 32), 64), :],
            dst_ref=recv.at[slot],
            send_sem=send_sem.at[sem],
            recv_sem=recv_sem.at[slot],
            device_id={"mp": dest},
            device_id_type=MESH,
        )

    def send(j, c):
        copy(lax.rem(me + j, N), j, j).start()
        return c

    lax.fori_loop(1, N, send, 0)
    total = eacc[pl.ds(pl.multiple_of(32 * me, 32), 64), :]

    def take(j, acc):
        copy(lax.rem(me + j, N), j, j).wait_recv()
        return acc + recv[j].astype(F32)

    total = lax.fori_loop(1, N, take, total)
    lat_out[...] = total.astype(BF16)

    def done(j, c):
        copy(lax.rem(me + j, N), j, j).wait_send()
        return c

    lax.fori_loop(1, N, done, 0)


def decoder_kernel(lat, coef, w48, b_in, wmid, b_mid, head, out,
                   wbuf, ls, h3, s1, m3, rg, sem):
    me = lax.axis_index("mp")
    copies = [pltpu.make_async_copy(wmid.at[pl.ds(3 * i, 3)], wbuf.at[pl.ds(3 * i, 3)], sem.at[i]) for i in range(3)]
    for c in copies:
        c.start()
    v = lat[...].astype(F32)
    for i, t in enumerate((right(v), v, left(v))):
        ls[i, 0:64, :] = t
        ls[i, 64:72, :] = jnp.zeros((8, 128), F32)
    edge = lax.broadcasted_iota(jnp.int32, (128, 512), 0)
    first, last = edge == 0, edge == 127

    def spread(dst, r, val, down, up):
        at = pl.ds(pl.multiple_of(r * 128, 128), 128)
        dst[at, down * 512 : down * 512 + 512] = jnp.where(first, 0.0, pltpu.roll(val, 1, 0)).astype(BF16)
        dst[at, 512:1024] = val.astype(BF16)
        dst[at, up * 512 : up * 512 + 512] = jnp.where(last, 0.0, pltpu.roll(val, 127, 0)).astype(BF16)

    def hidden(r, c):
        at = pl.ds(4 * r, 16)
        x48 = jnp.concatenate([ls[0, at, :], ls[1, at, :], ls[2, at, :]], axis=0)
        pre = dot(x48.T.astype(BF16), w48[...]) + b_in[...]
        sg = sigmoid(pre)
        row = 8 * me - 3 + r
        inside = jnp.logical_and(row >= 0, row < 128)
        act = jnp.where(inside, pre * sg, 0.0)
        s1[pl.ds(pl.multiple_of(r * 128, 128), 128), :] = sg * (1.0 + pre * (1.0 - sg))
        spread(h3, r, act, 0, 2)
        return c

    lax.fori_loop(0, 14, hidden, 0)
    for c in copies:
        c.wait()

    def mixed(b, c):
        acc = jnp.broadcast_to(b_mid[...], (512, 512))
        for ky in range(3):
            for kx in range(3):
                a = h3[pl.ds(pl.multiple_of((b * 4 + ky) * 128, 128), 512), kx * 512 : kx * 512 + 512]
                acc = acc + dot_nt(a, wbuf[3 * ky + kx])
        for i in range(4):
            pre = acc[i * 128 : (i + 1) * 128]
            sg = sigmoid(pre)
            r = b * 4 + i
            row = 8 * me - 2 + r
            inside = jnp.logical_and(row >= 0, row < 128)
            g = jnp.where(inside, head[...] * (sg * (1.0 + pre * (1.0 - sg))), 0.0)
            spread(m3, r, g, 2, 0)
        return c

    lax.fori_loop(0, 3, mixed, 0)

    def hgrad(b, c):
        acc = jnp.zeros((640, 512), F32)
        for ky in range(3):
            a = m3[pl.ds(pl.multiple_of((b * 5 + 2 - ky) * 128, 128), 640), :]
            acc = acc + dot(a, wbuf[3 * ky : 3 * ky + 3].reshape(1536, 512))
        for i in range(5):
            r = b * 5 + i
            row = 8 * me - 1 + r
            inside = jnp.logical_and(row >= 0, row < 128)
            g = acc[i * 128 : (i + 1) * 128] * s1[pl.ds(pl.multiple_of((r + 2) * 128, 128), 128), :]
            g = jnp.where(inside, g, 0.0).astype(BF16)
            q = dot_nt(w48[...], g)
            rg[pl.ds(pl.multiple_of(r * 16, 16), 16), :] = q[16:32] + left(q[0:16]) + right(q[32:48])
        return c

    lax.fori_loop(0, 2, hgrad, 0)
    ratio = coef[0:1, :]
    for r in range(8):
        g = rg[(r + 2) * 16 : (r + 2) * 16 + 4] + rg[(r + 1) * 16 + 4 : (r + 1) * 16 + 8]
        g = g + rg[r * 16 + 8 : r * 16 + 12]
        ls[0, 4 * r : 4 * r + 4, :] = g * ratio
    out[...] = ls[0, 0:32, :].astype(BF16)


def grads_kernel(ng, f2, e48t, fg_out, wg_out, recv, ns, im, stage, wrecv, send_sem, recv_sem, wsend_sem, wrecv_sem):
    me = lax.axis_index("mp")
    my_dp = lax.axis_index("dp")
    barrier = pltpu.get_barrier_semaphore()

    def greet(j, c):
        pl.semaphore_signal(barrier, inc=1, device_id={"mp": lax.rem(me + j, N)}, device_id_type=MESH)
        pl.semaphore_signal(barrier, inc=1, device_id={"dp": lax.rem(my_dp + j, N)}, device_id_type=MESH)
        return c

    lax.fori_loop(1, N, greet, 0)
    recv[me] = ng[...]
    pl.semaphore_wait(barrier, 2 * (N - 1))

    def copy(peer, slot):
        return pltpu.make_async_remote_copy(
            src_ref=ng,
            dst_ref=recv.at[slot],
            send_sem=send_sem.at[peer],
            recv_sem=recv_sem.at[slot],
            device_id={"mp": peer},
            device_id_type=MESH,
        )

    def send(j, c):
        copy(lax.rem(me + j, N), me).start()
        return c

    lax.fori_loop(1, N, send, 0)
    ns[:, 0:8, :] = jnp.zeros((3, 8, 128), F32)
    ns[:, 512:528, :] = jnp.zeros((3, 16, 128), F32)

    def take(j, c):
        peer = lax.rem(me + j, N)
        copy(peer, peer).wait_recv()
        return c

    lax.fori_loop(1, N, take, 0)

    def shift(s, c):
        v = recv[s].astype(F32)
        at = pl.ds(4 + 32 * s, 32)
        ns[0, at, :] = left(v)
        ns[1, at, :] = v
        ns[2, at, :] = right(v)
        return c

    lax.fori_loop(0, N, shift, 0)

    def columns(b, acc):
        parts = []
        for i in range(8):
            at = pl.ds(4 * (b * 8 + i), 16)
            parts.append(jnp.concatenate([ns[k, at, :].astype(BF16) for k in range(3)], axis=0))
        block = jnp.concatenate(parts, axis=1)
        at = pl.ds(pl.multiple_of(b * 1024, 1024), 1024)
        im[:, at] = block
        return acc + dot_nt(f2[:, at], block)

    wg = lax.fori_loop(0, 16, columns, jnp.zeros((32, 48), F32))
    wg = jnp.concatenate([wg[0:24], jnp.zeros((24, 80), F32)], axis=1)
    lane = lax.broadcasted_iota(jnp.int32, (24, 128), 1)
    ordered = jnp.zeros((24, 128), F32)
    for k in range(9):
        ky, kx = divmod(k, 3)
        src = kx * 16 + (2 - ky) * 4
        moved = pltpu.roll(wg, (4 * k - src) % 128, 1)
        ordered = jnp.where(jnp.logical_and(lane >= 4 * k, lane < 4 * k + 4), moved, ordered)
    packed = ordered[0:8] + pltpu.roll(ordered[8:16], 40, 1) + pltpu.roll(ordered[16:24], 80, 1)
    wrecv[my_dp] = packed

    def wcopy(peer, slot):
        return pltpu.make_async_remote_copy(
            src_ref=wrecv.at[my_dp],
            dst_ref=wrecv.at[slot],
            send_sem=wsend_sem.at[peer],
            recv_sem=wrecv_sem.at[slot],
            device_id={"dp": peer},
            device_id_type=MESH,
        )

    def wsend(j, c):
        wcopy(lax.rem(my_dp + j, N), my_dp).start()
        return c

    lax.fori_loop(1, N, wsend, 0)

    def feature(b, c):
        p = dot(e48t[...], im[:, pl.ds(pl.multiple_of(b * 1024, 1024), 1024)])
        for i in range(8):
            stage[pl.ds(b * 8 + i, 24, stride=STRIDE), :] = p[0:24, i * 128 : (i + 1) * 128]
        return c

    lax.fori_loop(0, 16, feature, 0)
    for ch in range(20):
        fg_out[0, ch] = stage[ch * STRIDE : ch * STRIDE + 128, :].astype(BF16)

    def wtake(j, c):
        peer = lax.rem(my_dp + j, N)
        wcopy(peer, peer).wait_recv()
        return c

    lax.fori_loop(1, N, wtake, 0)
    total = wrecv[0]
    for s in range(1, N):
        total = total + wrecv[s]
    total = total * (1.0 / 16384.0)
    wg_out[0:8, :] = total[:, 0:36]
    wg_out[8:16, :] = pltpu.roll(total, 88, 1)[:, 0:36]
    wg_out[16:20, :] = pltpu.roll(total, 48, 1)[0:4, 0:36]

    def done(j, c):
        copy(lax.rem(me + j, N), me).wait_send()
        wcopy(lax.rem(my_dp + j, N), my_dp).wait_send()
        return c

    lax.fori_loop(1, N, done, 0)


def body(features, w_out, noisy_latent, timestep, w_in, b_in, w_mid, b_mid, reward_head):
    e = w_out.reshape(20, 3, 3, 4)[:, ::-1].transpose(0, 2, 1, 3).reshape(20, 3, 12)
    e48t = jnp.pad(e, ((0, 12), (0, 0), (0, 4))).reshape(32, 48)
    e48 = e48t.T
    w = w_in.reshape(3, 3, 512, 4).transpose(1, 0, 3, 2).reshape(3, 12, 512)
    w48 = jnp.pad(w, ((0, 0), (0, 4), (0, 0))).reshape(48, 512)

    lat, f2, coef = pl.pallas_call(
        latent_kernel,
        out_shape=(
            jax.ShapeDtypeStruct((64, 128), BF16),
            jax.ShapeDtypeStruct((32, 16384), BF16),
            jax.ShapeDtypeStruct((8, 128), F32),
        ),
        in_specs=[VM, VM, VM, pl.BlockSpec(memory_space=pltpu.SMEM), VM],
        out_specs=(VM, VM, VM),
        scratch_shapes=[
            pltpu.VMEM((24 * STRIDE, 128), F32),
            pltpu.VMEM((130 * 16, 128), F32),
            pltpu.VMEM((544, 128), F32),
            pltpu.VMEM((32, 128), F32),
            pltpu.VMEM((544, 128), BF16),
            pltpu.VMEM((N, 64, 128), BF16),
            pltpu.SemaphoreType.DMA((N,)),
            pltpu.SemaphoreType.DMA((N,)),
        ],
        compiler_params=pltpu.CompilerParams(collective_id=0, has_side_effects=True, vmem_limit_bytes=24 << 20),
        name="latent",
    )(features, e48, noisy_latent, timestep, jnp.asarray(noise_table()))

    ng = pl.pallas_call(
        decoder_kernel,
        out_shape=jax.ShapeDtypeStruct((32, 128), BF16),
        in_specs=[VM, VM, VM, VM, pl.BlockSpec(memory_space=pl.ANY), VM, VM],
        out_specs=VM,
        scratch_shapes=[
            pltpu.VMEM((9, 512, 512), BF16),
            pltpu.VMEM((3, 72, 128), F32),
            pltpu.VMEM((14 * 128, 1536), BF16),
            pltpu.VMEM((14 * 128, 512), F32),
            pltpu.VMEM((12 * 128, 1536), BF16),
            pltpu.VMEM((160, 128), F32),
            pltpu.SemaphoreType.DMA((3,)),
        ],
        compiler_params=pltpu.CompilerParams(vmem_limit_bytes=48 << 20),
        name="decoder",
    )(lat, coef, w48, b_in.reshape(1, 512), w_mid, b_mid.reshape(1, 512), reward_head.reshape(1, 512))

    return pl.pallas_call(
        grads_kernel,
        out_shape=(
            jax.ShapeDtypeStruct((1, 20, 128, 128), BF16),
            jax.ShapeDtypeStruct((20, 36), F32),
        ),
        in_specs=[VM, VM, VM],
        out_specs=(VM, VM),
        scratch_shapes=[
            pltpu.VMEM((N, 32, 128), BF16),
            pltpu.VMEM((3, 528, 128), F32),
            pltpu.VMEM((48, 16384), BF16),
            pltpu.VMEM((24 * STRIDE, 128), F32),
            pltpu.VMEM((N, 8, 128), F32),
            pltpu.SemaphoreType.DMA((N,)),
            pltpu.SemaphoreType.DMA((N,)),
            pltpu.SemaphoreType.DMA((N,)),
            pltpu.SemaphoreType.DMA((N,)),
        ],
        compiler_params=pltpu.CompilerParams(collective_id=1, has_side_effects=True, vmem_limit_bytes=24 << 20),
        name="grads",
    )(ng, f2, e48t)


def solution(mesh):
    in_specs = (
        P("dp", "mp", None, None),
        P("mp", None),
        P("dp", None, "mp", None),
        P("dp"),
        P(),
        P(),
        P(),
        P(),
        P(),
    )
    out_specs = (P("dp", "mp", None, None), P("mp", None))
    return jax.shard_map(body, mesh=mesh, in_specs=in_specs, out_specs=out_specs, check_vma=False)
```

```python
import jax
import jax.numpy as jnp
import numpy as np
from jax import lax
from jax.experimental import pallas as pl
from jax.experimental.pallas import tpu as pltpu
from jax.sharding import PartitionSpec as P

F32 = jnp.float32
BF16 = jnp.bfloat16
MESH = pl.DeviceIdType.MESH
N = 16
STRIDE = 136
CHUNK = 1024
NT = (((1,), (1,)), ((), ()))


def noise_table():
    betas = np.linspace(0.00085**0.5, 0.012**0.5, 1000, dtype=np.float32) ** 2
    table = np.cumprod((1.0 - betas).astype(np.float32), dtype=np.float32)
    return np.pad(table, (0, 24)).reshape(8, 128)


def iota(shape, dim):
    return lax.broadcasted_iota(jnp.int32, shape, dim)


def dot(a, b):
    return jnp.dot(a, b, preferred_element_type=F32)


def dot_nt(a, b):
    return lax.dot_general(a, b, NT, preferred_element_type=F32)


def right(v):
    return jnp.where(iota(v.shape, 1) == 0, 0.0, pltpu.roll(v, 1, 1))


def left(v):
    return jnp.where(iota(v.shape, 1) == 127, 0.0, pltpu.roll(v, 127, 1))


def rows(start, size):
    return pl.ds(pl.multiple_of(start, size), size)


def each(lo, hi, step):
    def run(j, c):
        step(j)
        return c

    lax.fori_loop(lo, hi, run, 0)


def kernel(
    feat, w_out, noisy, tstep, table, w_in, b_in, w_mid, b_mid, head,
    fg_out, wg_out,
    fbuf, wobuf, nbuf, tbuf, tabbuf, wibuf, bibuf, wmbuf, bmbuf, hbuf,
    stage, f2, rs, eacc, nz, eloc, recv, e48, e48t, w48, ls,
    h3, s1, m3, gacc, lacc, ngblk, grecv, ns, im, fgb, wgb, wrecv,
    in_sem, out_sem, send_sem, recv_sem, gsend_sem, grecv_sem, wsend_sem, wrecv_sem,
):
    me = lax.axis_index("mp")
    my_dp = lax.axis_index("dp")
    pairs = ((feat, fbuf), (w_out, wobuf), (noisy, nbuf), (tstep, tbuf), (table, tabbuf),
             (w_in, wibuf), (b_in, bibuf), (b_mid, bmbuf), (head, hbuf), (w_mid, wmbuf))
    loads = [pltpu.make_async_copy(src, dst, in_sem.at[i]) for i, (src, dst) in enumerate(pairs)]
    for copy in loads:
        copy.start()
    barrier = pltpu.get_barrier_semaphore()

    def greet(j):
        pl.semaphore_signal(barrier, inc=1, device_id={"mp": lax.rem(me + j, N)}, device_id_type=MESH)
        pl.semaphore_signal(barrier, inc=1, device_id={"dp": lax.rem(my_dp + j, N)}, device_id_type=MESH)

    each(1, N, greet)

    for copy in loads[1:5]:
        copy.wait()
    level = jnp.sum(
        jnp.where(iota((8, 128), 0) * 128 + iota((8, 128), 1) == tbuf[0], tabbuf[...], 0.0), keepdims=True
    )
    root_a = jnp.sqrt(level)
    root_b = jnp.sqrt(1.0 - level)
    ratio = root_b / root_a

    def tap_column(b):
        j = lax.shift_right_logical(b, 2) & 3
        k = 3 * (2 - j) + lax.shift_right_logical(b, 4)
        return jnp.where(j < 3, 4 * k + (b & 3), -1)

    pick = jnp.where(iota((36, 48), 0) == tap_column(iota((36, 48), 1)), 1.0, 0.0).astype(BF16)
    pick_t = jnp.where(iota((48, 36), 1) == tap_column(iota((48, 36), 0)), 1.0, 0.0).astype(BF16)
    e48t[...] = jnp.zeros((32, 48), F32)
    e48t[0:20, :] = dot(wobuf[...], pick)
    e48[...] = jnp.zeros((48, 32), F32)
    e48[:, 0:20] = dot_nt(pick_t, wobuf[...])

    loads[0].wait()
    for c in range(20):
        stage[c * STRIDE : c * STRIDE + 128, :] = fbuf[0, c].astype(F32)
    for c in range(20, 24):
        stage[c * STRIDE : c * STRIDE + 128, :] = jnp.zeros((128, 128), F32)
    rs[0:16, :] = jnp.zeros((16, 128), F32)
    rs[129 * 16 : 130 * 16, :] = jnp.zeros((16, 128), F32)
    e_rows = e48[...].astype(BF16)

    def unet_rows(b):
        parts = []
        for i in range(CHUNK // 128):
            v = stage[pl.ds(b * (CHUNK // 128) + i, 24, stride=STRIDE), :]
            parts.append(jnp.concatenate([v, jnp.zeros((8, 128), F32)], axis=0).astype(BF16))
        block = jnp.concatenate(parts, axis=1)
        f2[:, rows(b * CHUNK, CHUNK)] = block
        p = dot(e_rows, block)
        for i in range(CHUNK // 128):
            q = p[:, i * 128 : (i + 1) * 128]
            y = b * (CHUNK // 128) + i
            rs[rows((y + 1) * 16, 16), :] = q[16:32] + right(q[0:16]) + left(q[32:48])

    each(0, 16384 // CHUNK, unet_rows)

    for o in range(4):
        nz[pl.ds(o, 8, stride=4), :] = nbuf[0, o]
    eacc[0:8, :] = jnp.zeros((8, 128), F32)
    eacc[520:528, :] = jnp.zeros((8, 128), F32)
    low = iota((8, 128), 0) < 4

    def unet_pairs(b):
        def at(y, half):
            return rs[rows((y + 1) * 16 + 8 * half, 8), :]

        for i in range(4):
            y = 8 * b + 2 * i
            e = at(y + 1, 0)
            e += jnp.where(low, pltpu.roll(at(y, 0), 4, 0), pltpu.roll(at(y, 1), 4, 0))
            e += jnp.where(low, at(y - 1, 1), pltpu.roll(at(y + 2, 0), 4, 0))
            eacc[rows(8 + 4 * y, 8), :] = -ratio * e

    each(0, 16, unet_pairs)
    mine = pl.ds(pl.multiple_of(8 + 32 * me, 8), 32)
    eacc[mine, :] = eacc[mine, :] + nz[...] / root_a
    eloc[...] = eacc[...].astype(BF16)

    def lat_copy(dest, slot):
        return pltpu.make_async_remote_copy(
            src_ref=eloc.at[pl.ds(pl.multiple_of(32 * dest, 32), 48), :],
            dst_ref=recv.at[slot],
            send_sem=send_sem.at[slot],
            recv_sem=recv_sem.at[slot],
            device_id={"mp": dest},
            device_id_type=MESH,
        )

    pl.semaphore_wait(barrier, 2 * (N - 1))
    each(1, N, lambda j: lat_copy(lax.rem(me + j, N), j).start())

    loads[5].wait()
    loads[6].wait()
    w_rows = jnp.zeros((48, 512), F32)
    for k in range(9):
        ky, kx = divmod(k, 3)
        put = jnp.where(iota((48, 4), 0) == kx * 16 + ky * 4 + iota((48, 4), 1), 1.0, 0.0).astype(BF16)
        w_rows = w_rows + dot_nt(put, wibuf[k])
    w48[...] = w_rows.astype(BF16)
    for copy in loads[7:]:
        copy.wait()

    total = eacc[pl.ds(pl.multiple_of(32 * me, 32), 48), :]

    def lat_take(j, acc):
        lat_copy(lax.rem(me + j, N), j).wait_recv()
        return acc + recv[j].astype(F32)

    total = lax.fori_loop(1, N, lat_take, total)

    lat = total.astype(BF16).astype(F32)
    for i, t in enumerate((right(lat), lat, left(lat))):
        ls[i, 0:48, :] = t
        ls[i, 48:56, :] = jnp.zeros((8, 128), F32)
    edge = iota((128, 512), 0)
    first, last = edge == 0, edge == 127

    def spread(dst, r, val, down, up):
        at = rows(r * 128, 128)
        dst[at, down * 512 : down * 512 + 512] = jnp.where(first, 0.0, pltpu.roll(val, 1, 0)).astype(BF16)
        dst[at, 512:1024] = val.astype(BF16)
        dst[at, up * 512 : up * 512 + 512] = jnp.where(last, 0.0, pltpu.roll(val, 127, 0)).astype(BF16)

    def hidden(r):
        at = pl.ds(4 * r, 16)
        x48 = jnp.concatenate([ls[0, at, :], ls[1, at, :], ls[2, at, :]], axis=0)
        pre = dot(x48.T.astype(BF16), w48[...]) + bibuf[...]
        row = 8 * me - 1 + r
        half = jnp.where(jnp.logical_and(row >= 0, row < 128), 0.5, 0.0)
        sig = half * jnp.tanh(0.5 * pre) + half
        act = pre * sig
        s1[rows(r * 128, 128), :] = sig + act * (1.0 - sig)
        spread(h3, r, act, 0, 2)

    each(0, 10, hidden)

    def mixed(b):
        acc = jnp.broadcast_to(bmbuf[...], (4 * 128, 512))
        for ky in range(3):
            for kx in range(3):
                a = h3[pl.ds(pl.multiple_of((b * 4 + ky) * 128, 128), 4 * 128), kx * 512 : kx * 512 + 512]
                acc = acc + dot_nt(a, wmbuf[3 * ky + kx])
        for i in range(4):
            pre = acc[i * 128 : (i + 1) * 128]
            sig = 0.5 * jnp.tanh(0.5 * pre) + 0.5
            spread(m3, b * 4 + i, hbuf[...] * (sig + (pre * sig) * (1.0 - sig)), 2, 0)

    each(0, 8 // 4, mixed)

    gacc[1024:1280, :] = jnp.zeros((256, 512), F32)
    for ky in range(3):
        g = dot(m3[...], wmbuf[3 * ky : 3 * ky + 3].reshape(1536, 512))
        at = pl.ds(ky * 128, 1024)
        gacc[at, :] = g if ky == 0 else gacc[at, :] + g
    lacc[...] = jnp.zeros((56, 128), F32)

    def latent_rows(r):
        at = rows(r * 128, 128)
        g = (gacc[at, :] * s1[at, :]).astype(BF16)
        q = dot_nt(w48[...], g)
        at = pl.ds(4 * r, 16)
        lacc[at, :] = lacc[at, :] + (q[16:32] + left(q[0:16]) + right(q[32:48]))

    each(0, 10, latent_rows)
    ngblk[...] = (-ratio * lacc[0:48, :]).astype(BF16)

    def ng_copy(peer, slot):
        return pltpu.make_async_remote_copy(
            src_ref=ngblk,
            dst_ref=grecv.at[slot],
            send_sem=gsend_sem.at[peer],
            recv_sem=grecv_sem.at[slot],
            device_id={"mp": peer},
            device_id_type=MESH,
        )

    def ng_take(j):
        peer = lax.rem(me + j, N)
        ng_copy(peer, peer).wait_recv()

    each(1, N, lambda j: ng_copy(lax.rem(me + j, N), me).start())
    grecv[me] = ngblk[...]
    ns[:, 0:8, :] = jnp.zeros((3, 8, 128), F32)
    ns[:, 512:528, :] = jnp.zeros((3, 16, 128), F32)
    each(1, N, ng_take)

    def shift(s, c):
        at = pl.ds(4 + 32 * s, 32)
        v = grecv[s].astype(F32)
        above = jnp.where(s > 0, grecv[jnp.maximum(s - 1, 0), 40 - 8 : 48].astype(F32)[8:16], 0.0)
        below = jnp.where(s < N - 1, grecv[jnp.minimum(s + 1, N - 1), 0:16].astype(F32)[0:8], 0.0)
        v = jnp.concatenate([v[8:16] + above, v[16:32], v[32:40] + below], axis=0)
        ns[0, at, :] = left(v)
        ns[1, at, :] = v
        ns[2, at, :] = right(v)
        return c

    lax.fori_loop(0, N, shift, 0)

    def columns(b, acc):
        parts = []
        for i in range(CHUNK // 128):
            at = pl.ds(4 * (b * (CHUNK // 128) + i), 16)
            parts.append(jnp.concatenate([ns[k, at, :].astype(BF16) for k in range(3)], axis=0))
        block = jnp.concatenate(parts, axis=1)
        at = rows(b * CHUNK, CHUNK)
        im[:, at] = block
        return acc + dot_nt(f2[:, at], block)

    wg = lax.fori_loop(0, 16384 // CHUNK, columns, jnp.zeros((32, 48), F32))
    wg = jnp.concatenate([wg[0:24], jnp.zeros((24, 80), F32)], axis=1)
    lane = iota((24, 128), 1)
    ordered = jnp.zeros((24, 128), F32)
    for k in range(9):
        ky, kx = divmod(k, 3)
        moved = pltpu.roll(wg, (4 * k - kx * 16 - (2 - ky) * 4) % 128, 1)
        ordered = jnp.where(jnp.logical_and(lane >= 4 * k, lane < 4 * k + 4), moved, ordered)
    wrecv[my_dp] = ordered[0:8] + pltpu.roll(ordered[8:16], 40, 1) + pltpu.roll(ordered[16:24], 80, 1)

    def wg_copy(peer, slot):
        return pltpu.make_async_remote_copy(
            src_ref=wrecv.at[my_dp],
            dst_ref=wrecv.at[slot],
            send_sem=wsend_sem.at[peer],
            recv_sem=wrecv_sem.at[slot],
            device_id={"dp": peer},
            device_id_type=MESH,
        )

    def wg_take(j):
        peer = lax.rem(my_dp + j, N)
        wg_copy(peer, peer).wait_recv()

    each(1, N, lambda j: wg_copy(lax.rem(my_dp + j, N), my_dp).start())

    e_cols = e48t[...].astype(BF16)

    def feature(b):
        p = dot(e_cols, im[:, rows(b * CHUNK, CHUNK)])
        for i in range(CHUNK // 128):
            stage[pl.ds(b * (CHUNK // 128) + i, 24, stride=STRIDE), :] = p[0:24, i * 128 : (i + 1) * 128]

    each(0, 16384 // CHUNK, feature)
    for c in range(20):
        fgb[0, c] = stage[c * STRIDE : c * STRIDE + 128, :].astype(BF16)
    fg_store = pltpu.make_async_copy(fgb, fg_out, out_sem.at[0])
    fg_store.start()
    each(1, N, wg_take)
    acc = wrecv[0]
    for s in range(1, N):
        acc = acc + wrecv[s]
    acc = acc * (1.0 / 16384.0)
    wgb[0:8, :] = acc[:, 0:36]
    wgb[8:16, :] = pltpu.roll(acc, 88, 1)[:, 0:36]
    wgb[16:20, :] = pltpu.roll(acc, 48, 1)[0:4, 0:36]
    wg_store = pltpu.make_async_copy(wgb, wg_out, out_sem.at[1])
    wg_store.start()

    def sent(j):
        lat_copy(lax.rem(me + j, N), j).wait_send()
        ng_copy(lax.rem(me + j, N), me).wait_send()
        wg_copy(lax.rem(my_dp + j, N), my_dp).wait_send()

    each(1, N, sent)
    fg_store.wait()
    wg_store.wait()


def body(features, w_out, noisy_latent, timestep, w_in, b_in, w_mid, b_mid, reward_head):
    hbm = pl.BlockSpec(memory_space=pltpu.HBM)
    dma = pltpu.SemaphoreType.DMA
    return pl.pallas_call(
        kernel,
        out_shape=(
            jax.ShapeDtypeStruct((1, 20, 128, 128), BF16),
            jax.ShapeDtypeStruct((20, 36), F32),
        ),
        in_specs=[hbm] * 10,
        out_specs=(hbm, hbm),
        scratch_shapes=[
            pltpu.VMEM((1, 20, 128, 128), BF16),
            pltpu.VMEM((20, 36), BF16),
            pltpu.VMEM((1, 4, 8, 128), F32),
            pltpu.SMEM((1,), jnp.int32),
            pltpu.VMEM((8, 128), F32),
            pltpu.VMEM((9, 512, 4), BF16),
            pltpu.VMEM((1, 512), F32),
            pltpu.VMEM((9, 512, 512), BF16),
            pltpu.VMEM((1, 512), F32),
            pltpu.VMEM((1, 512), F32),
            pltpu.VMEM((24 * STRIDE, 128), F32),
            pltpu.VMEM((32, 16384), BF16),
            pltpu.VMEM((130 * 16, 128), F32),
            pltpu.VMEM((528, 128), F32),
            pltpu.VMEM((32, 128), F32),
            pltpu.VMEM((528, 128), BF16),
            pltpu.VMEM((N, 48, 128), BF16),
            pltpu.VMEM((48, 32), F32),
            pltpu.VMEM((32, 48), F32),
            pltpu.VMEM((48, 512), BF16),
            pltpu.VMEM((3, 56, 128), F32),
            pltpu.VMEM((10 * 128, 1536), BF16),
            pltpu.VMEM((10 * 128, 512), F32),
            pltpu.VMEM((8 * 128, 1536), BF16),
            pltpu.VMEM((10 * 128, 512), F32),
            pltpu.VMEM((56, 128), F32),
            pltpu.VMEM((48, 128), BF16),
            pltpu.VMEM((N, 48, 128), BF16),
            pltpu.VMEM((3, 528, 128), F32),
            pltpu.VMEM((48, 16384), BF16),
            pltpu.VMEM((1, 20, 128, 128), BF16),
            pltpu.VMEM((20, 36), F32),
            pltpu.VMEM((N, 8, 128), F32),
            dma((10,)), dma((2,)), dma((N,)), dma((N,)), dma((N,)), dma((N,)), dma((N,)), dma((N,)),
        ],
        compiler_params=pltpu.CompilerParams(collective_id=0, has_side_effects=True, vmem_limit_bytes=56 << 20),
        name="step",
    )(
        features, w_out, noisy_latent, timestep, jnp.asarray(noise_table()), w_in,
        b_in.reshape(1, 512), w_mid, b_mid.reshape(1, 512), reward_head.reshape(1, 512),
    )


def solution(mesh):
    in_specs = (
        P("dp", "mp", None, None), P("mp", None), P("dp", None, "mp", None), P("dp"), P(), P(), P(), P(), P(),
    )
    out_specs = (P("dp", "mp", None, None), P("mp", None))
    return jax.shard_map(body, mesh=mesh, in_specs=in_specs, out_specs=out_specs, check_vma=False)
```

```python
import jax
import jax.numpy as jnp
import numpy as np
from jax import lax
from jax.experimental import pallas as pl
from jax.experimental.pallas import tpu as pltpu
from jax.sharding import PartitionSpec as P

F32 = jnp.float32
BF16 = jnp.bfloat16
MESH = pl.DeviceIdType.MESH
N = 16
STRIDE = 136
CHUNK = 1024
NT = (((1,), (1,)), ((), ()))


def noise_table():
    betas = np.linspace(0.00085**0.5, 0.012**0.5, 1000, dtype=np.float32) ** 2
    table = np.cumprod((1.0 - betas).astype(np.float32), dtype=np.float32)
    return np.pad(table, (0, 24)).reshape(8, 128)


def iota(shape, dim):
    return lax.broadcasted_iota(jnp.int32, shape, dim)


def dot(a, b):
    return jnp.dot(a, b, preferred_element_type=F32)


def dot_nt(a, b):
    return lax.dot_general(a, b, NT, preferred_element_type=F32)


def right(v):
    return jnp.where(iota(v.shape, 1) == 0, 0.0, pltpu.roll(v, 1, 1))


def left(v):
    return jnp.where(iota(v.shape, 1) == 127, 0.0, pltpu.roll(v, 127, 1))


def rows(start, size):
    return pl.ds(pl.multiple_of(start, size), size)


def each(lo, hi, step, unroll=1):
    def run(j, c):
        step(j)
        return c

    lax.fori_loop(lo, hi, run, 0, unroll=unroll)


def kernel(
    feat, w_out, noisy, tstep, table, w_in, b_in, w_mid, b_mid, head,
    fg_out, wg_out,
    fbuf, wobuf, nbuf, tbuf, tabbuf, wibuf, bibuf, wmbuf, bmbuf, hbuf,
    stage, f2, rs, eacc, nz, eloc, recv, e48, e48t, w48, ls,
    h3, s1, m3, gacc, lacc, ngblk, grecv, ns, im, wrecv,
    in_sem, send_sem, recv_sem, gsend_sem, grecv_sem, wsend_sem, wrecv_sem,
):
    me = lax.axis_index("mp")
    my_dp = lax.axis_index("dp")
    pairs = ((feat, fbuf), (w_out, wobuf), (noisy, nbuf), (tstep, tbuf), (table, tabbuf),
             (w_in, wibuf), (b_in, bibuf), (b_mid, bmbuf), (head, hbuf), (w_mid, wmbuf))
    loads = [pltpu.make_async_copy(src, dst, in_sem.at[i]) for i, (src, dst) in enumerate(pairs)]
    for copy in loads:
        copy.start()
    barrier = pltpu.get_barrier_semaphore()

    def greet(j):
        pl.semaphore_signal(barrier, inc=1, device_id={"mp": lax.rem(me + j, N)}, device_id_type=MESH)
        pl.semaphore_signal(barrier, inc=1, device_id={"dp": lax.rem(my_dp + j, N)}, device_id_type=MESH)

    each(1, N, greet)

    for copy in loads[1:5]:
        copy.wait()
    level = jnp.sum(
        jnp.where(iota((8, 128), 0) * 128 + iota((8, 128), 1) == tbuf[0], tabbuf[...], 0.0), keepdims=True
    )
    root_a = jnp.sqrt(level)
    root_b = jnp.sqrt(1.0 - level)
    ratio = root_b / root_a

    def tap_column(b):
        j = lax.shift_right_logical(b, 2) & 3
        k = 3 * (2 - j) + lax.shift_right_logical(b, 4)
        return jnp.where(j < 3, 4 * k + (b & 3), -1)

    pick = jnp.where(iota((36, 48), 0) == tap_column(iota((36, 48), 1)), 1.0, 0.0).astype(BF16)
    pick_t = jnp.where(iota((48, 36), 1) == tap_column(iota((48, 36), 0)), 1.0, 0.0).astype(BF16)
    e48t[...] = jnp.zeros((32, 48), F32)
    e48t[0:20, :] = dot(wobuf[...], pick)
    e48[...] = jnp.zeros((48, 32), F32)
    e48[:, 0:20] = dot_nt(pick_t, wobuf[...])

    loads[0].wait()
    for c in range(20):
        stage[c * STRIDE : c * STRIDE + 128, :] = fbuf[0, c].astype(F32)
    for c in range(20, 24):
        stage[c * STRIDE : c * STRIDE + 128, :] = jnp.zeros((128, 128), F32)
    rs[0:16, :] = jnp.zeros((16, 128), F32)
    rs[129 * 16 : 130 * 16, :] = jnp.zeros((16, 128), F32)
    e_rows = e48[...].astype(BF16)

    def unet_rows(b):
        parts = []
        for i in range(CHUNK // 128):
            v = stage[pl.ds(b * (CHUNK // 128) + i, 24, stride=STRIDE), :]
            parts.append(jnp.concatenate([v, jnp.zeros((8, 128), F32)], axis=0).astype(BF16))
        block = jnp.concatenate(parts, axis=1)
        f2[:, rows(b * CHUNK, CHUNK)] = block
        p = dot(e_rows, block)
        for i in range(CHUNK // 128):
            q = p[:, i * 128 : (i + 1) * 128]
            y = b * (CHUNK // 128) + i
            rs[rows((y + 1) * 16, 16), :] = q[16:32] + right(q[0:16]) + left(q[32:48])

    each(0, 16384 // CHUNK, unet_rows, 4)

    for o in range(4):
        nz[pl.ds(o, 8, stride=4), :] = nbuf[0, o]
    eacc[0:8, :] = jnp.zeros((8, 128), F32)
    eacc[520:528, :] = jnp.zeros((8, 128), F32)
    low = iota((8, 128), 0) < 4

    def unet_pairs(b):
        def at(y, half):
            return rs[rows((y + 1) * 16 + 8 * half, 8), :]

        for i in range(4):
            y = 8 * b + 2 * i
            e = at(y + 1, 0)
            e += jnp.where(low, pltpu.roll(at(y, 0), 4, 0), pltpu.roll(at(y, 1), 4, 0))
            e += jnp.where(low, at(y - 1, 1), pltpu.roll(at(y + 2, 0), 4, 0))
            eacc[rows(8 + 4 * y, 8), :] = -ratio * e

    each(0, 16, unet_pairs)
    mine = pl.ds(pl.multiple_of(8 + 32 * me, 8), 32)
    eacc[mine, :] = eacc[mine, :] + nz[...] / root_a
    eloc[...] = eacc[...].astype(BF16)

    def lat_copy(dest, slot):
        return pltpu.make_async_remote_copy(
            src_ref=eloc.at[pl.ds(pl.multiple_of(32 * dest, 32), 48), :],
            dst_ref=recv.at[slot],
            send_sem=send_sem.at[slot],
            recv_sem=recv_sem.at[slot],
            device_id={"mp": dest},
            device_id_type=MESH,
        )

    pl.semaphore_wait(barrier, 2 * (N - 1))
    each(1, N, lambda j: lat_copy(lax.rem(me + j, N), j).start())

    loads[5].wait()
    loads[6].wait()
    w_rows = jnp.zeros((48, 512), F32)
    for k in range(9):
        ky, kx = divmod(k, 3)
        put = jnp.where(iota((48, 4), 0) == kx * 16 + ky * 4 + iota((48, 4), 1), 1.0, 0.0).astype(BF16)
        w_rows = w_rows + dot(put, wibuf[k])
    w48[...] = w_rows.astype(BF16)
    for copy in loads[7:]:
        copy.wait()

    total = eacc[pl.ds(pl.multiple_of(32 * me, 32), 48), :]

    def lat_take(j, acc):
        lat_copy(lax.rem(me + j, N), j).wait_recv()
        return acc + recv[j].astype(F32)

    total = lax.fori_loop(1, N, lat_take, total)

    lat = total.astype(BF16).astype(F32)
    for i, t in enumerate((right(lat), lat, left(lat))):
        ls[i, 0:48, :] = t
        ls[i, 48:56, :] = jnp.zeros((8, 128), F32)
    edge = iota((128, 512), 0)
    first, last = edge == 0, edge == 127

    def spread(dst, r, val, down, up):
        at = rows(r * 128, 128)
        dst[at, down * 512 : down * 512 + 512] = jnp.where(first, 0.0, pltpu.roll(val, 1, 0)).astype(BF16)
        dst[at, 512:1024] = val.astype(BF16)
        dst[at, up * 512 : up * 512 + 512] = jnp.where(last, 0.0, pltpu.roll(val, 127, 0)).astype(BF16)

    def hidden(r):
        at = pl.ds(4 * r, 16)
        x48 = jnp.concatenate([ls[0, at, :], ls[1, at, :], ls[2, at, :]], axis=0)
        pre = dot(x48.T.astype(BF16), w48[...]) + bibuf[...]
        row = 8 * me - 1 + r
        half = jnp.where(jnp.logical_and(row >= 0, row < 128), 0.5, 0.0)
        sig = half * jnp.tanh(0.5 * pre) + half
        act = pre * sig
        s1[rows(r * 128, 128), :] = sig + act * (1.0 - sig)
        spread(h3, r, act, 0, 2)

    each(0, 10, hidden, 5)

    def mixed(b):
        acc = jnp.broadcast_to(bmbuf[...], (4 * 128, 512))
        for ky in range(3):
            for kx in range(3):
                a = h3[pl.ds(pl.multiple_of((b * 4 + ky) * 128, 128), 4 * 128), kx * 512 : kx * 512 + 512]
                acc = acc + dot_nt(a, wmbuf[3 * ky + kx])
        for i in range(4):
            pre = acc[i * 128 : (i + 1) * 128]
            sig = 0.5 * jnp.tanh(0.5 * pre) + 0.5
            spread(m3, b * 4 + i, hbuf[...] * (sig + (pre * sig) * (1.0 - sig)), 2, 0)

    each(0, 8 // 4, mixed, 2)

    gacc[1024:1280, :] = jnp.zeros((256, 512), F32)
    for ky in range(3):
        g = dot(m3[...], wmbuf[3 * ky : 3 * ky + 3].reshape(1536, 512))
        at = pl.ds(ky * 128, 1024)
        gacc[at, :] = g if ky == 0 else gacc[at, :] + g
    lacc[...] = jnp.zeros((56, 128), F32)

    def latent_rows(r):
        at = rows(r * 128, 128)
        g = (gacc[at, :] * s1[at, :]).astype(BF16)
        q = dot_nt(w48[...], g)
        at = pl.ds(4 * r, 16)
        lacc[at, :] = lacc[at, :] + (q[16:32] + left(q[0:16]) + right(q[32:48]))

    each(0, 10, latent_rows, 10)
    ngblk[...] = (-ratio * lacc[0:48, :]).astype(BF16)

    def ng_copy(peer, slot):
        return pltpu.make_async_remote_copy(
            src_ref=ngblk,
            dst_ref=grecv.at[slot],
            send_sem=gsend_sem.at[peer],
            recv_sem=grecv_sem.at[slot],
            device_id={"mp": peer},
            device_id_type=MESH,
        )

    def ng_take(j):
        peer = lax.rem(me + j, N)
        ng_copy(peer, peer).wait_recv()

    each(1, N, lambda j: ng_copy(lax.rem(me + j, N), me).start())
    grecv[me] = ngblk[...]
    ns[:, 0:8, :] = jnp.zeros((3, 8, 128), F32)
    ns[:, 512:528, :] = jnp.zeros((3, 16, 128), F32)
    each(1, N, ng_take)

    def shift(s, c):
        at = pl.ds(4 + 32 * s, 32)
        v = grecv[s].astype(F32)
        above = jnp.where(s > 0, grecv[jnp.maximum(s - 1, 0), 40 - 8 : 48].astype(F32)[8:16], 0.0)
        below = jnp.where(s < N - 1, grecv[jnp.minimum(s + 1, N - 1), 0:16].astype(F32)[0:8], 0.0)
        v = jnp.concatenate([v[8:16] + above, v[16:32], v[32:40] + below], axis=0)
        ns[0, at, :] = left(v)
        ns[1, at, :] = v
        ns[2, at, :] = right(v)
        return c

    lax.fori_loop(0, N, shift, 0, unroll=4)

    def columns(b, acc):
        parts = []
        for i in range(CHUNK // 128):
            at = pl.ds(4 * (b * (CHUNK // 128) + i), 16)
            parts.append(jnp.concatenate([ns[k, at, :].astype(BF16) for k in range(3)], axis=0))
        block = jnp.concatenate(parts, axis=1)
        at = rows(b * CHUNK, CHUNK)
        im[:, at] = block
        return acc + dot_nt(f2[:, at], block)

    wg = lax.fori_loop(0, 16384 // CHUNK, columns, jnp.zeros((32, 48), F32), unroll=4)
    wg = jnp.concatenate([wg[0:24], jnp.zeros((24, 80), F32)], axis=1)
    lane = iota((24, 128), 1)
    ordered = jnp.zeros((24, 128), F32)
    for k in range(9):
        ky, kx = divmod(k, 3)
        moved = pltpu.roll(wg, (4 * k - kx * 16 - (2 - ky) * 4) % 128, 1)
        ordered = jnp.where(jnp.logical_and(lane >= 4 * k, lane < 4 * k + 4), moved, ordered)
    wrecv[my_dp] = ordered[0:8] + pltpu.roll(ordered[8:16], 40, 1) + pltpu.roll(ordered[16:24], 80, 1)

    def wg_copy(peer, slot):
        return pltpu.make_async_remote_copy(
            src_ref=wrecv.at[my_dp],
            dst_ref=wrecv.at[slot],
            send_sem=wsend_sem.at[peer],
            recv_sem=wrecv_sem.at[slot],
            device_id={"dp": peer},
            device_id_type=MESH,
        )

    def wg_take(j):
        peer = lax.rem(my_dp + j, N)
        wg_copy(peer, peer).wait_recv()

    each(1, N, lambda j: wg_copy(lax.rem(my_dp + j, N), my_dp).start())

    e_cols = e48t[...].astype(BF16)

    def feature(b):
        p = dot(e_cols, im[:, rows(b * CHUNK, CHUNK)])
        for i in range(CHUNK // 128):
            stage[pl.ds(b * (CHUNK // 128) + i, 24, stride=STRIDE), :] = p[0:24, i * 128 : (i + 1) * 128]

    each(0, 16384 // CHUNK, feature, 4)
    for c in range(20):
        fg_out[0, c] = stage[c * STRIDE : c * STRIDE + 128, :].astype(BF16)
    each(1, N, wg_take)
    acc = wrecv[0]
    for s in range(1, N):
        acc = acc + wrecv[s]
    acc = acc * (1.0 / 16384.0)
    wg_out[0:8, :] = acc[:, 0:36]
    wg_out[8:16, :] = pltpu.roll(acc, 88, 1)[:, 0:36]
    wg_out[16:20, :] = pltpu.roll(acc, 48, 1)[0:4, 0:36]

    def sent(j):
        lat_copy(lax.rem(me + j, N), j).wait_send()
        ng_copy(lax.rem(me + j, N), me).wait_send()
        wg_copy(lax.rem(my_dp + j, N), my_dp).wait_send()

    each(1, N, sent)


def body(features, w_out, noisy_latent, timestep, w_in, b_in, w_mid, b_mid, reward_head):
    hbm = pl.BlockSpec(memory_space=pltpu.HBM)
    dma = pltpu.SemaphoreType.DMA
    return pl.pallas_call(
        kernel,
        out_shape=(
            jax.ShapeDtypeStruct((1, 20, 128, 128), BF16),
            jax.ShapeDtypeStruct((20, 36), F32),
        ),
        in_specs=[hbm] * 10,
        out_specs=(pl.BlockSpec(memory_space=pltpu.VMEM),) * 2,
        scratch_shapes=[
            pltpu.VMEM((1, 20, 128, 128), BF16),
            pltpu.VMEM((20, 36), BF16),
            pltpu.VMEM((1, 4, 8, 128), F32),
            pltpu.SMEM((1,), jnp.int32),
            pltpu.VMEM((8, 128), F32),
            pltpu.VMEM((9, 4, 512), BF16),
            pltpu.VMEM((1, 512), F32),
            pltpu.VMEM((9, 512, 512), BF16),
            pltpu.VMEM((1, 512), F32),
            pltpu.VMEM((1, 512), F32),
            pltpu.VMEM((24 * STRIDE, 128), F32),
            pltpu.VMEM((32, 16384), BF16),
            pltpu.VMEM((130 * 16, 128), F32),
            pltpu.VMEM((528, 128), F32),
            pltpu.VMEM((32, 128), F32),
            pltpu.VMEM((528, 128), BF16),
            pltpu.VMEM((N, 48, 128), BF16),
            pltpu.VMEM((48, 32), F32),
            pltpu.VMEM((32, 48), F32),
            pltpu.VMEM((48, 512), BF16),
            pltpu.VMEM((3, 56, 128), F32),
            pltpu.VMEM((10 * 128, 1536), BF16),
            pltpu.VMEM((10 * 128, 512), F32),
            pltpu.VMEM((8 * 128, 1536), BF16),
            pltpu.VMEM((10 * 128, 512), F32),
            pltpu.VMEM((56, 128), F32),
            pltpu.VMEM((48, 128), BF16),
            pltpu.VMEM((N, 48, 128), BF16),
            pltpu.VMEM((3, 528, 128), F32),
            pltpu.VMEM((48, 16384), BF16),
            pltpu.VMEM((N, 8, 128), F32),
            dma((10,)), dma((N,)), dma((N,)), dma((N,)), dma((N,)), dma((N,)), dma((N,)),
        ],
        compiler_params=pltpu.CompilerParams(collective_id=0, has_side_effects=True, vmem_limit_bytes=56 << 20),
        name="step",
    )(
        features, w_out, noisy_latent, timestep, jnp.asarray(noise_table()), w_in.transpose(0, 2, 1),
        b_in.reshape(1, 512), w_mid, b_mid.reshape(1, 512), reward_head.reshape(1, 512),
    )


def solution(mesh):
    in_specs = (
        P("dp", "mp", None, None), P("mp", None), P("dp", None, "mp", None), P("dp"), P(), P(), P(), P(), P(),
    )
    out_specs = (P("dp", "mp", None, None), P("mp", None))
    return jax.shard_map(body, mesh=mesh, in_specs=in_specs, out_specs=out_specs, check_vma=False)
```

```python
import jax
import jax.numpy as jnp
import numpy as np
from jax import lax
from jax.experimental import pallas as pl
from jax.experimental.pallas import tpu as pltpu
from jax.sharding import PartitionSpec as P

F32 = jnp.float32
BF16 = jnp.bfloat16
MESH = pl.DeviceIdType.MESH
N = 16
STRIDE = 136
CHUNK = 1024
NT = (((1,), (1,)), ((), ()))


MP_FAR = sorted(
    ((z, y, c) for z in range(2) for y in range(4) for c in range(2) if z or y or c),
    key=lambda d: -4 * (d[0] + min(d[1], 4 - d[1])) - d[2],
)
DP_FAR = sorted(
    ((x, z) for x in range(4) for z in range(4) if x or z),
    key=lambda d: -min(d[0], 4 - d[0]) - 2 * min(d[1], 4 - d[1]),
)


def noise_table():
    betas = np.linspace(0.00085**0.5, 0.012**0.5, 1000, dtype=np.float32) ** 2
    table = np.cumprod((1.0 - betas).astype(np.float32), dtype=np.float32)
    return np.pad(table, (0, 24)).reshape(8, 128)


def iota(shape, dim):
    return lax.broadcasted_iota(jnp.int32, shape, dim)


def dot(a, b):
    return jnp.dot(a, b, preferred_element_type=F32)


def dot_nt(a, b):
    return lax.dot_general(a, b, NT, preferred_element_type=F32)


def right(v):
    return jnp.where(iota(v.shape, 1) == 0, 0.0, pltpu.roll(v, 1, 1))


def left(v):
    return jnp.where(iota(v.shape, 1) == 127, 0.0, pltpu.roll(v, 127, 1))


def rows(start, size):
    return pl.ds(pl.multiple_of(start, size), size)


def each(lo, hi, step, unroll=1):
    def run(j, c):
        step(j)
        return c

    lax.fori_loop(lo, hi, run, 0, unroll=unroll)


def kernel(
    feat, w_out, noisy, tstep, table, w_in, b_in, w_mid, b_mid, head,
    fg_out, wg_out,
    fbuf, wobuf, nbuf, tbuf, tabbuf, wibuf, bibuf, wmbuf, bmbuf, hbuf,
    stage, f2, rs, eacc, nz, eloc, recv, e48, e48t, w48, ls,
    h3, s1, m3, gacc, lacc, ngblk, grecv, ns, im, fgb, wgb, wrecv,
    in_sem, out_sem, send_sem, recv_sem, gsend_sem, grecv_sem, wsend_sem, wrecv_sem,
):
    me = lax.axis_index("mp")
    my_dp = lax.axis_index("dp")
    pairs = ((feat, fbuf), (w_out, wobuf), (noisy, nbuf), (tstep, tbuf), (table, tabbuf),
             (w_in, wibuf), (b_in, bibuf), (b_mid, bmbuf), (head, hbuf), (w_mid, wmbuf))
    mp_peers = [
        lax.rem(me // 8 + z, 2) * 8 + lax.rem(lax.rem(me // 2, 4) + y, 4) * 2 + lax.rem(lax.rem(me, 2) + c, 2)
        for z, y, c in MP_FAR
    ]
    dp_peers = [lax.rem(my_dp // 4 + x, 4) * 4 + lax.rem(lax.rem(my_dp, 4) + z, 4) for x, z in DP_FAR]
    loads = [pltpu.make_async_copy(src, dst, in_sem.at[i]) for i, (src, dst) in enumerate(pairs)]
    for copy in loads[:-1]:
        copy.start()
    barrier = pltpu.get_barrier_semaphore()

    def greet(j):
        pl.semaphore_signal(barrier, inc=1, device_id={"mp": lax.rem(me + j, N)}, device_id_type=MESH)
        pl.semaphore_signal(barrier, inc=1, device_id={"dp": lax.rem(my_dp + j, N)}, device_id_type=MESH)

    each(1, N, greet)

    for copy in loads[1:5]:
        copy.wait()
    level = jnp.sum(
        jnp.where(iota((8, 128), 0) * 128 + iota((8, 128), 1) == tbuf[0], tabbuf[...], 0.0), keepdims=True
    )
    root_a = jnp.sqrt(level)
    root_b = jnp.sqrt(1.0 - level)
    ratio = root_b / root_a

    def tap_column(b):
        j = lax.shift_right_logical(b, 2) & 3
        k = 3 * (2 - j) + lax.shift_right_logical(b, 4)
        return jnp.where(j < 3, 4 * k + (b & 3), -1)

    pick = jnp.where(iota((36, 48), 0) == tap_column(iota((36, 48), 1)), 1.0, 0.0).astype(BF16)
    pick_t = jnp.where(iota((48, 36), 1) == tap_column(iota((48, 36), 0)), 1.0, 0.0).astype(BF16)
    e48t[...] = jnp.zeros((32, 48), F32)
    e48t[0:20, :] = dot(wobuf[...], pick)
    e48[...] = jnp.zeros((48, 32), F32)
    e48[:, 0:20] = dot_nt(pick_t, wobuf[...])

    loads[0].wait()
    loads[-1].start()
    for c in range(20):
        stage[c * STRIDE : c * STRIDE + 128, :] = fbuf[0, c].astype(F32)
    for c in range(20, 24):
        stage[c * STRIDE : c * STRIDE + 128, :] = jnp.zeros((128, 128), F32)
    rs[0:16, :] = jnp.zeros((16, 128), F32)
    rs[129 * 16 : 130 * 16, :] = jnp.zeros((16, 128), F32)
    e_rows = e48[...].astype(BF16)

    def unet_rows(b):
        parts = []
        for i in range(CHUNK // 128):
            v = stage[pl.ds(b * (CHUNK // 128) + i, 24, stride=STRIDE), :]
            parts.append(jnp.concatenate([v, jnp.zeros((8, 128), F32)], axis=0).astype(BF16))
        block = jnp.concatenate(parts, axis=1)
        f2[:, rows(b * CHUNK, CHUNK)] = block
        p = dot(e_rows, block)
        for i in range(CHUNK // 128):
            q = p[:, i * 128 : (i + 1) * 128]
            y = b * (CHUNK // 128) + i
            rs[rows((y + 1) * 16, 16), :] = q[16:32] + right(q[0:16]) + left(q[32:48])

    each(0, 16384 // CHUNK, unet_rows, 4)

    for o in range(4):
        nz[pl.ds(o, 8, stride=4), :] = nbuf[0, o]
    eacc[0:8, :] = jnp.zeros((8, 128), F32)
    eacc[520:528, :] = jnp.zeros((8, 128), F32)
    low = iota((8, 128), 0) < 4

    def unet_pairs(b):
        def at(y, half):
            return rs[rows((y + 1) * 16 + 8 * half, 8), :]

        for i in range(4):
            y = 8 * b + 2 * i
            e = at(y + 1, 0)
            e += jnp.where(low, pltpu.roll(at(y, 0), 4, 0), pltpu.roll(at(y, 1), 4, 0))
            e += jnp.where(low, at(y - 1, 1), pltpu.roll(at(y + 2, 0), 4, 0))
            eacc[rows(8 + 4 * y, 8), :] = -ratio * e

    each(0, 16, unet_pairs)
    mine = pl.ds(pl.multiple_of(8 + 32 * me, 8), 32)
    eacc[mine, :] = eacc[mine, :] + nz[...] / root_a
    eloc[...] = eacc[...].astype(BF16)

    def lat_copy(dest, slot):
        return pltpu.make_async_remote_copy(
            src_ref=eloc.at[pl.ds(pl.multiple_of(32 * dest, 32), 48), :],
            dst_ref=recv.at[slot],
            send_sem=send_sem.at[slot],
            recv_sem=recv_sem.at[slot],
            device_id={"mp": dest},
            device_id_type=MESH,
        )

    pl.semaphore_wait(barrier, 2 * (N - 1))
    for j, peer in enumerate(mp_peers):
        lat_copy(peer, j + 1).start()

    loads[5].wait()
    loads[6].wait()
    w_rows = jnp.zeros((48, 512), F32)
    for k in range(9):
        ky, kx = divmod(k, 3)
        put = jnp.where(iota((48, 4), 0) == kx * 16 + ky * 4 + iota((48, 4), 1), 1.0, 0.0).astype(BF16)
        w_rows = w_rows + dot(put, wibuf[k])
    w48[...] = w_rows.astype(BF16)
    for copy in loads[7:]:
        copy.wait()

    total = eacc[pl.ds(pl.multiple_of(32 * me, 32), 48), :]

    def lat_take(j, acc):
        lat_copy(lax.rem(me + j, N), j).wait_recv()
        return acc + recv[j].astype(F32)

    total = lax.fori_loop(1, N, lat_take, total)

    lat = total.astype(BF16).astype(F32)
    for i, t in enumerate((right(lat), lat, left(lat))):
        ls[i, 0:48, :] = t
        ls[i, 48:56, :] = jnp.zeros((8, 128), F32)
    edge = iota((128, 512), 0)
    first, last = edge == 0, edge == 127

    def spread(dst, r, val, down, up):
        at = rows(r * 128, 128)
        dst[at, down * 512 : down * 512 + 512] = jnp.where(first, 0.0, pltpu.roll(val, 1, 0)).astype(BF16)
        dst[at, 512:1024] = val.astype(BF16)
        dst[at, up * 512 : up * 512 + 512] = jnp.where(last, 0.0, pltpu.roll(val, 127, 0)).astype(BF16)

    def hidden(r):
        at = pl.ds(4 * r, 16)
        x48 = jnp.concatenate([ls[0, at, :], ls[1, at, :], ls[2, at, :]], axis=0)
        pre = dot(x48.T.astype(BF16), w48[...]) + bibuf[...]
        row = 8 * me - 1 + r
        half = jnp.where(jnp.logical_and(row >= 0, row < 128), 0.5, 0.0)
        sig = half * jnp.tanh(0.5 * pre) + half
        act = pre * sig
        s1[rows(r * 128, 128), :] = sig + act * (1.0 - sig)
        spread(h3, r, act, 0, 2)

    each(0, 10, hidden, 10)

    def mixed(b):
        acc = jnp.broadcast_to(bmbuf[...], (4 * 128, 512))
        for ky in range(3):
            for kx in range(3):
                a = h3[pl.ds(pl.multiple_of((b * 4 + ky) * 128, 128), 4 * 128), kx * 512 : kx * 512 + 512]
                acc = acc + dot_nt(a, wmbuf[3 * ky + kx])
        for i in range(4):
            pre = acc[i * 128 : (i + 1) * 128]
            sig = 0.5 * jnp.tanh(0.5 * pre) + 0.5
            spread(m3, b * 4 + i, hbuf[...] * (sig + (pre * sig) * (1.0 - sig)), 2, 0)

    each(0, 8 // 4, mixed, 2)

    gacc[1024:1280, :] = jnp.zeros((256, 512), F32)
    for ky in range(3):
        g = dot(m3[...], wmbuf[3 * ky : 3 * ky + 3].reshape(1536, 512))
        at = pl.ds(ky * 128, 1024)
        gacc[at, :] = g if ky == 0 else gacc[at, :] + g
    lacc[...] = jnp.zeros((56, 128), F32)

    def latent_rows(r):
        at = rows(r * 128, 128)
        g = (gacc[at, :] * s1[at, :]).astype(BF16)
        q = dot_nt(w48[...], g)
        at = pl.ds(4 * r, 16)
        lacc[at, :] = lacc[at, :] + (q[16:32] + left(q[0:16]) + right(q[32:48]))

    each(0, 10, latent_rows, 10)
    ngblk[...] = (-ratio * lacc[0:48, :]).astype(BF16)

    def ng_copy(peer, slot):
        return pltpu.make_async_remote_copy(
            src_ref=ngblk,
            dst_ref=grecv.at[slot],
            send_sem=gsend_sem.at[peer],
            recv_sem=grecv_sem.at[slot],
            device_id={"mp": peer},
            device_id_type=MESH,
        )

    def ng_take(j):
        peer = lax.rem(me + j, N)
        ng_copy(peer, peer).wait_recv()

    for peer in mp_peers:
        ng_copy(peer, me).start()
    grecv[me] = ngblk[...]
    ns[:, 0:8, :] = jnp.zeros((3, 8, 128), F32)
    ns[:, 512:528, :] = jnp.zeros((3, 16, 128), F32)
    each(1, N, ng_take)

    def shift(s, c):
        at = pl.ds(4 + 32 * s, 32)
        v = grecv[s].astype(F32)
        above = jnp.where(s > 0, grecv[jnp.maximum(s - 1, 0), 40 - 8 : 48].astype(F32)[8:16], 0.0)
        below = jnp.where(s < N - 1, grecv[jnp.minimum(s + 1, N - 1), 0:16].astype(F32)[0:8], 0.0)
        v = jnp.concatenate([v[8:16] + above, v[16:32], v[32:40] + below], axis=0)
        ns[0, at, :] = left(v)
        ns[1, at, :] = v
        ns[2, at, :] = right(v)
        return c

    lax.fori_loop(0, N, shift, 0, unroll=4)

    def columns(b, acc):
        parts = []
        for i in range(CHUNK // 128):
            at = pl.ds(4 * (b * (CHUNK // 128) + i), 16)
            parts.append(jnp.concatenate([ns[k, at, :].astype(BF16) for k in range(3)], axis=0))
        block = jnp.concatenate(parts, axis=1)
        at = rows(b * CHUNK, CHUNK)
        im[:, at] = block
        return acc + dot_nt(f2[:, at], block)

    wg = lax.fori_loop(0, 16384 // CHUNK, columns, jnp.zeros((32, 48), F32), unroll=4)
    wg = jnp.concatenate([wg[0:24], jnp.zeros((24, 80), F32)], axis=1)
    lane = iota((24, 128), 1)
    ordered = jnp.zeros((24, 128), F32)
    for k in range(9):
        ky, kx = divmod(k, 3)
        moved = pltpu.roll(wg, (4 * k - kx * 16 - (2 - ky) * 4) % 128, 1)
        ordered = jnp.where(jnp.logical_and(lane >= 4 * k, lane < 4 * k + 4), moved, ordered)
    wrecv[my_dp] = ordered[0:8] + pltpu.roll(ordered[8:16], 40, 1) + pltpu.roll(ordered[16:24], 80, 1)

    def wg_copy(peer, slot):
        return pltpu.make_async_remote_copy(
            src_ref=wrecv.at[my_dp],
            dst_ref=wrecv.at[slot],
            send_sem=wsend_sem.at[peer],
            recv_sem=wrecv_sem.at[slot],
            device_id={"dp": peer},
            device_id_type=MESH,
        )

    def wg_take(j):
        peer = lax.rem(my_dp + j, N)
        wg_copy(peer, peer).wait_recv()

    for peer in dp_peers:
        wg_copy(peer, my_dp).start()

    e_cols = e48t[...].astype(BF16)

    def feature(b):
        p = dot(e_cols, im[:, rows(b * CHUNK, CHUNK)])
        for i in range(CHUNK // 128):
            stage[pl.ds(b * (CHUNK // 128) + i, 24, stride=STRIDE), :] = p[0:24, i * 128 : (i + 1) * 128]

    each(0, 16384 // CHUNK, feature, 16)
    for c in range(20):
        fgb[0, c] = stage[c * STRIDE : c * STRIDE + 128, :].astype(BF16)
    fg_store = pltpu.make_async_copy(fgb, fg_out, out_sem.at[0])
    fg_store.start()
    def sent(j):
        lat_copy(lax.rem(me + j, N), j).wait_send()
        ng_copy(lax.rem(me + j, N), me).wait_send()

    each(1, N, sent)
    each(1, N, wg_take)
    acc = wrecv[0]
    for s in range(1, N):
        acc = acc + wrecv[s]
    acc = acc * (1.0 / 16384.0)
    wgb[0:8, :] = acc[:, 0:36]
    wgb[8:16, :] = pltpu.roll(acc, 88, 1)[:, 0:36]
    wgb[16:20, :] = pltpu.roll(acc, 48, 1)[0:4, 0:36]
    wg_store = pltpu.make_async_copy(wgb, wg_out, out_sem.at[1])
    wg_store.start()
    each(1, N, lambda j: wg_copy(lax.rem(my_dp + j, N), my_dp).wait_send())
    fg_store.wait()
    wg_store.wait()


def publish(fg, wg, fg_out, wg_out, sem):
    copies = [pltpu.make_async_copy(wg, wg_out, sem.at[4])]
    for i in range(4):
        part = pl.ds(5 * i, 5)
        copies.append(pltpu.make_async_copy(fg.at[0, part], fg_out.at[0, part], sem.at[i]))
    for copy in copies:
        copy.start()
    for copy in copies:
        copy.wait()


def body(features, w_out, noisy_latent, timestep, w_in, b_in, w_mid, b_mid, reward_head):
    hbm = pl.BlockSpec(memory_space=pltpu.HBM)
    dma = pltpu.SemaphoreType.DMA
    shapes = (jax.ShapeDtypeStruct((1, 20, 128, 128), BF16), jax.ShapeDtypeStruct((20, 36), F32))
    fg, wg = pl.pallas_call(
        kernel,
        out_shape=shapes,
        in_specs=[hbm] * 10,
        out_specs=(hbm, hbm),
        scratch_shapes=[
            pltpu.VMEM((1, 20, 128, 128), BF16),
            pltpu.VMEM((20, 36), BF16),
            pltpu.VMEM((1, 4, 8, 128), F32),
            pltpu.SMEM((1,), jnp.int32),
            pltpu.VMEM((8, 128), F32),
            pltpu.VMEM((9, 4, 512), BF16),
            pltpu.VMEM((1, 512), F32),
            pltpu.VMEM((9, 512, 512), BF16),
            pltpu.VMEM((1, 512), F32),
            pltpu.VMEM((1, 512), F32),
            pltpu.VMEM((24 * STRIDE, 128), F32),
            pltpu.VMEM((32, 16384), BF16),
            pltpu.VMEM((130 * 16, 128), F32),
            pltpu.VMEM((528, 128), F32),
            pltpu.VMEM((32, 128), F32),
            pltpu.VMEM((528, 128), BF16),
            pltpu.VMEM((N, 48, 128), BF16),
            pltpu.VMEM((48, 32), F32),
            pltpu.VMEM((32, 48), F32),
            pltpu.VMEM((48, 512), BF16),
            pltpu.VMEM((3, 56, 128), F32),
            pltpu.VMEM((10 * 128, 1536), BF16),
            pltpu.VMEM((10 * 128, 512), F32),
            pltpu.VMEM((8 * 128, 1536), BF16),
            pltpu.VMEM((10 * 128, 512), F32),
            pltpu.VMEM((56, 128), F32),
            pltpu.VMEM((48, 128), BF16),
            pltpu.VMEM((N, 48, 128), BF16),
            pltpu.VMEM((3, 528, 128), F32),
            pltpu.VMEM((48, 16384), BF16),
            pltpu.VMEM((1, 20, 128, 128), BF16),
            pltpu.VMEM((20, 36), F32),
            pltpu.VMEM((N, 8, 128), F32),
            dma((10,)), dma((2,)), dma((N,)), dma((N,)), dma((N,)), dma((N,)), dma((N,)), dma((N,)),
        ],
        compiler_params=pltpu.CompilerParams(collective_id=0, has_side_effects=True, vmem_limit_bytes=56 << 20),
        name="step",
    )(
        features, w_out, noisy_latent, timestep, jnp.asarray(noise_table()), w_in.transpose(0, 2, 1),
        b_in.reshape(1, 512), w_mid, b_mid.reshape(1, 512), reward_head.reshape(1, 512),
    )
    return pl.pallas_call(
        publish,
        out_shape=shapes,
        in_specs=[hbm, hbm],
        out_specs=(hbm, hbm),
        scratch_shapes=[dma((5,))],
        compiler_params=pltpu.CompilerParams(vmem_limit_bytes=56 << 20),
        name="publish",
    )(fg, wg)


def solution(mesh):
    in_specs = (
        P("dp", "mp", None, None), P("mp", None), P("dp", None, "mp", None), P("dp"), P(), P(), P(), P(), P(),
    )
    out_specs = (P("dp", "mp", None, None), P("mp", None))
    return jax.shard_map(body, mesh=mesh, in_specs=in_specs, out_specs=out_specs, check_vma=False)
```

```python
import jax
import jax.numpy as jnp
import numpy as np
from jax import lax
from jax.experimental import pallas as pl
from jax.experimental.pallas import tpu as pltpu
from jax.sharding import PartitionSpec as P

F32 = jnp.float32
BF16 = jnp.bfloat16
MESH = pl.DeviceIdType.MESH
N = 16
STRIDE = 136
CHUNK = 1024
NT = (((1,), (1,)), ((), ()))


MP_FAR = sorted(
    ((z, y, c) for z in range(2) for y in range(4) for c in range(2) if z or y or c),
    key=lambda d: -4 * (d[0] + min(d[1], 4 - d[1])) - d[2],
)
DP_FAR = sorted(
    ((x, z) for x in range(4) for z in range(4) if x or z),
    key=lambda d: -min(d[0], 4 - d[0]) - 2 * min(d[1], 4 - d[1]),
)


def noise_table():
    betas = np.linspace(0.00085**0.5, 0.012**0.5, 1000, dtype=np.float32) ** 2
    table = np.cumprod((1.0 - betas).astype(np.float32), dtype=np.float32)
    return np.pad(table, (0, 24)).reshape(8, 128)


def iota(shape, dim):
    return lax.broadcasted_iota(jnp.int32, shape, dim)


def dot(a, b):
    return jnp.dot(a, b, preferred_element_type=F32)


def dot_nt(a, b):
    return lax.dot_general(a, b, NT, preferred_element_type=F32)


def right(v):
    return jnp.where(iota(v.shape, 1) == 0, 0.0, pltpu.roll(v, 1, 1))


def left(v):
    return jnp.where(iota(v.shape, 1) == 127, 0.0, pltpu.roll(v, 127, 1))


def rows(start, size):
    return pl.ds(pl.multiple_of(start, size), size)


def each(lo, hi, step, unroll=1):
    def run(j, c):
        step(j)
        return c

    lax.fori_loop(lo, hi, run, 0, unroll=unroll)


def kernel(
    feat, w_out, noisy, tstep, table, w_in, b_in, w_mid, b_mid, head,
    fg_out, wg_out,
    fbuf, wobuf, nbuf, tbuf, tabbuf, wibuf, bibuf, wmbuf, bmbuf, hbuf,
    stage, f2, rs, eacc, nz, eloc, recv, e48, e48t, w48, ls,
    h3, s1, m3, gacc, lacc, ngblk, grecv, ns, im, wrecv,
    in_sem, send_sem, recv_sem, gsend_sem, grecv_sem, wsend_sem, wrecv_sem,
):
    me = lax.axis_index("mp")
    my_dp = lax.axis_index("dp")
    pairs = ((feat, fbuf), (w_out, wobuf), (noisy, nbuf), (tstep, tbuf), (table, tabbuf),
             (w_in, wibuf), (b_in, bibuf), (b_mid, bmbuf), (head, hbuf), (w_mid, wmbuf))
    mp_peers = [
        lax.rem(me // 8 + z, 2) * 8 + lax.rem(lax.rem(me // 2, 4) + y, 4) * 2 + lax.rem(lax.rem(me, 2) + c, 2)
        for z, y, c in MP_FAR
    ]
    dp_peers = [lax.rem(my_dp // 4 + x, 4) * 4 + lax.rem(lax.rem(my_dp, 4) + z, 4) for x, z in DP_FAR]
    loads = [pltpu.make_async_copy(src, dst, in_sem.at[i]) for i, (src, dst) in enumerate(pairs)]
    for copy in loads[:-1]:
        copy.start()
    barrier = pltpu.get_barrier_semaphore()

    def greet(j):
        pl.semaphore_signal(barrier, inc=1, device_id={"mp": lax.rem(me + j, N)}, device_id_type=MESH)
        pl.semaphore_signal(barrier, inc=1, device_id={"dp": lax.rem(my_dp + j, N)}, device_id_type=MESH)

    each(1, N, greet)

    for copy in loads[1:5]:
        copy.wait()
    level = jnp.sum(
        jnp.where(iota((8, 128), 0) * 128 + iota((8, 128), 1) == tbuf[0], tabbuf[...], 0.0), keepdims=True
    )
    root_a = jnp.sqrt(level)
    root_b = jnp.sqrt(1.0 - level)
    ratio = root_b / root_a

    def tap_column(b):
        j = lax.shift_right_logical(b, 2) & 3
        k = 3 * (2 - j) + lax.shift_right_logical(b, 4)
        return jnp.where(j < 3, 4 * k + (b & 3), -1)

    pick = jnp.where(iota((36, 48), 0) == tap_column(iota((36, 48), 1)), 1.0, 0.0).astype(BF16)
    pick_t = jnp.where(iota((48, 36), 1) == tap_column(iota((48, 36), 0)), 1.0, 0.0).astype(BF16)
    e48t[...] = jnp.zeros((32, 48), F32)
    e48t[0:20, :] = dot(wobuf[...], pick)
    e48[...] = jnp.zeros((48, 32), F32)
    e48[:, 0:20] = dot_nt(pick_t, wobuf[...])

    loads[0].wait()
    loads[-1].start()
    for c in range(20):
        stage[c * STRIDE : c * STRIDE + 128, :] = fbuf[0, c].astype(F32)
    for c in range(20, 24):
        stage[c * STRIDE : c * STRIDE + 128, :] = jnp.zeros((128, 128), F32)
    rs[0:16, :] = jnp.zeros((16, 128), F32)
    rs[129 * 16 : 130 * 16, :] = jnp.zeros((16, 128), F32)
    e_rows = e48[...].astype(BF16)

    def unet_rows(b):
        parts = []
        for i in range(CHUNK // 128):
            v = stage[pl.ds(b * (CHUNK // 128) + i, 24, stride=STRIDE), :]
            parts.append(jnp.concatenate([v, jnp.zeros((8, 128), F32)], axis=0).astype(BF16))
        block = jnp.concatenate(parts, axis=1)
        f2[:, rows(b * CHUNK, CHUNK)] = block
        p = dot(e_rows, block)
        for i in range(CHUNK // 128):
            q = p[:, i * 128 : (i + 1) * 128]
            y = b * (CHUNK // 128) + i
            rs[rows((y + 1) * 16, 16), :] = q[16:32] + right(q[0:16]) + left(q[32:48])

    each(0, 16384 // CHUNK, unet_rows, 4)

    for o in range(4):
        nz[pl.ds(o, 8, stride=4), :] = nbuf[0, o]
    eacc[0:8, :] = jnp.zeros((8, 128), F32)
    eacc[520:528, :] = jnp.zeros((8, 128), F32)
    low = iota((8, 128), 0) < 4

    def unet_pairs(b):
        def at(y, half):
            return rs[rows((y + 1) * 16 + 8 * half, 8), :]

        for i in range(4):
            y = 8 * b + 2 * i
            e = at(y + 1, 0)
            e += jnp.where(low, pltpu.roll(at(y, 0), 4, 0), pltpu.roll(at(y, 1), 4, 0))
            e += jnp.where(low, at(y - 1, 1), pltpu.roll(at(y + 2, 0), 4, 0))
            eacc[rows(8 + 4 * y, 8), :] = -ratio * e

    each(0, 16, unet_pairs)
    mine = pl.ds(pl.multiple_of(8 + 32 * me, 8), 32)
    eacc[mine, :] = eacc[mine, :] + nz[...] / root_a
    eloc[...] = eacc[...].astype(BF16)

    def lat_copy(dest, slot):
        return pltpu.make_async_remote_copy(
            src_ref=eloc.at[pl.ds(pl.multiple_of(32 * dest, 32), 48), :],
            dst_ref=recv.at[slot],
            send_sem=send_sem.at[slot],
            recv_sem=recv_sem.at[slot],
            device_id={"mp": dest},
            device_id_type=MESH,
        )

    pl.semaphore_wait(barrier, 2 * (N - 1))
    for j, peer in enumerate(mp_peers):
        lat_copy(peer, j + 1).start()

    loads[5].wait()
    loads[6].wait()
    w_rows = jnp.zeros((48, 512), F32)
    for k in range(9):
        ky, kx = divmod(k, 3)
        put = jnp.where(iota((48, 4), 0) == kx * 16 + ky * 4 + iota((48, 4), 1), 1.0, 0.0).astype(BF16)
        w_rows = w_rows + dot(put, wibuf[k])
    w48[...] = w_rows.astype(BF16)
    for copy in loads[7:]:
        copy.wait()

    total = eacc[pl.ds(pl.multiple_of(32 * me, 32), 48), :]

    def lat_take(j, acc):
        lat_copy(lax.rem(me + j, N), j).wait_recv()
        return acc + recv[j].astype(F32)

    total = lax.fori_loop(1, N, lat_take, total)

    lat = total.astype(BF16).astype(F32)
    for i, t in enumerate((right(lat), lat, left(lat))):
        ls[i, 0:48, :] = t
        ls[i, 48:56, :] = jnp.zeros((8, 128), F32)
    edge = iota((128, 512), 0)
    first, last = edge == 0, edge == 127

    def spread(dst, r, val, down, up):
        at = rows(r * 128, 128)
        dst[at, down * 512 : down * 512 + 512] = jnp.where(first, 0.0, pltpu.roll(val, 1, 0)).astype(BF16)
        dst[at, 512:1024] = val.astype(BF16)
        dst[at, up * 512 : up * 512 + 512] = jnp.where(last, 0.0, pltpu.roll(val, 127, 0)).astype(BF16)

    def hidden(r):
        at = pl.ds(4 * r, 16)
        x48 = jnp.concatenate([ls[0, at, :], ls[1, at, :], ls[2, at, :]], axis=0)
        pre = dot(x48.T.astype(BF16), w48[...]) + bibuf[...]
        row = 8 * me - 1 + r
        half = jnp.where(jnp.logical_and(row >= 0, row < 128), 0.5, 0.0)
        sig = half * jnp.tanh(0.5 * pre) + half
        act = pre * sig
        s1[rows(r * 128, 128), :] = sig + act * (1.0 - sig)
        spread(h3, r, act, 0, 2)

    each(0, 10, hidden, 10)

    def mixed(b):
        acc = jnp.broadcast_to(bmbuf[...], (4 * 128, 512))
        for ky in range(3):
            for kx in range(3):
                a = h3[pl.ds(pl.multiple_of((b * 4 + ky) * 128, 128), 4 * 128), kx * 512 : kx * 512 + 512]
                acc = acc + dot_nt(a, wmbuf[3 * ky + kx])
        for i in range(4):
            pre = acc[i * 128 : (i + 1) * 128]
            sig = 0.5 * jnp.tanh(0.5 * pre) + 0.5
            spread(m3, b * 4 + i, hbuf[...] * (sig + (pre * sig) * (1.0 - sig)), 2, 0)

    each(0, 8 // 4, mixed, 2)

    gacc[1024:1280, :] = jnp.zeros((256, 512), F32)
    for ky in range(3):
        g = dot(m3[...], wmbuf[3 * ky : 3 * ky + 3].reshape(1536, 512))
        at = pl.ds(ky * 128, 1024)
        gacc[at, :] = g if ky == 0 else gacc[at, :] + g
    lacc[...] = jnp.zeros((56, 128), F32)

    def latent_rows(r):
        at = rows(r * 128, 128)
        g = (gacc[at, :] * s1[at, :]).astype(BF16)
        q = dot_nt(w48[...], g)
        at = pl.ds(4 * r, 16)
        lacc[at, :] = lacc[at, :] + (q[16:32] + left(q[0:16]) + right(q[32:48]))

    each(0, 10, latent_rows, 10)
    ngblk[...] = (-ratio * lacc[0:48, :]).astype(BF16)

    def ng_copy(peer, slot):
        return pltpu.make_async_remote_copy(
            src_ref=ngblk,
            dst_ref=grecv.at[slot],
            send_sem=gsend_sem.at[peer],
            recv_sem=grecv_sem.at[slot],
            device_id={"mp": peer},
            device_id_type=MESH,
        )

    def ng_take(j):
        peer = lax.rem(me + j, N)
        ng_copy(peer, peer).wait_recv()

    for peer in mp_peers:
        ng_copy(peer, me).start()
    grecv[me] = ngblk[...]
    ns[:, 0:8, :] = jnp.zeros((3, 8, 128), F32)
    ns[:, 512:528, :] = jnp.zeros((3, 16, 128), F32)
    each(1, N, ng_take)

    def shift(s, c):
        at = pl.ds(4 + 32 * s, 32)
        v = grecv[s].astype(F32)
        above = jnp.where(s > 0, grecv[jnp.maximum(s - 1, 0), 40 - 8 : 48].astype(F32)[8:16], 0.0)
        below = jnp.where(s < N - 1, grecv[jnp.minimum(s + 1, N - 1), 0:16].astype(F32)[0:8], 0.0)
        v = jnp.concatenate([v[8:16] + above, v[16:32], v[32:40] + below], axis=0)
        ns[0, at, :] = left(v)
        ns[1, at, :] = v
        ns[2, at, :] = right(v)
        return c

    lax.fori_loop(0, N, shift, 0, unroll=4)

    def columns(b, acc):
        parts = []
        for i in range(CHUNK // 128):
            at = pl.ds(4 * (b * (CHUNK // 128) + i), 16)
            parts.append(jnp.concatenate([ns[k, at, :].astype(BF16) for k in range(3)], axis=0))
        block = jnp.concatenate(parts, axis=1)
        at = rows(b * CHUNK, CHUNK)
        im[:, at] = block
        return acc + dot_nt(f2[:, at], block)

    wg = lax.fori_loop(0, 16384 // CHUNK, columns, jnp.zeros((32, 48), F32), unroll=4)
    wg = jnp.concatenate([wg[0:24], jnp.zeros((24, 80), F32)], axis=1)
    lane = iota((24, 128), 1)
    ordered = jnp.zeros((24, 128), F32)
    for k in range(9):
        ky, kx = divmod(k, 3)
        moved = pltpu.roll(wg, (4 * k - kx * 16 - (2 - ky) * 4) % 128, 1)
        ordered = jnp.where(jnp.logical_and(lane >= 4 * k, lane < 4 * k + 4), moved, ordered)
    wrecv[my_dp] = ordered[0:8] + pltpu.roll(ordered[8:16], 40, 1) + pltpu.roll(ordered[16:24], 80, 1)

    def wg_copy(peer, slot):
        return pltpu.make_async_remote_copy(
            src_ref=wrecv.at[my_dp],
            dst_ref=wrecv.at[slot],
            send_sem=wsend_sem.at[peer],
            recv_sem=wrecv_sem.at[slot],
            device_id={"dp": peer},
            device_id_type=MESH,
        )

    def wg_take(j):
        peer = lax.rem(my_dp + j, N)
        wg_copy(peer, peer).wait_recv()

    for peer in dp_peers:
        wg_copy(peer, my_dp).start()

    e_cols = e48t[...].astype(BF16)

    def feature(b):
        p = dot(e_cols, im[:, rows(b * CHUNK, CHUNK)])
        for i in range(CHUNK // 128):
            stage[pl.ds(b * (CHUNK // 128) + i, 24, stride=STRIDE), :] = p[0:24, i * 128 : (i + 1) * 128]

    each(0, 16384 // CHUNK, feature, 16)
    for c in range(20):
        fg_out[0, c] = stage[c * STRIDE : c * STRIDE + 128, :].astype(BF16)
    def sent(j):
        lat_copy(lax.rem(me + j, N), j).wait_send()
        ng_copy(lax.rem(me + j, N), me).wait_send()

    each(1, N, sent)
    each(1, N, wg_take)
    acc = wrecv[0]
    for s in range(1, N):
        acc = acc + wrecv[s]
    acc = acc * (1.0 / 16384.0)
    wg_out[0:8, :] = acc[:, 0:36]
    wg_out[8:16, :] = pltpu.roll(acc, 88, 1)[:, 0:36]
    wg_out[16:20, :] = pltpu.roll(acc, 48, 1)[0:4, 0:36]
    each(1, N, lambda j: wg_copy(lax.rem(my_dp + j, N), my_dp).wait_send())


def publish(fg, wg, fg_out, wg_out, sem):
    copies = [pltpu.make_async_copy(fg, fg_out, sem.at[0]), pltpu.make_async_copy(wg, wg_out, sem.at[1])]
    for copy in copies:
        copy.start()
    for copy in copies:
        copy.wait()


def body(features, w_out, noisy_latent, timestep, w_in, b_in, w_mid, b_mid, reward_head):
    hbm = pl.BlockSpec(memory_space=pltpu.HBM)
    vmem = pl.BlockSpec(memory_space=pltpu.VMEM)
    dma = pltpu.SemaphoreType.DMA
    shapes = (jax.ShapeDtypeStruct((1, 20, 128, 128), BF16), jax.ShapeDtypeStruct((20, 36), F32))
    fg, wg = pl.pallas_call(
        kernel,
        out_shape=(pltpu.VMEM(shapes[0].shape, BF16), pltpu.VMEM(shapes[1].shape, F32)),
        in_specs=[hbm] * 10,
        out_specs=(vmem, vmem),
        scratch_shapes=[
            pltpu.VMEM((1, 20, 128, 128), BF16),
            pltpu.VMEM((20, 36), BF16),
            pltpu.VMEM((1, 4, 8, 128), F32),
            pltpu.SMEM((1,), jnp.int32),
            pltpu.VMEM((8, 128), F32),
            pltpu.VMEM((9, 4, 512), BF16),
            pltpu.VMEM((1, 512), F32),
            pltpu.VMEM((9, 512, 512), BF16),
            pltpu.VMEM((1, 512), F32),
            pltpu.VMEM((1, 512), F32),
            pltpu.VMEM((24 * STRIDE, 128), F32),
            pltpu.VMEM((32, 16384), BF16),
            pltpu.VMEM((130 * 16, 128), F32),
            pltpu.VMEM((528, 128), F32),
            pltpu.VMEM((32, 128), F32),
            pltpu.VMEM((528, 128), BF16),
            pltpu.VMEM((N, 48, 128), BF16),
            pltpu.VMEM((48, 32), F32),
            pltpu.VMEM((32, 48), F32),
            pltpu.VMEM((48, 512), BF16),
            pltpu.VMEM((3, 56, 128), F32),
            pltpu.VMEM((10 * 128, 1536), BF16),
            pltpu.VMEM((10 * 128, 512), F32),
            pltpu.VMEM((8 * 128, 1536), BF16),
            pltpu.VMEM((10 * 128, 512), F32),
            pltpu.VMEM((56, 128), F32),
            pltpu.VMEM((48, 128), BF16),
            pltpu.VMEM((N, 48, 128), BF16),
            pltpu.VMEM((3, 528, 128), F32),
            pltpu.VMEM((48, 16384), BF16),
            pltpu.VMEM((N, 8, 128), F32),
            dma((10,)), dma((N,)), dma((N,)), dma((N,)), dma((N,)), dma((N,)), dma((N,)),
        ],
        compiler_params=pltpu.CompilerParams(collective_id=0, has_side_effects=True, vmem_limit_bytes=56 << 20),
        name="step",
    )(
        features, w_out, noisy_latent, timestep, jnp.asarray(noise_table()), w_in.transpose(0, 2, 1),
        b_in.reshape(1, 512), w_mid, b_mid.reshape(1, 512), reward_head.reshape(1, 512),
    )
    return pl.pallas_call(
        publish,
        out_shape=shapes,
        in_specs=[vmem, vmem],
        out_specs=(hbm, hbm),
        scratch_shapes=[dma((2,))],
        compiler_params=pltpu.CompilerParams(vmem_limit_bytes=1 << 20),
        name="publish",
    )(fg, wg)


def solution(mesh):
    in_specs = (
        P("dp", "mp", None, None), P("mp", None), P("dp", None, "mp", None), P("dp"), P(), P(), P(), P(), P(),
    )
    out_specs = (P("dp", "mp", None, None), P("mp", None))
    return jax.shard_map(body, mesh=mesh, in_specs=in_specs, out_specs=out_specs, check_vma=False)
```

```python
import jax
import jax.numpy as jnp
import numpy as np
from jax import lax
from jax.experimental import pallas as pl
from jax.experimental.pallas import tpu as pltpu
from jax.sharding import PartitionSpec as P

F32 = jnp.float32
BF16 = jnp.bfloat16
MESH = pl.DeviceIdType.MESH
N = 16
STRIDE = 136
CHUNK = 1024
NT = (((1,), (1,)), ((), ()))


MP_FAR = sorted(
    ((z, y, c) for z in range(2) for y in range(4) for c in range(2) if z or y or c),
    key=lambda d: -4 * (d[0] + min(d[1], 4 - d[1])) - d[2],
)
DP_FAR = sorted(
    ((x, z) for x in range(4) for z in range(4) if x or z),
    key=lambda d: -min(d[0], 4 - d[0]) - 2 * min(d[1], 4 - d[1]),
)


def noise_table():
    betas = np.linspace(0.00085**0.5, 0.012**0.5, 1000, dtype=np.float32) ** 2
    table = np.cumprod((1.0 - betas).astype(np.float32), dtype=np.float32)
    return np.pad(table, (0, 24)).reshape(8, 128)


def iota(shape, dim):
    return lax.broadcasted_iota(jnp.int32, shape, dim)


def dot(a, b):
    return jnp.dot(a, b, preferred_element_type=F32)


def dot_nt(a, b):
    return lax.dot_general(a, b, NT, preferred_element_type=F32)


def right(v):
    return jnp.where(iota(v.shape, 1) == 0, 0.0, pltpu.roll(v, 1, 1))


def left(v):
    return jnp.where(iota(v.shape, 1) == 127, 0.0, pltpu.roll(v, 127, 1))


def rows(start, size):
    return pl.ds(pl.multiple_of(start, size), size)


def each(lo, hi, step, unroll=1):
    def run(j, c):
        step(j)
        return c

    lax.fori_loop(lo, hi, run, 0, unroll=unroll)


def kernel(
    feat, w_out, noisy, tstep, table, w_in, b_in, w_mid, b_mid, head,
    fg_out, wg_out,
    fbuf, wobuf, nbuf, tbuf, tabbuf, wibuf, bibuf, wmbuf, bmbuf, hbuf,
    stage, f2, rs, eacc, nz, eloc, recv, e48, e48t, w48, ls,
    plus, minus, t3, s1, x3, lacc, ngblk, grecv, ns, im, wrecv,
    in_sem, send_sem, recv_sem, gsend_sem, grecv_sem, wsend_sem, wrecv_sem,
):
    me = lax.axis_index("mp")
    my_dp = lax.axis_index("dp")
    pairs = ((feat, fbuf), (w_out, wobuf), (noisy, nbuf), (tstep, tbuf), (table, tabbuf),
             (w_in, wibuf), (b_in, bibuf), (b_mid, bmbuf), (head, hbuf), (w_mid, wmbuf))
    mp_peers = [
        lax.rem(me // 8 + z, 2) * 8 + lax.rem(lax.rem(me // 2, 4) + y, 4) * 2 + lax.rem(lax.rem(me, 2) + c, 2)
        for z, y, c in MP_FAR
    ]
    dp_peers = [lax.rem(my_dp // 4 + x, 4) * 4 + lax.rem(lax.rem(my_dp, 4) + z, 4) for x, z in DP_FAR]
    loads = [pltpu.make_async_copy(src, dst, in_sem.at[i]) for i, (src, dst) in enumerate(pairs)]
    for copy in loads[:-1]:
        copy.start()
    barrier = pltpu.get_barrier_semaphore()

    def greet(j):
        pl.semaphore_signal(barrier, inc=1, device_id={"mp": lax.rem(me + j, N)}, device_id_type=MESH)
        pl.semaphore_signal(barrier, inc=1, device_id={"dp": lax.rem(my_dp + j, N)}, device_id_type=MESH)

    each(1, N, greet)

    for copy in loads[1:5]:
        copy.wait()
    level = jnp.sum(
        jnp.where(iota((8, 128), 0) * 128 + iota((8, 128), 1) == tbuf[0], tabbuf[...], 0.0), keepdims=True
    )
    root_a = jnp.sqrt(level)
    root_b = jnp.sqrt(1.0 - level)
    ratio = root_b / root_a

    def tap_column(b):
        j = lax.shift_right_logical(b, 2) & 3
        k = 3 * (2 - j) + lax.shift_right_logical(b, 4)
        return jnp.where(j < 3, 4 * k + (b & 3), -1)

    pick = jnp.where(iota((36, 48), 0) == tap_column(iota((36, 48), 1)), 1.0, 0.0).astype(BF16)
    pick_t = jnp.where(iota((48, 36), 1) == tap_column(iota((48, 36), 0)), 1.0, 0.0).astype(BF16)
    e48t[...] = jnp.zeros((32, 48), F32)
    e48t[0:20, :] = dot(wobuf[...], pick)
    e48[...] = jnp.zeros((48, 32), F32)
    e48[:, 0:20] = dot_nt(pick_t, wobuf[...])

    loads[0].wait()
    loads[-1].start()
    for c in range(20):
        stage[c * STRIDE : c * STRIDE + 128, :] = fbuf[0, c].astype(F32)
    for c in range(20, 24):
        stage[c * STRIDE : c * STRIDE + 128, :] = jnp.zeros((128, 128), F32)
    rs[0:16, :] = jnp.zeros((16, 128), F32)
    rs[129 * 16 : 130 * 16, :] = jnp.zeros((16, 128), F32)
    e_rows = e48[...].astype(BF16)

    def unet_rows(b):
        parts = []
        for i in range(CHUNK // 128):
            v = stage[pl.ds(b * (CHUNK // 128) + i, 24, stride=STRIDE), :]
            parts.append(jnp.concatenate([v, jnp.zeros((8, 128), F32)], axis=0).astype(BF16))
        block = jnp.concatenate(parts, axis=1)
        f2[:, rows(b * CHUNK, CHUNK)] = block
        p = dot(e_rows, block)
        for i in range(CHUNK // 128):
            q = p[:, i * 128 : (i + 1) * 128]
            y = b * (CHUNK // 128) + i
            rs[rows((y + 1) * 16, 16), :] = q[16:32] + right(q[0:16]) + left(q[32:48])

    each(0, 16384 // CHUNK, unet_rows, 4)

    for o in range(4):
        nz[pl.ds(o, 8, stride=4), :] = nbuf[0, o]
    eacc[0:8, :] = jnp.zeros((8, 128), F32)
    eacc[520:528, :] = jnp.zeros((8, 128), F32)
    low = iota((8, 128), 0) < 4

    def unet_pairs(b):
        def at(y, half):
            return rs[rows((y + 1) * 16 + 8 * half, 8), :]

        for i in range(4):
            y = 8 * b + 2 * i
            e = at(y + 1, 0)
            e += jnp.where(low, pltpu.roll(at(y, 0), 4, 0), pltpu.roll(at(y, 1), 4, 0))
            e += jnp.where(low, at(y - 1, 1), pltpu.roll(at(y + 2, 0), 4, 0))
            eacc[rows(8 + 4 * y, 8), :] = -ratio * e

    each(0, 16, unet_pairs)
    mine = pl.ds(pl.multiple_of(8 + 32 * me, 8), 32)
    eacc[mine, :] = eacc[mine, :] + nz[...] / root_a
    eloc[...] = eacc[...].astype(BF16)

    def lat_copy(dest, slot):
        return pltpu.make_async_remote_copy(
            src_ref=eloc.at[pl.ds(pl.multiple_of(32 * dest, 32), 48), :],
            dst_ref=recv.at[slot],
            send_sem=send_sem.at[slot],
            recv_sem=recv_sem.at[slot],
            device_id={"mp": dest},
            device_id_type=MESH,
        )

    pl.semaphore_wait(barrier, 2 * (N - 1))
    for j, peer in enumerate(mp_peers):
        lat_copy(peer, j + 1).start()

    loads[5].wait()
    loads[6].wait()
    w_rows = jnp.zeros((48, 512), F32)
    for k in range(9):
        ky, kx = divmod(k, 3)
        put = jnp.where(iota((48, 4), 0) == kx * 16 + ky * 4 + iota((48, 4), 1), 1.0, 0.0).astype(BF16)
        w_rows = w_rows + dot(put, wibuf[k])
    w48[...] = w_rows.astype(BF16)
    for copy in loads[7:]:
        copy.wait()

    def points(i):
        kx = i // 8
        at = pl.ds(pl.multiple_of(lax.rem(i, 8) * 64, 64), 64)
        even = 0.5 * (wmbuf[kx, at, :].astype(F32) + wmbuf[6 + kx, at, :].astype(F32))
        odd = 0.5 * wmbuf[3 + kx, at, :].astype(F32)
        plus[kx, at, :] = (even + odd).astype(BF16)
        minus[kx, at, :] = (even - odd).astype(BF16)

    each(0, 24, points)

    total = eacc[pl.ds(pl.multiple_of(32 * me, 32), 48), :]

    def lat_take(j, acc):
        lat_copy(lax.rem(me + j, N), j).wait_recv()
        return acc + recv[j].astype(F32)

    total = lax.fori_loop(1, N, lat_take, total)

    lat = total.astype(BF16).astype(F32)
    for i, t in enumerate((right(lat), lat, left(lat))):
        ls[i, 0:48, :] = t
        ls[i, 48:56, :] = jnp.zeros((8, 128), F32)
    edge = iota((128, 512), 0)
    first, last = edge == 0, edge == 127

    def spread(dst, q, p, val, down, up):
        at = pl.ds(p * 128, 128)
        dst[q, at, down * 512 : down * 512 + 512] = jnp.where(first, 0.0, pltpu.roll(val, 1, 0)).astype(BF16)
        dst[q, at, 512:1024] = val.astype(BF16)
        dst[q, at, up * 512 : up * 512 + 512] = jnp.where(last, 0.0, pltpu.roll(val, 127, 0)).astype(BF16)

    def hidden(r):
        at = slice(4 * r, 4 * r + 16)
        x48 = jnp.concatenate([ls[0, at, :], ls[1, at, :], ls[2, at, :]], axis=0)
        pre = dot(x48.T.astype(BF16), w48[...]) + bibuf[...]
        row = 8 * me - 1 + r
        half = jnp.where(jnp.logical_and(row >= 0, row < 128), 0.5, 0.0)
        sig = half * jnp.tanh(0.5 * pre) + half
        act = pre * sig
        s1[r * 128 : (r + 1) * 128, :] = sig + act * (1.0 - sig)
        return act

    acts = {}
    for p in range(4):
        for r in range(2 * p, 2 * p + 4):
            if r not in acts:
                acts[r] = hidden(r)
        d0, d1, d2, d3 = (acts[2 * p + i] for i in range(4))
        for q, t in enumerate((d0 - d2, d1 + d2, d2 - d1, d1 - d3)):
            spread(t3, q, p, t, 0, 2)

    def mixed(g):
        at = slice(g * 4 * 128, (g + 1) * 4 * 128)
        prod = []
        for q in range(4):
            acc = None
            for kx in range(3):
                tap = (wmbuf.at[kx], plus.at[kx], minus.at[kx], wmbuf.at[6 + kx])[q]
                d = dot_nt(t3[q, at, kx * 512 : kx * 512 + 512], tap[...])
                acc = d if acc is None else acc + d
            prod.append(acc)
        for i in range(4):
            m0, m1, m2, m3 = (m[i * 128 : (i + 1) * 128] for m in prod)
            m1 = m1 + bmbuf[...]
            grads = []
            for pre in (m0 + m1 + m2, m1 - m2 - m3):
                sig = 0.5 * jnp.tanh(0.5 * pre) + 0.5
                grads.append(hbuf[...] * (sig + (pre * sig) * (1.0 - sig)))
            g0, g1 = grads
            for q, x in enumerate((g0, g0 + g1, g0 - g1, g1)):
                spread(x3, q, g * 4 + i, x, 2, 0)

    for g in range(4 // 4):
        mixed(g)

    lacc[...] = jnp.zeros((56, 128), F32)

    def latent_rows(r, val):
        g = (val * s1[r * 128 : (r + 1) * 128, :]).astype(BF16)
        q = dot_nt(w48[...], g)
        at = slice(4 * r, 4 * r + 16)
        lacc[at, :] = lacc[at, :] + (q[16:32] + left(q[0:16]) + right(q[32:48]))

    carry = None
    for g in range(4 // 4):
        at = slice(g * 4 * 128, (g + 1) * 4 * 128)
        taps = (wmbuf.at[0:3], plus, minus, wmbuf.at[6:9])
        prod = [dot(x3[q, at, :], taps[q][...].reshape(1536, 512)) for q in range(4)]
        for i in range(4):
            p0, p1, p2, p3 = (m[i * 128 : (i + 1) * 128] for m in prod)
            c0, c1, c2, c3 = p0, p1 - p2 - p3, p1 + p2 - p0, p3
            if carry is not None:
                c0, c1 = c0 + carry[0], c1 + carry[1]
            p = g * 4 + i
            latent_rows(2 * p, c0)
            latent_rows(2 * p + 1, c1)
            carry = (c2, c3)
    latent_rows(8, carry[0])
    latent_rows(9, carry[1])
    ngblk[...] = (-ratio * lacc[0:48, :]).astype(BF16)

    def ng_copy(peer, slot):
        return pltpu.make_async_remote_copy(
            src_ref=ngblk,
            dst_ref=grecv.at[slot],
            send_sem=gsend_sem.at[peer],
            recv_sem=grecv_sem.at[slot],
            device_id={"mp": peer},
            device_id_type=MESH,
        )

    def ng_take(j):
        peer = lax.rem(me + j, N)
        ng_copy(peer, peer).wait_recv()

    for peer in mp_peers:
        ng_copy(peer, me).start()
    grecv[me] = ngblk[...]
    ns[:, 0:8, :] = jnp.zeros((3, 8, 128), F32)
    ns[:, 512:528, :] = jnp.zeros((3, 16, 128), F32)
    each(1, N, ng_take)

    def shift(s, c):
        at = pl.ds(4 + 32 * s, 32)
        v = grecv[s].astype(F32)
        above = jnp.where(s > 0, grecv[jnp.maximum(s - 1, 0), 40 - 8 : 48].astype(F32)[8:16], 0.0)
        below = jnp.where(s < N - 1, grecv[jnp.minimum(s + 1, N - 1), 0:16].astype(F32)[0:8], 0.0)
        v = jnp.concatenate([v[8:16] + above, v[16:32], v[32:40] + below], axis=0)
        ns[0, at, :] = left(v)
        ns[1, at, :] = v
        ns[2, at, :] = right(v)
        return c

    lax.fori_loop(0, N, shift, 0, unroll=4)

    def columns(b, acc):
        parts = []
        for i in range(CHUNK // 128):
            at = pl.ds(4 * (b * (CHUNK // 128) + i), 16)
            parts.append(jnp.concatenate([ns[k, at, :].astype(BF16) for k in range(3)], axis=0))
        block = jnp.concatenate(parts, axis=1)
        at = rows(b * CHUNK, CHUNK)
        im[:, at] = block
        return acc + dot_nt(f2[:, at], block)

    wg = lax.fori_loop(0, 16384 // CHUNK, columns, jnp.zeros((32, 48), F32), unroll=4)
    wg = jnp.concatenate([wg[0:24], jnp.zeros((24, 80), F32)], axis=1)
    lane = iota((24, 128), 1)
    ordered = jnp.zeros((24, 128), F32)
    for k in range(9):
        ky, kx = divmod(k, 3)
        moved = pltpu.roll(wg, (4 * k - kx * 16 - (2 - ky) * 4) % 128, 1)
        ordered = jnp.where(jnp.logical_and(lane >= 4 * k, lane < 4 * k + 4), moved, ordered)
    wrecv[my_dp] = ordered[0:8] + pltpu.roll(ordered[8:16], 40, 1) + pltpu.roll(ordered[16:24], 80, 1)

    def wg_copy(peer, slot):
        return pltpu.make_async_remote_copy(
            src_ref=wrecv.at[my_dp],
            dst_ref=wrecv.at[slot],
            send_sem=wsend_sem.at[peer],
            recv_sem=wrecv_sem.at[slot],
            device_id={"dp": peer},
            device_id_type=MESH,
        )

    def wg_take(j):
        peer = lax.rem(my_dp + j, N)
        wg_copy(peer, peer).wait_recv()

    for peer in dp_peers:
        wg_copy(peer, my_dp).start()

    e_cols = e48t[...].astype(BF16)

    def feature(b):
        p = dot(e_cols, im[:, rows(b * CHUNK, CHUNK)])
        for i in range(CHUNK // 128):
            stage[pl.ds(b * (CHUNK // 128) + i, 24, stride=STRIDE), :] = p[0:24, i * 128 : (i + 1) * 128]

    each(0, 16384 // CHUNK, feature, 16)
    for c in range(20):
        fg_out[0, c] = stage[c * STRIDE : c * STRIDE + 128, :].astype(BF16)
    def sent(j):
        lat_copy(lax.rem(me + j, N), j).wait_send()
        ng_copy(lax.rem(me + j, N), me).wait_send()

    each(1, N, sent)
    each(1, N, wg_take)
    acc = wrecv[0]
    for s in range(1, N):
        acc = acc + wrecv[s]
    acc = acc * (1.0 / 16384.0)
    wg_out[0:8, :] = acc[:, 0:36]
    wg_out[8:16, :] = pltpu.roll(acc, 88, 1)[:, 0:36]
    wg_out[16:20, :] = pltpu.roll(acc, 48, 1)[0:4, 0:36]
    each(1, N, lambda j: wg_copy(lax.rem(my_dp + j, N), my_dp).wait_send())


def publish(fg, wg, fg_out, wg_out, sem):
    copies = [pltpu.make_async_copy(fg, fg_out, sem.at[0]), pltpu.make_async_copy(wg, wg_out, sem.at[1])]
    for copy in copies:
        copy.start()
    for copy in copies:
        copy.wait()


def body(features, w_out, noisy_latent, timestep, w_in, b_in, w_mid, b_mid, reward_head):
    hbm = pl.BlockSpec(memory_space=pltpu.HBM)
    vmem = pl.BlockSpec(memory_space=pltpu.VMEM)
    dma = pltpu.SemaphoreType.DMA
    shapes = (jax.ShapeDtypeStruct((1, 20, 128, 128), BF16), jax.ShapeDtypeStruct((20, 36), F32))
    fg, wg = pl.pallas_call(
        kernel,
        out_shape=(pltpu.VMEM(shapes[0].shape, BF16), pltpu.VMEM(shapes[1].shape, F32)),
        in_specs=[hbm] * 10,
        out_specs=(vmem, vmem),
        scratch_shapes=[
            pltpu.VMEM((1, 20, 128, 128), BF16),
            pltpu.VMEM((20, 36), BF16),
            pltpu.VMEM((1, 4, 8, 128), F32),
            pltpu.SMEM((1,), jnp.int32),
            pltpu.VMEM((8, 128), F32),
            pltpu.VMEM((9, 4, 512), BF16),
            pltpu.VMEM((1, 512), F32),
            pltpu.VMEM((9, 512, 512), BF16),
            pltpu.VMEM((1, 512), F32),
            pltpu.VMEM((1, 512), F32),
            pltpu.VMEM((24 * STRIDE, 128), F32),
            pltpu.VMEM((32, 16384), BF16),
            pltpu.VMEM((130 * 16, 128), F32),
            pltpu.VMEM((528, 128), F32),
            pltpu.VMEM((32, 128), F32),
            pltpu.VMEM((528, 128), BF16),
            pltpu.VMEM((N, 48, 128), BF16),
            pltpu.VMEM((48, 32), F32),
            pltpu.VMEM((32, 48), F32),
            pltpu.VMEM((48, 512), BF16),
            pltpu.VMEM((3, 56, 128), F32),
            pltpu.VMEM((3, 512, 512), BF16),
            pltpu.VMEM((3, 512, 512), BF16),
            pltpu.VMEM((4, 512, 1536), BF16),
            pltpu.VMEM((10 * 128, 512), F32),
            pltpu.VMEM((4, 512, 1536), BF16),
            pltpu.VMEM((56, 128), F32),
            pltpu.VMEM((48, 128), BF16),
            pltpu.VMEM((N, 48, 128), BF16),
            pltpu.VMEM((3, 528, 128), F32),
            pltpu.VMEM((48, 16384), BF16),
            pltpu.VMEM((N, 8, 128), F32),
            dma((10,)), dma((N,)), dma((N,)), dma((N,)), dma((N,)), dma((N,)), dma((N,)),
        ],
        compiler_params=pltpu.CompilerParams(collective_id=0, has_side_effects=True, vmem_limit_bytes=56 << 20),
        name="step",
    )(
        features, w_out, noisy_latent, timestep, jnp.asarray(noise_table()), w_in.transpose(0, 2, 1),
        b_in.reshape(1, 512), w_mid, b_mid.reshape(1, 512), reward_head.reshape(1, 512),
    )
    return pl.pallas_call(
        publish,
        out_shape=shapes,
        in_specs=[vmem, vmem],
        out_specs=(hbm, hbm),
        scratch_shapes=[dma((2,))],
        compiler_params=pltpu.CompilerParams(vmem_limit_bytes=1 << 20),
        name="publish",
    )(fg, wg)


def solution(mesh):
    in_specs = (
        P("dp", "mp", None, None), P("mp", None), P("dp", None, "mp", None), P("dp"), P(), P(), P(), P(), P(),
    )
    out_specs = (P("dp", "mp", None, None), P("mp", None))
    return jax.shard_map(body, mesh=mesh, in_specs=in_specs, out_specs=out_specs, check_vma=False)
```

```python
import jax
import jax.numpy as jnp
import numpy as np
from jax import lax
from jax.experimental import pallas as pl
from jax.experimental.pallas import tpu as pltpu
from jax.sharding import PartitionSpec as P

F32 = jnp.float32
BF16 = jnp.bfloat16
MESH = pl.DeviceIdType.MESH
N = 16
STRIDE = 136
CHUNK = 1024
NT = (((1,), (1,)), ((), ()))


MP_FAR = sorted(
    ((z, y, c) for z in range(2) for y in range(4) for c in range(2) if z or y or c),
    key=lambda d: -4 * (d[0] + min(d[1], 4 - d[1])) - d[2],
)
DP_FAR = sorted(
    ((x, z) for x in range(4) for z in range(4) if x or z),
    key=lambda d: -min(d[0], 4 - d[0]) - 2 * min(d[1], 4 - d[1]),
)


SLOT = {q: i for i, q in enumerate((a, b) for a in range(4) for b in range(4) if a % 3 or b % 3)}


def noise_table():
    betas = np.linspace(0.00085**0.5, 0.012**0.5, 1000, dtype=np.float32) ** 2
    table = np.cumprod((1.0 - betas).astype(np.float32), dtype=np.float32)
    return np.pad(table, (0, 24)).reshape(8, 128)


def iota(shape, dim):
    return lax.broadcasted_iota(jnp.int32, shape, dim)


def dot(a, b):
    return jnp.dot(a, b, preferred_element_type=F32)


def dot_nt(a, b):
    return lax.dot_general(a, b, NT, preferred_element_type=F32)


def right(v):
    return jnp.where(iota(v.shape, 1) == 0, 0.0, pltpu.roll(v, 1, 1))


def left(v):
    return jnp.where(iota(v.shape, 1) == 127, 0.0, pltpu.roll(v, 127, 1))


def rows(start, size):
    return pl.ds(pl.multiple_of(start, size), size)


def each(lo, hi, step, unroll=1):
    def run(j, c):
        step(j)
        return c

    lax.fori_loop(lo, hi, run, 0, unroll=unroll)


def kernel(
    feat, w_out, noisy, tstep, table, w_in, b_in, w_mid, b_mid, head,
    fg_out, wg_out,
    fbuf, wobuf, nbuf, tbuf, tabbuf, wibuf, bibuf, wmbuf, bmbuf, hbuf,
    stage, f2, rs, eacc, nz, eloc, recv, e48, e48t, w48, ls,
    upts, t3, s1, x3, gbuf, mm, lacc, ngblk, grecv, ns, im, wrecv,
    in_sem, send_sem, recv_sem, gsend_sem, grecv_sem, wsend_sem, wrecv_sem,
):
    me = lax.axis_index("mp")
    my_dp = lax.axis_index("dp")
    pairs = ((feat, fbuf), (w_out, wobuf), (noisy, nbuf), (tstep, tbuf), (table, tabbuf),
             (w_in, wibuf), (b_in, bibuf), (b_mid, bmbuf), (head, hbuf), (w_mid, wmbuf))
    mp_peers = [
        lax.rem(me // 8 + z, 2) * 8 + lax.rem(lax.rem(me // 2, 4) + y, 4) * 2 + lax.rem(lax.rem(me, 2) + c, 2)
        for z, y, c in MP_FAR
    ]
    dp_peers = [lax.rem(my_dp // 4 + x, 4) * 4 + lax.rem(lax.rem(my_dp, 4) + z, 4) for x, z in DP_FAR]
    loads = [pltpu.make_async_copy(src, dst, in_sem.at[i]) for i, (src, dst) in enumerate(pairs)]
    for copy in loads[:-1]:
        copy.start()
    barrier = pltpu.get_barrier_semaphore()

    def greet(j):
        pl.semaphore_signal(barrier, inc=1, device_id={"mp": lax.rem(me + j, N)}, device_id_type=MESH)
        pl.semaphore_signal(barrier, inc=1, device_id={"dp": lax.rem(my_dp + j, N)}, device_id_type=MESH)

    each(1, N, greet)

    for copy in loads[1:5]:
        copy.wait()
    level = jnp.sum(
        jnp.where(iota((8, 128), 0) * 128 + iota((8, 128), 1) == tbuf[0], tabbuf[...], 0.0), keepdims=True
    )
    root_a = jnp.sqrt(level)
    root_b = jnp.sqrt(1.0 - level)
    ratio = root_b / root_a

    def tap_column(b):
        j = lax.shift_right_logical(b, 2) & 3
        k = 3 * (2 - j) + lax.shift_right_logical(b, 4)
        return jnp.where(j < 3, 4 * k + (b & 3), -1)

    pick = jnp.where(iota((36, 48), 0) == tap_column(iota((36, 48), 1)), 1.0, 0.0).astype(BF16)
    pick_t = jnp.where(iota((48, 36), 1) == tap_column(iota((48, 36), 0)), 1.0, 0.0).astype(BF16)
    e48t[...] = jnp.zeros((32, 48), F32)
    e48t[0:20, :] = dot(wobuf[...], pick)
    e48[...] = jnp.zeros((48, 32), F32)
    e48[:, 0:20] = dot_nt(pick_t, wobuf[...])

    loads[0].wait()
    loads[-1].start()
    for c in range(20):
        stage[c * STRIDE : c * STRIDE + 128, :] = fbuf[0, c].astype(F32)
    for c in range(20, 24):
        stage[c * STRIDE : c * STRIDE + 128, :] = jnp.zeros((128, 128), F32)
    rs[0:16, :] = jnp.zeros((16, 128), F32)
    rs[129 * 16 : 130 * 16, :] = jnp.zeros((16, 128), F32)
    e_rows = e48[...].astype(BF16)

    def unet_rows(b):
        parts = []
        for i in range(CHUNK // 128):
            v = stage[pl.ds(b * (CHUNK // 128) + i, 24, stride=STRIDE), :]
            parts.append(jnp.concatenate([v, jnp.zeros((8, 128), F32)], axis=0).astype(BF16))
        block = jnp.concatenate(parts, axis=1)
        f2[:, rows(b * CHUNK, CHUNK)] = block
        p = dot(e_rows, block)
        for i in range(CHUNK // 128):
            q = p[:, i * 128 : (i + 1) * 128]
            y = b * (CHUNK // 128) + i
            rs[rows((y + 1) * 16, 16), :] = q[16:32] + right(q[0:16]) + left(q[32:48])

    each(0, 16384 // CHUNK, unet_rows, 4)

    for o in range(4):
        nz[pl.ds(o, 8, stride=4), :] = nbuf[0, o]
    eacc[0:8, :] = jnp.zeros((8, 128), F32)
    eacc[520:528, :] = jnp.zeros((8, 128), F32)
    low = iota((8, 128), 0) < 4

    def unet_pairs(b):
        def at(y, half):
            return rs[rows((y + 1) * 16 + 8 * half, 8), :]

        for i in range(4):
            y = 8 * b + 2 * i
            e = at(y + 1, 0)
            e += jnp.where(low, pltpu.roll(at(y, 0), 4, 0), pltpu.roll(at(y, 1), 4, 0))
            e += jnp.where(low, at(y - 1, 1), pltpu.roll(at(y + 2, 0), 4, 0))
            eacc[rows(8 + 4 * y, 8), :] = -ratio * e

    each(0, 16, unet_pairs)
    mine = pl.ds(pl.multiple_of(8 + 32 * me, 8), 32)
    eacc[mine, :] = eacc[mine, :] + nz[...] / root_a
    eloc[...] = eacc[...].astype(BF16)

    def lat_copy(dest, slot):
        return pltpu.make_async_remote_copy(
            src_ref=eloc.at[pl.ds(pl.multiple_of(32 * dest, 32), 48), :],
            dst_ref=recv.at[slot],
            send_sem=send_sem.at[slot],
            recv_sem=recv_sem.at[slot],
            device_id={"mp": dest},
            device_id_type=MESH,
        )

    pl.semaphore_wait(barrier, 2 * (N - 1))
    for j, peer in enumerate(mp_peers):
        lat_copy(peer, j + 1).start()

    loads[5].wait()
    loads[6].wait()
    w_rows = jnp.zeros((48, 512), F32)
    for k in range(9):
        ky, kx = divmod(k, 3)
        put = jnp.where(iota((48, 4), 0) == kx * 16 + ky * 4 + iota((48, 4), 1), 1.0, 0.0).astype(BF16)
        w_rows = w_rows + dot(put, wibuf[k])
    w48[...] = w_rows.astype(BF16)
    for copy in loads[7:]:
        copy.wait()

    def points(i):
        at = pl.ds(pl.multiple_of(i * 16, 16), 16)
        cols = []
        for kx in range(3):
            w0, w1, w2 = (wmbuf[3 * ky + kx, at, :].astype(F32) for ky in range(3))
            even, odd = 0.5 * (w0 + w2), 0.5 * w1
            cols.append((w0, even + odd, even - odd, w2))
        for qy in range(4):
            w0, w1, w2 = (col[qy] for col in cols)
            even, odd = 0.5 * (w0 + w2), 0.5 * w1
            for qx, u in enumerate((w0, even + odd, even - odd, w2)):
                if (qy, qx) in SLOT:
                    upts[SLOT[qy, qx], at, :] = u.astype(BF16)

    each(0, 32, points, 4)

    def taps(qy, qx, d, c):
        if (qy, qx) in SLOT:
            return upts[SLOT[qy, qx], d, c]
        return wmbuf[2 * qy + 2 * qx // 3, d, c]

    total = eacc[pl.ds(pl.multiple_of(32 * me, 32), 48), :]

    def lat_take(j, acc):
        lat_copy(lax.rem(me + j, N), j).wait_recv()
        return acc + recv[j].astype(F32)

    total = lax.fori_loop(1, N, lat_take, total)

    def column(b):
        return jnp.where(b < 64, 2 * b, 2 * b - 127)

    to_halves = jnp.where(iota((128, 128), 0) == column(iota((128, 128), 1)), 1.0, 0.0).astype(BF16)
    to_columns = jnp.where(iota((128, 128), 1) == column(iota((128, 128), 0)), 1.0, 0.0).astype(BF16)

    def from_right(v):
        lane = iota(v.shape, 1)
        v = jnp.where(lane < 64, pltpu.roll(v, 64, 1), pltpu.roll(v, 63, 1))
        return jnp.where(lane == 127, 0.0, v)

    def from_left(v):
        lane = iota(v.shape, 1)
        v = jnp.where(lane < 64, pltpu.roll(v, 65, 1), pltpu.roll(v, 64, 1))
        return jnp.where(lane == 0, 0.0, v)

    lat = dot(total.astype(BF16), to_halves)
    for i, t in enumerate((from_left(lat), lat, from_right(lat))):
        ls[i, 0:48, :] = t
        ls[i, 48:56, :] = jnp.zeros((8, 128), F32)

    def down(v):
        return jnp.where(iota(v.shape, 0) == 0, 0.0, pltpu.roll(v, 1, 0))

    def up(v):
        return jnp.where(iota(v.shape, 0) == 63, 0.0, pltpu.roll(v, 63, 0))

    def combine(m0, m1, m2, m3):
        return m0 + m1 + m2, m1 - m2 - m3

    def scatter(p0, p1, p2, p3):
        return p0, p1 - p2 - p3, p1 + p2 - p0, p3

    def hidden(r):
        at = slice(4 * r, 4 * r + 16)
        x48 = jnp.concatenate([ls[0, at, :], ls[1, at, :], ls[2, at, :]], axis=0)
        pre = dot(x48.T.astype(BF16), w48[...]) + bibuf[...]
        row = 8 * me - 1 + r
        half = jnp.where(jnp.logical_and(row >= 0, row < 128), 0.5, 0.0)
        sig = half * jnp.tanh(0.5 * pre) + half
        act = pre * sig
        s1[r * 128 : (r + 1) * 128, :] = sig + act * (1.0 - sig)
        return act

    acts = {}
    for p in range(4):
        for r in range(2 * p, 2 * p + 4):
            if r not in acts:
                acts[r] = hidden(r)
        d0, d1, d2, d3 = (acts[2 * p + i] for i in range(4))
        for qy, t in enumerate((d0 - d2, d1 + d2, d2 - d1, d1 - d3)):
            even, odd = t[0:64], t[64:128]
            for qx, u in enumerate((down(odd) - odd, even + odd, odd - even, even - up(even))):
                t3[4 * qy + qx, p * 64 : p * 64 + 64, :] = u.astype(BF16)

    HALF = 512 // 2

    def channels(n):
        return slice(n * HALF, (n + 1) * HALF)

    def forward(n, qy):
        for qx in range(4):
            mm[n % 2, 4 * qy + qx] = dot_nt(t3[4 * qy + qx], taps(qy, qx, channels(n), slice(None)))

    def mixed(n, p):
        at, ch = slice(p * 64, p * 64 + 64), channels(n)
        grads = []
        sums = [combine(*(mm[n % 2, 4 * qy + qx, at, :] for qx in range(4))) for qy in range(4)]
        for side in range(2):
            m0, m1, m2, m3 = (pair[side] for pair in sums)
            out = []
            for pre in combine(m0, m1 + bmbuf[:, ch], m2, m3):
                sig = 0.5 * jnp.tanh(0.5 * pre) + 0.5
                out.append(hbuf[:, ch] * (sig + (pre * sig) * (1.0 - sig)))
            g0, g1 = out
            grads.append((g0, g0 + g1, g0 - g1, g1))
        for qy in range(4):
            even, odd = grads[0][qy], grads[1][qy]
            for qx, u in enumerate((even, even + odd, even - odd, odd)):
                x3[4 * qy + qx, at, ch] = u.astype(BF16)

    for n in range(2):
        for qy in range(4):
            forward(n, qy)
            if n > 0:
                mixed(n - 1, qy)
    for p in range(4):
        mixed(2 - 1, p)

    lacc[...] = jnp.zeros((56, 128), F32)

    def latent_rows(n, r, val):
        at, ch = slice(r * 128, (r + 1) * 128), channels(n)
        gbuf[at, ch] = (val * s1[at, ch]).astype(BF16)

    def finish(n, r, p0, p1, p2, p3):
        c0, c1, c2, c3 = scatter(p0, p1, p2, p3)
        latent_rows(n, r, jnp.concatenate([c1 + down(c3), c2 + up(c0)], axis=0))

    def backward(n, qy):
        for qx in range(4):
            mm[n % 2, 4 * qy + qx] = dot(x3[4 * qy + qx], taps(qy, qx, slice(None), channels(n)))

    def give(n, p, carry):
        at = slice(p * 64, p * 64 + 64)
        given = [scatter(*(mm[n % 2, 4 * qy + qx, at, :] for qy in range(4))) for qx in range(4)]
        if carry is not None:
            given = [(g[0] + c[0], g[1] + c[1], g[2], g[3]) for g, c in zip(given, carry)]
        finish(n, 2 * p, *(g[0] for g in given))
        finish(n, 2 * p + 1, *(g[1] for g in given))
        carry = [(g[2], g[3]) for g in given]
        if p == 3:
            finish(n, 8, *(c[0] for c in carry))
            finish(n, 9, *(c[1] for c in carry))
        return carry

    carry = None
    for n in range(2):
        for qy in range(4):
            backward(n, qy)
            if n > 0:
                carry = give(n - 1, qy, carry)
        carry = None
    for p in range(4):
        carry = give(2 - 1, p, carry)
    lat_parts = dot_nt(w48[...], gbuf[...])
    for r in range(10):
        q = lat_parts[:, r * 128 : (r + 1) * 128]
        at = slice(4 * r, 4 * r + 16)
        lacc[at, :] = lacc[at, :] + (q[16:32] + from_right(q[0:16]) + from_left(q[32:48]))
    ngblk[...] = dot((-ratio * lacc[0:48, :]).astype(BF16), to_columns).astype(BF16)

    def ng_copy(peer, slot):
        return pltpu.make_async_remote_copy(
            src_ref=ngblk,
            dst_ref=grecv.at[slot],
            send_sem=gsend_sem.at[peer],
            recv_sem=grecv_sem.at[slot],
            device_id={"mp": peer},
            device_id_type=MESH,
        )

    def ng_take(j):
        peer = lax.rem(me + j, N)
        ng_copy(peer, peer).wait_recv()

    for peer in mp_peers:
        ng_copy(peer, me).start()
    grecv[me] = ngblk[...]
    ns[:, 0:8, :] = jnp.zeros((3, 8, 128), F32)
    ns[:, 512:528, :] = jnp.zeros((3, 16, 128), F32)
    each(1, N, ng_take)

    def shift(s, c):
        at = pl.ds(4 + 32 * s, 32)
        v = grecv[s].astype(F32)
        above = jnp.where(s > 0, grecv[jnp.maximum(s - 1, 0), 40 - 8 : 48].astype(F32)[8:16], 0.0)
        below = jnp.where(s < N - 1, grecv[jnp.minimum(s + 1, N - 1), 0:16].astype(F32)[0:8], 0.0)
        v = jnp.concatenate([v[8:16] + above, v[16:32], v[32:40] + below], axis=0)
        ns[0, at, :] = left(v)
        ns[1, at, :] = v
        ns[2, at, :] = right(v)
        return c

    lax.fori_loop(0, N, shift, 0, unroll=16)

    def columns(b, acc):
        parts = []
        for i in range(CHUNK // 128):
            at = pl.ds(4 * (b * (CHUNK // 128) + i), 16)
            parts.append(jnp.concatenate([ns[k, at, :].astype(BF16) for k in range(3)], axis=0))
        block = jnp.concatenate(parts, axis=1)
        at = rows(b * CHUNK, CHUNK)
        im[:, at] = block
        return acc + dot_nt(f2[:, at], block)

    wg = lax.fori_loop(0, 16384 // CHUNK, columns, jnp.zeros((32, 48), F32), unroll=8)
    wg = jnp.concatenate([wg[0:24], jnp.zeros((24, 80), F32)], axis=1)
    lane = iota((24, 128), 1)
    ordered = jnp.zeros((24, 128), F32)
    for k in range(9):
        ky, kx = divmod(k, 3)
        moved = pltpu.roll(wg, (4 * k - kx * 16 - (2 - ky) * 4) % 128, 1)
        ordered = jnp.where(jnp.logical_and(lane >= 4 * k, lane < 4 * k + 4), moved, ordered)
    wrecv[my_dp] = ordered[0:8] + pltpu.roll(ordered[8:16], 40, 1) + pltpu.roll(ordered[16:24], 80, 1)

    def wg_copy(peer, slot):
        return pltpu.make_async_remote_copy(
            src_ref=wrecv.at[my_dp],
            dst_ref=wrecv.at[slot],
            send_sem=wsend_sem.at[peer],
            recv_sem=wrecv_sem.at[slot],
            device_id={"dp": peer},
            device_id_type=MESH,
        )

    def wg_take(j):
        peer = lax.rem(my_dp + j, N)
        wg_copy(peer, peer).wait_recv()

    for peer in dp_peers:
        wg_copy(peer, my_dp).start()

    e_cols = e48t[...].astype(BF16)

    def feature(b):
        p = dot(e_cols, im[:, rows(b * CHUNK, CHUNK)])
        for i in range(CHUNK // 128):
            stage[pl.ds(b * (CHUNK // 128) + i, 24, stride=STRIDE), :] = p[0:24, i * 128 : (i + 1) * 128]

    each(0, 16384 // CHUNK, feature, 16)
    for c in range(20):
        fg_out[0, c] = stage[c * STRIDE : c * STRIDE + 128, :].astype(BF16)
    def sent(j):
        lat_copy(lax.rem(me + j, N), j).wait_send()
        ng_copy(lax.rem(me + j, N), me).wait_send()

    each(1, N, sent)
    each(1, N, wg_take)
    acc = wrecv[0]
    for s in range(1, N):
        acc = acc + wrecv[s]
    acc = acc * (1.0 / 16384.0)
    wg_out[0:8, :] = acc[:, 0:36]
    wg_out[8:16, :] = pltpu.roll(acc, 88, 1)[:, 0:36]
    wg_out[16:20, :] = pltpu.roll(acc, 48, 1)[0:4, 0:36]
    each(1, N, lambda j: wg_copy(lax.rem(my_dp + j, N), my_dp).wait_send())


def publish(fg, wg, fg_out, wg_out, sem):
    copies = [pltpu.make_async_copy(fg, fg_out, sem.at[0]), pltpu.make_async_copy(wg, wg_out, sem.at[1])]
    for copy in copies:
        copy.start()
    for copy in copies:
        copy.wait()


def body(features, w_out, noisy_latent, timestep, w_in, b_in, w_mid, b_mid, reward_head):
    hbm = pl.BlockSpec(memory_space=pltpu.HBM)
    vmem = pl.BlockSpec(memory_space=pltpu.VMEM)
    dma = pltpu.SemaphoreType.DMA
    shapes = (jax.ShapeDtypeStruct((1, 20, 128, 128), BF16), jax.ShapeDtypeStruct((20, 36), F32))
    fg, wg = pl.pallas_call(
        kernel,
        out_shape=(pltpu.VMEM(shapes[0].shape, BF16), pltpu.VMEM(shapes[1].shape, F32)),
        in_specs=[hbm] * 10,
        out_specs=(vmem, vmem),
        scratch_shapes=[
            pltpu.VMEM((1, 20, 128, 128), BF16),
            pltpu.VMEM((20, 36), BF16),
            pltpu.VMEM((1, 4, 8, 128), F32),
            pltpu.SMEM((1,), jnp.int32),
            pltpu.VMEM((8, 128), F32),
            pltpu.VMEM((9, 4, 512), BF16),
            pltpu.VMEM((1, 512), F32),
            pltpu.VMEM((9, 512, 512), BF16),
            pltpu.VMEM((1, 512), F32),
            pltpu.VMEM((1, 512), F32),
            pltpu.VMEM((24 * STRIDE, 128), F32),
            pltpu.VMEM((32, 16384), BF16),
            pltpu.VMEM((130 * 16, 128), F32),
            pltpu.VMEM((528, 128), F32),
            pltpu.VMEM((32, 128), F32),
            pltpu.VMEM((528, 128), BF16),
            pltpu.VMEM((N, 48, 128), BF16),
            pltpu.VMEM((48, 32), F32),
            pltpu.VMEM((32, 48), F32),
            pltpu.VMEM((48, 512), BF16),
            pltpu.VMEM((3, 56, 128), F32),
            pltpu.VMEM((12, 512, 512), BF16),
            pltpu.VMEM((16, 256, 512), BF16),
            pltpu.VMEM((10 * 128, 512), F32),
            pltpu.VMEM((16, 256, 512), BF16),
            pltpu.VMEM((10 * 128, 512), BF16),
            pltpu.VMEM((2, 16, 256, 512 // 2), F32),
            pltpu.VMEM((56, 128), F32),
            pltpu.VMEM((48, 128), BF16),
            pltpu.VMEM((N, 48, 128), BF16),
            pltpu.VMEM((3, 528, 128), F32),
            pltpu.VMEM((48, 16384), BF16),
            pltpu.VMEM((N, 8, 128), F32),
            dma((10,)), dma((N,)), dma((N,)), dma((N,)), dma((N,)), dma((N,)), dma((N,)),
        ],
        compiler_params=pltpu.CompilerParams(collective_id=0, has_side_effects=True, vmem_limit_bytes=56 << 20),
        name="step",
    )(
        features, w_out, noisy_latent, timestep, jnp.asarray(noise_table()), w_in.transpose(0, 2, 1),
        b_in.reshape(1, 512), w_mid, b_mid.reshape(1, 512), reward_head.reshape(1, 512),
    )
    return pl.pallas_call(
        publish,
        out_shape=shapes,
        in_specs=[vmem, vmem],
        out_specs=(hbm, hbm),
        scratch_shapes=[dma((2,))],
        compiler_params=pltpu.CompilerParams(vmem_limit_bytes=1 << 20),
        name="publish",
    )(fg, wg)


def solution(mesh):
    in_specs = (
        P("dp", "mp", None, None), P("mp", None), P("dp", None, "mp", None), P("dp"), P(), P(), P(), P(), P(),
    )
    out_specs = (P("dp", "mp", None, None), P("mp", None))
    return jax.shard_map(body, mesh=mesh, in_specs=in_specs, out_specs=out_specs, check_vma=False)
```

```python
import jax
import jax.numpy as jnp
import numpy as np
from jax import lax
from jax.experimental import pallas as pl
from jax.experimental.pallas import tpu as pltpu
from jax.sharding import PartitionSpec as P

F32 = jnp.float32
BF16 = jnp.bfloat16
MESH = pl.DeviceIdType.MESH
N = 16
STRIDE = 136
CHUNK = 1024
NT = (((1,), (1,)), ((), ()))


MP_FAR = sorted(
    ((z, y, c) for z in range(2) for y in range(4) for c in range(2) if z or y or c),
    key=lambda d: -4 * (d[0] + min(d[1], 4 - d[1])) - d[2],
)
DP_FAR = sorted(
    ((x, z) for x in range(4) for z in range(4) if x or z),
    key=lambda d: -min(d[0], 4 - d[0]) - 2 * min(d[1], 4 - d[1]),
)


SLOT = {q: i for i, q in enumerate((a, b) for a in range(4) for b in range(4) if a % 3 or b % 3)}


def noise_table():
    betas = np.linspace(0.00085**0.5, 0.012**0.5, 1000, dtype=np.float32) ** 2
    table = np.cumprod((1.0 - betas).astype(np.float32), dtype=np.float32)
    return np.pad(table, (0, 24)).reshape(8, 128)


def iota(shape, dim):
    return lax.broadcasted_iota(jnp.int32, shape, dim)


def dot(a, b):
    return jnp.dot(a, b, preferred_element_type=F32)


def dot_nt(a, b):
    return lax.dot_general(a, b, NT, preferred_element_type=F32)


def right(v):
    return jnp.where(iota(v.shape, 1) == 0, 0.0, pltpu.roll(v, 1, 1))


def left(v):
    return jnp.where(iota(v.shape, 1) == 127, 0.0, pltpu.roll(v, 127, 1))


def rows(start, multiple, size=None):
    return pl.ds(pl.multiple_of(start, multiple), size or multiple)


def each(lo, hi, step, unroll=1):
    def run(j, c):
        step(j)
        return c

    lax.fori_loop(lo, hi, run, 0, unroll=unroll)


def kernel(
    feat, w_out, noisy, tstep, table, w_in, b_in, w_mid, b_mid, head,
    fg_out, wg_out,
    fbuf, wobuf, nbuf, tbuf, tabbuf, wibuf, bibuf, wmbuf, bmbuf, hbuf,
    stage, f2, rs, eacc, nz, eloc, recv, e48, e48t, w48, ls,
    upts, t3, s1, x3, gbuf, mm, lacc, ngblk, grecv, ns, im, wrecv,
    in_sem, send_sem, recv_sem, gsend_sem, grecv_sem, wsend_sem, wrecv_sem,
):
    me = lax.axis_index("mp")
    my_dp = lax.axis_index("dp")
    pairs = ((feat, fbuf), (w_out, wobuf), (noisy, nbuf), (tstep, tbuf), (table, tabbuf),
             (w_in, wibuf), (b_in, bibuf), (b_mid, bmbuf), (head, hbuf), (w_mid, wmbuf))
    mp_peers = [
        lax.rem(me // 8 + z, 2) * 8 + lax.rem(lax.rem(me // 2, 4) + y, 4) * 2 + lax.rem(lax.rem(me, 2) + c, 2)
        for z, y, c in MP_FAR
    ]
    dp_peers = [lax.rem(my_dp // 4 + x, 4) * 4 + lax.rem(lax.rem(my_dp, 4) + z, 4) for x, z in DP_FAR]
    loads = [pltpu.make_async_copy(src, dst, in_sem.at[i]) for i, (src, dst) in enumerate(pairs)]
    for copy in loads[:-1]:
        copy.start()
    barrier = pltpu.get_barrier_semaphore()

    def greet(j):
        pl.semaphore_signal(barrier, inc=1, device_id={"mp": lax.rem(me + j, N)}, device_id_type=MESH)
        pl.semaphore_signal(barrier, inc=1, device_id={"dp": lax.rem(my_dp + j, N)}, device_id_type=MESH)

    each(1, N, greet)

    for copy in loads[1:5]:
        copy.wait()
    level = jnp.sum(
        jnp.where(iota((8, 128), 0) * 128 + iota((8, 128), 1) == tbuf[0], tabbuf[...], 0.0), keepdims=True
    )
    root_a = jnp.sqrt(level)
    root_b = jnp.sqrt(1.0 - level)
    ratio = root_b / root_a

    def tap_column(b):
        j = lax.shift_right_logical(b, 2) & 3
        k = 3 * (2 - j) + lax.shift_right_logical(b, 4)
        return jnp.where(j < 3, 4 * k + (b & 3), -1)

    pick = jnp.where(iota((36, 48), 0) == tap_column(iota((36, 48), 1)), 1.0, 0.0).astype(BF16)
    pick_t = jnp.where(iota((48, 36), 1) == tap_column(iota((48, 36), 0)), 1.0, 0.0).astype(BF16)
    e48t[...] = jnp.zeros((32, 48), F32)
    e48t[0:20, :] = dot(wobuf[...], pick)
    e48[...] = jnp.zeros((48, 32), F32)
    e48[:, 0:20] = dot_nt(pick_t, wobuf[...])

    loads[0].wait()
    loads[-1].start()
    for c in range(20):
        stage[c * STRIDE : c * STRIDE + 128, :] = fbuf[0, c].astype(F32)
    for c in range(20, 24):
        stage[c * STRIDE : c * STRIDE + 128, :] = jnp.zeros((128, 128), F32)
    rs[0:16, :] = jnp.zeros((16, 128), F32)
    rs[129 * 16 : 130 * 16, :] = jnp.zeros((16, 128), F32)
    e_rows = e48[...].astype(BF16)

    def unet_rows(b):
        parts = []
        for i in range(CHUNK // 128):
            v = stage[pl.ds(b * (CHUNK // 128) + i, 24, stride=STRIDE), :]
            parts.append(jnp.concatenate([v, jnp.zeros((8, 128), F32)], axis=0).astype(BF16))
        block = jnp.concatenate(parts, axis=1)
        f2[:, rows(b * CHUNK, CHUNK)] = block
        p = dot(e_rows, block)
        for i in range(CHUNK // 128):
            q = p[:, i * 128 : (i + 1) * 128]
            y = b * (CHUNK // 128) + i
            rs[rows((y + 1) * 16, 16), :] = q[16:32] + right(q[0:16]) + left(q[32:48])

    each(0, 16384 // CHUNK, unet_rows, 4)

    for o in range(4):
        nz[pl.ds(o, 8, stride=4), :] = nbuf[0, o]
    eacc[0:8, :] = jnp.zeros((8, 128), F32)
    eacc[520:528, :] = jnp.zeros((8, 128), F32)
    low = iota((8, 128), 0) < 4

    def unet_pairs(b):
        def at(y, half):
            return rs[rows((y + 1) * 16 + 8 * half, 8), :]

        for i in range(4):
            y = 8 * b + 2 * i
            e = at(y + 1, 0)
            e += jnp.where(low, pltpu.roll(at(y, 0), 4, 0), pltpu.roll(at(y, 1), 4, 0))
            e += jnp.where(low, at(y - 1, 1), pltpu.roll(at(y + 2, 0), 4, 0))
            eacc[rows(8 + 4 * y, 8), :] = -ratio * e

    each(0, 16, unet_pairs)
    mine = pl.ds(pl.multiple_of(8 + 32 * me, 8), 32)
    eacc[mine, :] = eacc[mine, :] + nz[...] / root_a
    eloc[...] = eacc[...].astype(BF16)

    def lat_copy(dest, slot):
        return pltpu.make_async_remote_copy(
            src_ref=eloc.at[pl.ds(pl.multiple_of(32 * dest, 32), 48), :],
            dst_ref=recv.at[slot],
            send_sem=send_sem.at[slot],
            recv_sem=recv_sem.at[slot],
            device_id={"mp": dest},
            device_id_type=MESH,
        )

    pl.semaphore_wait(barrier, 2 * (N - 1))
    for j, peer in enumerate(mp_peers):
        lat_copy(peer, j + 1).start()

    loads[5].wait()
    loads[6].wait()
    w_rows = jnp.zeros((48, 512), F32)
    for k in range(9):
        ky, kx = divmod(k, 3)
        put = jnp.where(iota((48, 4), 0) == kx * 16 + ky * 4 + iota((48, 4), 1), 1.0, 0.0).astype(BF16)
        w_rows = w_rows + dot(put, wibuf[k])
    w48[...] = w_rows.astype(BF16)
    for copy in loads[7:]:
        copy.wait()

    def points(i):
        at = pl.ds(pl.multiple_of(i * 16, 16), 16)
        cols = []
        for kx in range(3):
            w0, w1, w2 = (wmbuf[3 * ky + kx, at, :].astype(F32) for ky in range(3))
            even, odd = 0.5 * (w0 + w2), 0.5 * w1
            cols.append((w0, even + odd, even - odd, w2))
        for qy in range(4):
            w0, w1, w2 = (col[qy] for col in cols)
            even, odd = 0.5 * (w0 + w2), 0.5 * w1
            for qx, u in enumerate((w0, even + odd, even - odd, w2)):
                if (qy, qx) in SLOT:
                    upts[SLOT[qy, qx], at, :] = u.astype(BF16)

    each(0, 32, points, 4)

    def taps(qy, qx, d, c):
        if (qy, qx) in SLOT:
            return upts[SLOT[qy, qx], d, c]
        return wmbuf[2 * qy + 2 * qx // 3, d, c]

    total = eacc[pl.ds(pl.multiple_of(32 * me, 32), 48), :]

    def lat_take(j, acc):
        lat_copy(lax.rem(me + j, N), N - j).wait_recv()
        return acc + recv[N - j].astype(F32)

    total = lax.fori_loop(1, N, lat_take, total)

    def column(b):
        return jnp.where(b < 64, 2 * b, 2 * b - 127)

    to_halves = jnp.where(iota((128, 128), 0) == column(iota((128, 128), 1)), 1.0, 0.0).astype(BF16)
    to_columns = jnp.where(iota((128, 128), 1) == column(iota((128, 128), 0)), 1.0, 0.0).astype(BF16)

    def from_right(v):
        lane = iota(v.shape, 1)
        v = jnp.where(lane < 64, pltpu.roll(v, 64, 1), pltpu.roll(v, 63, 1))
        return jnp.where(lane == 127, 0.0, v)

    def from_left(v):
        lane = iota(v.shape, 1)
        v = jnp.where(lane < 64, pltpu.roll(v, 65, 1), pltpu.roll(v, 64, 1))
        return jnp.where(lane == 0, 0.0, v)

    lat = dot(total.astype(BF16), to_halves)
    for i, t in enumerate((from_left(lat), lat, from_right(lat))):
        ls[i, 0:48, :] = t
        ls[i, 48:56, :] = jnp.zeros((8, 128), F32)

    def down(v):
        return jnp.where(iota(v.shape, 0) == 0, 0.0, pltpu.roll(v, 1, 0))

    def up(v):
        return jnp.where(iota(v.shape, 0) == 63, 0.0, pltpu.roll(v, 63, 0))

    def combine(m0, m1, m2, m3):
        return m0 + m1 + m2, m1 - m2 - m3

    def scatter(p0, p1, p2, p3):
        return p0, p1 - p2 - p3, p1 + p2 - p0, p3

    def hidden(r):
        at = slice(4 * r, 4 * r + 16)
        x48 = jnp.concatenate([ls[0, at, :], ls[1, at, :], ls[2, at, :]], axis=0)
        pre = dot(x48.T.astype(BF16), w48[...]) + bibuf[...]
        row = 8 * me - 1 + r
        half = jnp.where(jnp.logical_and(row >= 0, row < 128), 0.5, 0.0)
        sig = half * jnp.tanh(0.5 * pre) + half
        act = pre * sig
        s1[r * 128 : (r + 1) * 128, :] = sig + act * (1.0 - sig)
        return act

    acts = {}
    for p in range(4):
        for r in range(2 * p, 2 * p + 4):
            if r not in acts:
                acts[r] = hidden(r)
        d0, d1, d2, d3 = (acts[2 * p + i] for i in range(4))
        for qy, t in enumerate((d0 - d2, d1 + d2, d2 - d1, d1 - d3)):
            even, odd = t[0:64], t[64:128]
            for qx, u in enumerate((down(odd) - odd, even + odd, odd - even, even - up(even))):
                t3[4 * qy + qx, p * 64 : p * 64 + 64, :] = u.astype(BF16)

    HALF = 512 // 2

    def channels(n):
        return slice(n * HALF, (n + 1) * HALF)

    def forward(n, qy):
        for qx in range(4):
            mm[n % 2, 4 * qy + qx] = dot_nt(t3[4 * qy + qx], taps(qy, qx, channels(n), slice(None)))

    def mixed(n, p):
        at, ch = slice(p * 64, p * 64 + 64), channels(n)
        grads = []
        sums = [combine(*(mm[n % 2, 4 * qy + qx, at, :] for qx in range(4))) for qy in range(4)]
        for side in range(2):
            m0, m1, m2, m3 = (pair[side] for pair in sums)
            out = []
            for pre in combine(m0, m1 + bmbuf[:, ch], m2, m3):
                sig = 0.5 * jnp.tanh(0.5 * pre) + 0.5
                out.append(hbuf[:, ch] * (sig + (pre * sig) * (1.0 - sig)))
            g0, g1 = out
            grads.append((g0, g0 + g1, g0 - g1, g1))
        for qy in range(4):
            even, odd = grads[0][qy], grads[1][qy]
            for qx, u in enumerate((even, even + odd, even - odd, odd)):
                x3[4 * qy + qx, at, ch] = u.astype(BF16)

    for n in range(2):
        for qy in range(4):
            forward(n, qy)
            if n > 0:
                mixed(n - 1, qy)
    for p in range(4):
        mixed(2 - 1, p)

    lacc[...] = jnp.zeros((56, 128), F32)

    def latent_rows(n, r, val):
        at, ch = slice(r * 128, (r + 1) * 128), channels(n)
        gbuf[at, ch] = (val * s1[at, ch]).astype(BF16)

    def finish(n, r, p0, p1, p2, p3):
        c0, c1, c2, c3 = scatter(p0, p1, p2, p3)
        latent_rows(n, r, jnp.concatenate([c1 + down(c3), c2 + up(c0)], axis=0))

    def backward(n, qy):
        for qx in range(4):
            mm[n % 2, 4 * qy + qx] = dot(x3[4 * qy + qx], taps(qy, qx, slice(None), channels(n)))

    def give(n, p, carry):
        at = slice(p * 64, p * 64 + 64)
        given = [scatter(*(mm[n % 2, 4 * qy + qx, at, :] for qy in range(4))) for qx in range(4)]
        if carry is not None:
            given = [(g[0] + c[0], g[1] + c[1], g[2], g[3]) for g, c in zip(given, carry)]
        finish(n, 2 * p, *(g[0] for g in given))
        finish(n, 2 * p + 1, *(g[1] for g in given))
        carry = [(g[2], g[3]) for g in given]
        if p == 3:
            finish(n, 8, *(c[0] for c in carry))
            finish(n, 9, *(c[1] for c in carry))
        return carry

    carry = None
    for n in range(2):
        for qy in range(4):
            backward(n, qy)
            if n > 0:
                carry = give(n - 1, qy, carry)
        carry = None
    for p in range(4):
        carry = give(2 - 1, p, carry)
    lat_parts = dot_nt(w48[...], gbuf[...])
    for r in range(10):
        q = lat_parts[:, r * 128 : (r + 1) * 128]
        at = slice(4 * r, 4 * r + 16)
        lacc[at, :] = lacc[at, :] + (q[16:32] + from_right(q[0:16]) + from_left(q[32:48]))
    ngblk[...] = dot((-ratio * lacc[0:48, :]).astype(BF16), to_columns).astype(BF16)

    def ng_copy(peer, slot):
        return pltpu.make_async_remote_copy(
            src_ref=ngblk,
            dst_ref=grecv.at[slot],
            send_sem=gsend_sem.at[peer],
            recv_sem=grecv_sem.at[slot],
            device_id={"mp": peer},
            device_id_type=MESH,
        )

    def add_rows(peer):
        at = rows(32 * peer, 16, 48)
        v = grecv[peer].astype(F32)
        ns[0, at, :] = ns[0, at, :] + left(v)
        ns[1, at, :] = ns[1, at, :] + v
        ns[2, at, :] = ns[2, at, :] + right(v)

    for peer in mp_peers:
        ng_copy(peer, me).start()
    grecv[me] = ngblk[...]
    ns[...] = jnp.zeros((3, 528, 128), F32)
    add_rows(me)
    for peer in reversed(mp_peers):
        ng_copy(peer, peer).wait_recv()
        add_rows(peer)
    ns[:, 0:8, :] = jnp.zeros((3, 8, 128), F32)
    ns[:, 520:528, :] = jnp.zeros((3, 8, 128), F32)

    def columns(b, acc):
        parts = []
        for i in range(CHUNK // 128):
            at = pl.ds(4 * (b * (CHUNK // 128) + i) + 4, 16)
            parts.append(jnp.concatenate([ns[k, at, :].astype(BF16) for k in range(3)], axis=0))
        block = jnp.concatenate(parts, axis=1)
        at = rows(b * CHUNK, CHUNK)
        im[:, at] = block
        return acc + dot_nt(f2[:, at], block)

    wg = lax.fori_loop(0, 16384 // CHUNK, columns, jnp.zeros((32, 48), F32), unroll=8)
    wg = jnp.concatenate([wg[0:24], jnp.zeros((24, 80), F32)], axis=1)
    lane = iota((24, 128), 1)
    ordered = jnp.zeros((24, 128), F32)
    for k in range(9):
        ky, kx = divmod(k, 3)
        moved = pltpu.roll(wg, (4 * k - kx * 16 - (2 - ky) * 4) % 128, 1)
        ordered = jnp.where(jnp.logical_and(lane >= 4 * k, lane < 4 * k + 4), moved, ordered)
    wrecv[my_dp] = ordered[0:8] + pltpu.roll(ordered[8:16], 40, 1) + pltpu.roll(ordered[16:24], 80, 1)

    def wg_copy(peer, slot):
        return pltpu.make_async_remote_copy(
            src_ref=wrecv.at[my_dp],
            dst_ref=wrecv.at[slot],
            send_sem=wsend_sem.at[peer],
            recv_sem=wrecv_sem.at[slot],
            device_id={"dp": peer},
            device_id_type=MESH,
        )

    def wg_take(j):
        peer = lax.rem(my_dp + j, N)
        wg_copy(peer, peer).wait_recv()

    for peer in dp_peers:
        wg_copy(peer, my_dp).start()

    e_cols = e48t[...].astype(BF16)

    def feature(b):
        p = dot(e_cols, im[:, rows(b * CHUNK, CHUNK)])
        for i in range(CHUNK // 128):
            stage[pl.ds(b * (CHUNK // 128) + i, 24, stride=STRIDE), :] = p[0:24, i * 128 : (i + 1) * 128]

    each(0, 16384 // CHUNK, feature, 16)
    for c in range(20):
        fg_out[0, c] = stage[c * STRIDE : c * STRIDE + 128, :].astype(BF16)
    def sent(j):
        lat_copy(lax.rem(me + j, N), j).wait_send()
        ng_copy(lax.rem(me + j, N), me).wait_send()

    each(1, N, sent)
    each(1, N, wg_take)
    acc = wrecv[0]
    for s in range(1, N):
        acc = acc + wrecv[s]
    acc = acc * (1.0 / 16384.0)
    wg_out[0:8, :] = acc[:, 0:36]
    wg_out[8:16, :] = pltpu.roll(acc, 88, 1)[:, 0:36]
    wg_out[16:20, :] = pltpu.roll(acc, 48, 1)[0:4, 0:36]
    each(1, N, lambda j: wg_copy(lax.rem(my_dp + j, N), my_dp).wait_send())


def publish(fg, wg, fg_out, wg_out, sem):
    copies = [pltpu.make_async_copy(fg, fg_out, sem.at[0]), pltpu.make_async_copy(wg, wg_out, sem.at[1])]
    for copy in copies:
        copy.start()
    for copy in copies:
        copy.wait()


def body(features, w_out, noisy_latent, timestep, w_in, b_in, w_mid, b_mid, reward_head):
    hbm = pl.BlockSpec(memory_space=pltpu.HBM)
    vmem = pl.BlockSpec(memory_space=pltpu.VMEM)
    dma = pltpu.SemaphoreType.DMA
    shapes = (jax.ShapeDtypeStruct((1, 20, 128, 128), BF16), jax.ShapeDtypeStruct((20, 36), F32))
    fg, wg = pl.pallas_call(
        kernel,
        out_shape=(pltpu.VMEM(shapes[0].shape, BF16), pltpu.VMEM(shapes[1].shape, F32)),
        in_specs=[hbm] * 10,
        out_specs=(vmem, vmem),
        scratch_shapes=[
            pltpu.VMEM((1, 20, 128, 128), BF16),
            pltpu.VMEM((20, 36), BF16),
            pltpu.VMEM((1, 4, 8, 128), F32),
            pltpu.SMEM((1,), jnp.int32),
            pltpu.VMEM((8, 128), F32),
            pltpu.VMEM((9, 4, 512), BF16),
            pltpu.VMEM((1, 512), F32),
            pltpu.VMEM((9, 512, 512), BF16),
            pltpu.VMEM((1, 512), F32),
            pltpu.VMEM((1, 512), F32),
            pltpu.VMEM((24 * STRIDE, 128), F32),
            pltpu.VMEM((32, 16384), BF16),
            pltpu.VMEM((130 * 16, 128), F32),
            pltpu.VMEM((528, 128), F32),
            pltpu.VMEM((32, 128), F32),
            pltpu.VMEM((528, 128), BF16),
            pltpu.VMEM((N, 48, 128), BF16),
            pltpu.VMEM((48, 32), F32),
            pltpu.VMEM((32, 48), F32),
            pltpu.VMEM((48, 512), BF16),
            pltpu.VMEM((3, 56, 128), F32),
            pltpu.VMEM((12, 512, 512), BF16),
            pltpu.VMEM((16, 256, 512), BF16),
            pltpu.VMEM((10 * 128, 512), F32),
            pltpu.VMEM((16, 256, 512), BF16),
            pltpu.VMEM((10 * 128, 512), BF16),
            pltpu.VMEM((2, 16, 256, 512 // 2), F32),
            pltpu.VMEM((56, 128), F32),
            pltpu.VMEM((48, 128), BF16),
            pltpu.VMEM((N, 48, 128), BF16),
            pltpu.VMEM((3, 528, 128), F32),
            pltpu.VMEM((48, 16384), BF16),
            pltpu.VMEM((N, 8, 128), F32),
            dma((10,)), dma((N,)), dma((N,)), dma((N,)), dma((N,)), dma((N,)), dma((N,)),
        ],
        compiler_params=pltpu.CompilerParams(collective_id=0, has_side_effects=True, vmem_limit_bytes=56 << 20),
        name="step",
    )(
        features, w_out, noisy_latent, timestep, jnp.asarray(noise_table()), w_in.transpose(0, 2, 1),
        b_in.reshape(1, 512), w_mid, b_mid.reshape(1, 512), reward_head.reshape(1, 512),
    )
    return pl.pallas_call(
        publish,
        out_shape=shapes,
        in_specs=[vmem, vmem],
        out_specs=(hbm, hbm),
        scratch_shapes=[dma((2,))],
        compiler_params=pltpu.CompilerParams(vmem_limit_bytes=1 << 20),
        name="publish",
    )(fg, wg)


def solution(mesh):
    in_specs = (
        P("dp", "mp", None, None), P("mp", None), P("dp", None, "mp", None), P("dp"), P(), P(), P(), P(), P(),
    )
    out_specs = (P("dp", "mp", None, None), P("mp", None))
    return jax.shard_map(body, mesh=mesh, in_specs=in_specs, out_specs=out_specs, check_vma=False)
```

```python
import jax
import jax.numpy as jnp
import numpy as np
from jax import lax
from jax.experimental import pallas as pl
from jax.experimental.pallas import tpu as pltpu
from jax.sharding import PartitionSpec as P

F32 = jnp.float32
BF16 = jnp.bfloat16
MESH = pl.DeviceIdType.MESH
N = 16
STRIDE = 136
CHUNK = 1024
NT = (((1,), (1,)), ((), ()))


MP_FAR = sorted(
    ((z, y, c) for z in range(2) for y in range(4) for c in range(2) if z or y or c),
    key=lambda d: -4 * (d[0] + min(d[1], 4 - d[1])) - d[2],
)
DP_FAR = sorted(
    ((x, z) for x in range(4) for z in range(4) if x or z),
    key=lambda d: -min(d[0], 4 - d[0]) - 2 * min(d[1], 4 - d[1]),
)


SLOT = {q: i for i, q in enumerate((a, b) for a in range(4) for b in range(4) if a % 3 or b % 3)}


def noise_table():
    betas = np.linspace(0.00085**0.5, 0.012**0.5, 1000, dtype=np.float32) ** 2
    table = np.cumprod((1.0 - betas).astype(np.float32), dtype=np.float32)
    return np.pad(table, (0, 24)).reshape(8, 128)


def iota(shape, dim):
    return lax.broadcasted_iota(jnp.int32, shape, dim)


def dot(a, b):
    return jnp.dot(a, b, preferred_element_type=F32)


def dot_nt(a, b):
    return lax.dot_general(a, b, NT, preferred_element_type=F32)


def right(v):
    return jnp.where(iota(v.shape, 1) == 0, 0.0, pltpu.roll(v, 1, 1))


def left(v):
    return jnp.where(iota(v.shape, 1) == 127, 0.0, pltpu.roll(v, 127, 1))


def rows(start, size):
    return pl.ds(pl.multiple_of(start, size), size)


def each(lo, hi, step, unroll=1):
    def run(j, c):
        step(j)
        return c

    lax.fori_loop(lo, hi, run, 0, unroll=unroll)


def kernel(
    feat, w_out, noisy, tstep, table, w_in, b_in, w_mid, b_mid, head,
    fg_out, wg_out,
    fbuf, wobuf, nbuf, tbuf, tabbuf, wibuf, bibuf, wmbuf, bmbuf, hbuf,
    stage, f2, rs, eacc, nz, eloc, recv, e48, e48t, w48, ls,
    upts, t3, s1, x3, gbuf, mm, lacc, ngblk, grecv, ns, im, wrecv,
    in_sem, send_sem, recv_sem, gsend_sem, grecv_sem, wsend_sem, wrecv_sem,
):
    me = lax.axis_index("mp")
    my_dp = lax.axis_index("dp")
    pairs = ((feat, fbuf), (w_out, wobuf), (noisy, nbuf), (tstep, tbuf), (table, tabbuf),
             (w_in, wibuf), (b_in, bibuf), (b_mid, bmbuf), (head, hbuf), (w_mid, wmbuf))
    mp_peers = [
        lax.rem(me // 8 + z, 2) * 8 + lax.rem(lax.rem(me // 2, 4) + y, 4) * 2 + lax.rem(lax.rem(me, 2) + c, 2)
        for z, y, c in MP_FAR
    ]
    dp_peers = [lax.rem(my_dp // 4 + x, 4) * 4 + lax.rem(lax.rem(my_dp, 4) + z, 4) for x, z in DP_FAR]
    loads = [pltpu.make_async_copy(src, dst, in_sem.at[i]) for i, (src, dst) in enumerate(pairs)]
    for copy in loads[:-1]:
        copy.start()
    barrier = pltpu.get_barrier_semaphore()

    def greet(j):
        pl.semaphore_signal(barrier, inc=1, device_id={"mp": lax.rem(me + j, N)}, device_id_type=MESH)
        pl.semaphore_signal(barrier, inc=1, device_id={"dp": lax.rem(my_dp + j, N)}, device_id_type=MESH)

    each(1, N, greet)

    for copy in loads[1:5]:
        copy.wait()
    level = jnp.sum(
        jnp.where(iota((8, 128), 0) * 128 + iota((8, 128), 1) == tbuf[0], tabbuf[...], 0.0), keepdims=True
    )
    root_a = jnp.sqrt(level)
    root_b = jnp.sqrt(1.0 - level)
    ratio = root_b / root_a

    def tap_column(b):
        j = lax.shift_right_logical(b, 2) & 3
        k = 3 * (2 - j) + lax.shift_right_logical(b, 4)
        return jnp.where(j < 3, 4 * k + (b & 3), -1)

    pick = jnp.where(iota((36, 48), 0) == tap_column(iota((36, 48), 1)), 1.0, 0.0).astype(BF16)
    pick_t = jnp.where(iota((48, 36), 1) == tap_column(iota((48, 36), 0)), 1.0, 0.0).astype(BF16)
    e48t[...] = jnp.zeros((32, 48), F32)
    e48t[0:20, :] = dot(wobuf[...], pick)
    e48[...] = jnp.zeros((48, 32), F32)
    e48[:, 0:20] = dot_nt(pick_t, wobuf[...])

    loads[0].wait()
    loads[-1].start()
    for c in range(20):
        stage[c * STRIDE : c * STRIDE + 128, :] = fbuf[0, c].astype(F32)
    for c in range(20, 24):
        stage[c * STRIDE : c * STRIDE + 128, :] = jnp.zeros((128, 128), F32)
    rs[0:16, :] = jnp.zeros((16, 128), F32)
    rs[129 * 16 : 130 * 16, :] = jnp.zeros((16, 128), F32)
    e_rows = e48[...].astype(BF16)

    def unet_rows(b):
        parts = []
        for i in range(CHUNK // 128):
            v = stage[pl.ds(b * (CHUNK // 128) + i, 24, stride=STRIDE), :]
            parts.append(jnp.concatenate([v, jnp.zeros((8, 128), F32)], axis=0).astype(BF16))
        block = jnp.concatenate(parts, axis=1)
        f2[:, rows(b * CHUNK, CHUNK)] = block
        p = dot(e_rows, block)
        for i in range(CHUNK // 128):
            q = p[:, i * 128 : (i + 1) * 128]
            y = b * (CHUNK // 128) + i
            rs[rows((y + 1) * 16, 16), :] = q[16:32] + right(q[0:16]) + left(q[32:48])

    each(0, 16384 // CHUNK, unet_rows, 4)

    for o in range(4):
        nz[pl.ds(o, 8, stride=4), :] = nbuf[0, o]
    eacc[0:8, :] = jnp.zeros((8, 128), F32)
    eacc[520:528, :] = jnp.zeros((8, 128), F32)
    low = iota((8, 128), 0) < 4

    def unet_pairs(b):
        def at(y, half):
            return rs[rows((y + 1) * 16 + 8 * half, 8), :]

        for i in range(4):
            y = 8 * b + 2 * i
            e = at(y + 1, 0)
            e += jnp.where(low, pltpu.roll(at(y, 0), 4, 0), pltpu.roll(at(y, 1), 4, 0))
            e += jnp.where(low, at(y - 1, 1), pltpu.roll(at(y + 2, 0), 4, 0))
            eacc[rows(8 + 4 * y, 8), :] = -ratio * e

    each(0, 16, unet_pairs)
    mine = pl.ds(pl.multiple_of(8 + 32 * me, 8), 32)
    eacc[mine, :] = eacc[mine, :] + nz[...] / root_a
    eloc[...] = eacc[...].astype(BF16)

    def lat_copy(dest, slot):
        return pltpu.make_async_remote_copy(
            src_ref=eloc.at[pl.ds(pl.multiple_of(32 * dest, 32), 48), :],
            dst_ref=recv.at[slot],
            send_sem=send_sem.at[slot],
            recv_sem=recv_sem.at[slot],
            device_id={"mp": dest},
            device_id_type=MESH,
        )

    pl.semaphore_wait(barrier, 2 * (N - 1))
    for j, peer in enumerate(mp_peers):
        lat_copy(peer, j + 1).start()

    loads[5].wait()
    loads[6].wait()
    w_rows = jnp.zeros((48, 512), F32)
    for k in range(9):
        ky, kx = divmod(k, 3)
        put = jnp.where(iota((48, 4), 0) == kx * 16 + ky * 4 + iota((48, 4), 1), 1.0, 0.0).astype(BF16)
        w_rows = w_rows + dot(put, wibuf[k])
    w48[...] = w_rows.astype(BF16)
    for copy in loads[7:]:
        copy.wait()

    def points(i):
        at = pl.ds(pl.multiple_of(i * 16, 16), 16)
        cols = []
        for kx in range(3):
            w0, w1, w2 = (wmbuf[3 * ky + kx, at, :].astype(F32) for ky in range(3))
            even, odd = 0.5 * (w0 + w2), 0.5 * w1
            cols.append((w0, even + odd, even - odd, w2))
        for qy in range(4):
            w0, w1, w2 = (col[qy] for col in cols)
            even, odd = 0.5 * (w0 + w2), 0.5 * w1
            for qx, u in enumerate((w0, even + odd, even - odd, w2)):
                if (qy, qx) in SLOT:
                    upts[SLOT[qy, qx], at, :] = u.astype(BF16)

    each(0, 32, points, 4)

    def taps(qy, qx, d, c):
        if (qy, qx) in SLOT:
            return upts[SLOT[qy, qx], d, c]
        return wmbuf[2 * qy + 2 * qx // 3, d, c]

    total = eacc[pl.ds(pl.multiple_of(32 * me, 32), 48), :]

    def lat_take(j, acc):
        lat_copy(lax.rem(me + j, N), j).wait_recv()
        return acc + recv[j].astype(F32)

    total = lax.fori_loop(1, N, lat_take, total)

    def column(b):
        return jnp.where(b < 64, 2 * b, 2 * b - 127)

    to_halves = jnp.where(iota((128, 128), 0) == column(iota((128, 128), 1)), 1.0, 0.0).astype(BF16)
    to_columns = jnp.where(iota((128, 128), 1) == column(iota((128, 128), 0)), 1.0, 0.0).astype(BF16)

    def from_right(v):
        lane = iota(v.shape, 1)
        v = jnp.where(lane < 64, pltpu.roll(v, 64, 1), pltpu.roll(v, 63, 1))
        return jnp.where(lane == 127, 0.0, v)

    def from_left(v):
        lane = iota(v.shape, 1)
        v = jnp.where(lane < 64, pltpu.roll(v, 65, 1), pltpu.roll(v, 64, 1))
        return jnp.where(lane == 0, 0.0, v)

    lat = dot(total.astype(BF16), to_halves)
    for i, t in enumerate((from_left(lat), lat, from_right(lat))):
        ls[i, 0:48, :] = t
        ls[i, 48:56, :] = jnp.zeros((8, 128), F32)

    def down(v):
        return jnp.where(iota(v.shape, 0) == 0, 0.0, pltpu.roll(v, 1, 0))

    def up(v):
        return jnp.where(iota(v.shape, 0) == 63, 0.0, pltpu.roll(v, 63, 0))

    def combine(m0, m1, m2, m3):
        return m0 + m1 + m2, m1 - m2 - m3

    def scatter(p0, p1, p2, p3):
        return p0, p1 - p2 - p3, p1 + p2 - p0, p3

    def hidden(r):
        at = slice(4 * r, 4 * r + 16)
        x48 = jnp.concatenate([ls[0, at, :], ls[1, at, :], ls[2, at, :]], axis=0)
        pre = dot(x48.T.astype(BF16), w48[...]) + bibuf[...]
        row = 8 * me - 1 + r
        half = jnp.where(jnp.logical_and(row >= 0, row < 128), 0.5, 0.0)
        sig = half * jnp.tanh(0.5 * pre) + half
        act = pre * sig
        s1[r * 128 : (r + 1) * 128, :] = sig + act * (1.0 - sig)
        return act

    acts = {}
    for p in range(4):
        for r in range(2 * p, 2 * p + 4):
            if r not in acts:
                acts[r] = hidden(r)
        d0, d1, d2, d3 = (acts[2 * p + i] for i in range(4))
        for qy, t in enumerate((d0 - d2, d1 + d2, d2 - d1, d1 - d3)):
            even, odd = t[0:64], t[64:128]
            for qx, u in enumerate((down(odd) - odd, even + odd, odd - even, even - up(even))):
                t3[4 * qy + qx, p * 64 : p * 64 + 64, :] = u.astype(BF16)

    HALF = 512 // 2

    def channels(n):
        return slice(n * HALF, (n + 1) * HALF)

    def forward(n, qy):
        for qx in range(4):
            mm[n % 2, 4 * qy + qx] = dot_nt(t3[4 * qy + qx], taps(qy, qx, channels(n), slice(None)))

    def mixed(n, p):
        at, ch = slice(p * 64, p * 64 + 64), channels(n)
        grads = []
        sums = [combine(*(mm[n % 2, 4 * qy + qx, at, :] for qx in range(4))) for qy in range(4)]
        for side in range(2):
            m0, m1, m2, m3 = (pair[side] for pair in sums)
            out = []
            for pre in combine(m0, m1 + bmbuf[:, ch], m2, m3):
                sig = 0.5 * jnp.tanh(0.5 * pre) + 0.5
                out.append(hbuf[:, ch] * (sig + (pre * sig) * (1.0 - sig)))
            g0, g1 = out
            grads.append((g0, g0 + g1, g0 - g1, g1))
        for qy in range(4):
            even, odd = grads[0][qy], grads[1][qy]
            for qx, u in enumerate((even, even + odd, even - odd, odd)):
                x3[4 * qy + qx, at, ch] = u.astype(BF16)

    for n in range(2):
        for qy in range(4):
            forward(n, qy)
            if n > 0:
                mixed(n - 1, qy)
    for p in range(4):
        mixed(2 - 1, p)

    lacc[...] = jnp.zeros((56, 128), F32)

    def latent_rows(n, r, val):
        at, ch = slice(r * 128, (r + 1) * 128), channels(n)
        gbuf[at, ch] = (val * s1[at, ch]).astype(BF16)

    def finish(n, r, p0, p1, p2, p3):
        c0, c1, c2, c3 = scatter(p0, p1, p2, p3)
        latent_rows(n, r, jnp.concatenate([c1 + down(c3), c2 + up(c0)], axis=0))

    def backward(n, qy):
        for qx in range(4):
            mm[n % 2, 4 * qy + qx] = dot(x3[4 * qy + qx], taps(qy, qx, slice(None), channels(n)))

    def give(n, p, carry):
        at = slice(p * 64, p * 64 + 64)
        given = [scatter(*(mm[n % 2, 4 * qy + qx, at, :] for qy in range(4))) for qx in range(4)]
        if carry is not None:
            given = [(g[0] + c[0], g[1] + c[1], g[2], g[3]) for g, c in zip(given, carry)]
        finish(n, 2 * p, *(g[0] for g in given))
        finish(n, 2 * p + 1, *(g[1] for g in given))
        carry = [(g[2], g[3]) for g in given]
        if p == 3:
            finish(n, 8, *(c[0] for c in carry))
            finish(n, 9, *(c[1] for c in carry))
        return carry

    carry = None
    for n in range(2):
        for qy in range(4):
            backward(n, qy)
            if n > 0:
                carry = give(n - 1, qy, carry)
        carry = None
    for p in range(4):
        carry = give(2 - 1, p, carry)
    lat_parts = dot_nt(w48[...], gbuf[...])
    for r in range(10):
        q = lat_parts[:, r * 128 : (r + 1) * 128]
        at = slice(4 * r, 4 * r + 16)
        lacc[at, :] = lacc[at, :] + (q[16:32] + from_right(q[0:16]) + from_left(q[32:48]))
    ngblk[...] = dot((-ratio * lacc[0:48, :]).astype(BF16), to_columns).astype(BF16)

    def ng_copy(peer, slot):
        return pltpu.make_async_remote_copy(
            src_ref=ngblk,
            dst_ref=grecv.at[slot],
            send_sem=gsend_sem.at[peer],
            recv_sem=grecv_sem.at[slot],
            device_id={"mp": peer},
            device_id_type=MESH,
        )

    def ng_take(j):
        peer = lax.rem(me + j, N)
        ng_copy(peer, peer).wait_recv()

    for peer in mp_peers:
        ng_copy(peer, me).start()
    grecv[me] = ngblk[...]
    ns[:, 0:8, :] = jnp.zeros((3, 8, 128), F32)
    ns[:, 512:528, :] = jnp.zeros((3, 16, 128), F32)
    each(1, N, ng_take)

    def shift(s, c):
        at = pl.ds(4 + 32 * s, 32)
        v = grecv[s].astype(F32)
        above = jnp.where(s > 0, grecv[jnp.maximum(s - 1, 0), 40 - 8 : 48].astype(F32)[8:16], 0.0)
        below = jnp.where(s < N - 1, grecv[jnp.minimum(s + 1, N - 1), 0:16].astype(F32)[0:8], 0.0)
        v = jnp.concatenate([v[8:16] + above, v[16:32], v[32:40] + below], axis=0)
        ns[0, at, :] = left(v)
        ns[1, at, :] = v
        ns[2, at, :] = right(v)
        return c

    lax.fori_loop(0, N, shift, 0, unroll=16)

    def columns(b, acc):
        parts = []
        for i in range(CHUNK // 128):
            at = pl.ds(4 * (b * (CHUNK // 128) + i), 16)
            parts.append(jnp.concatenate([ns[k, at, :].astype(BF16) for k in range(3)], axis=0))
        block = jnp.concatenate(parts, axis=1)
        at = rows(b * CHUNK, CHUNK)
        im[:, at] = block
        return acc + dot_nt(f2[:, at], block)

    wg = lax.fori_loop(0, 16384 // CHUNK, columns, jnp.zeros((32, 48), F32), unroll=8)
    wg = jnp.concatenate([wg[0:24], jnp.zeros((24, 80), F32)], axis=1)
    lane = iota((24, 128), 1)
    ordered = jnp.zeros((24, 128), F32)
    for k in range(9):
        ky, kx = divmod(k, 3)
        moved = pltpu.roll(wg, (4 * k - kx * 16 - (2 - ky) * 4) % 128, 1)
        ordered = jnp.where(jnp.logical_and(lane >= 4 * k, lane < 4 * k + 4), moved, ordered)
    packed = ordered[0:8] + pltpu.roll(ordered[8:16], 40, 1) + pltpu.roll(ordered[16:24], 80, 1)
    wrecv[my_dp] = packed.astype(BF16)

    def wg_copy(peer, slot):
        return pltpu.make_async_remote_copy(
            src_ref=wrecv.at[my_dp],
            dst_ref=wrecv.at[slot],
            send_sem=wsend_sem.at[peer],
            recv_sem=wrecv_sem.at[slot],
            device_id={"dp": peer},
            device_id_type=MESH,
        )

    def wg_take(j):
        peer = lax.rem(my_dp + j, N)
        wg_copy(peer, peer).wait_recv()

    for peer in dp_peers:
        wg_copy(peer, my_dp).start()

    e_cols = e48t[...].astype(BF16)

    def feature(b):
        p = dot(e_cols, im[:, rows(b * CHUNK, CHUNK)])
        for i in range(CHUNK // 128):
            stage[pl.ds(b * (CHUNK // 128) + i, 24, stride=STRIDE), :] = p[0:24, i * 128 : (i + 1) * 128]

    each(0, 16384 // CHUNK, feature, 16)
    for c in range(20):
        fg_out[0, c] = stage[c * STRIDE : c * STRIDE + 128, :].astype(BF16)
    def sent(j):
        lat_copy(lax.rem(me + j, N), j).wait_send()
        ng_copy(lax.rem(me + j, N), me).wait_send()
        wg_copy(lax.rem(my_dp + j, N), my_dp).wait_send()

    each(1, N, sent)
    each(1, N, wg_take)
    acc = wrecv[0].astype(F32)
    for s in range(1, N):
        acc = acc + wrecv[s].astype(F32)
    acc = acc * (1.0 / 16384.0)
    wg_out[0:8, :] = acc[:, 0:36]
    wg_out[8:16, :] = pltpu.roll(acc, 88, 1)[:, 0:36]
    wg_out[16:20, :] = pltpu.roll(acc, 48, 1)[0:4, 0:36]


def publish(fg, wg, fg_out, wg_out, sem):
    copies = [pltpu.make_async_copy(fg, fg_out, sem.at[0]), pltpu.make_async_copy(wg, wg_out, sem.at[1])]
    for copy in copies:
        copy.start()
    for copy in copies:
        copy.wait()


def body(features, w_out, noisy_latent, timestep, w_in, b_in, w_mid, b_mid, reward_head):
    hbm = pl.BlockSpec(memory_space=pltpu.HBM)
    vmem = pl.BlockSpec(memory_space=pltpu.VMEM)
    dma = pltpu.SemaphoreType.DMA
    shapes = (jax.ShapeDtypeStruct((1, 20, 128, 128), BF16), jax.ShapeDtypeStruct((20, 36), F32))
    fg, wg = pl.pallas_call(
        kernel,
        out_shape=(pltpu.VMEM(shapes[0].shape, BF16), pltpu.VMEM(shapes[1].shape, F32)),
        in_specs=[hbm] * 10,
        out_specs=(vmem, vmem),
        scratch_shapes=[
            pltpu.VMEM((1, 20, 128, 128), BF16),
            pltpu.VMEM((20, 36), BF16),
            pltpu.VMEM((1, 4, 8, 128), F32),
            pltpu.SMEM((1,), jnp.int32),
            pltpu.VMEM((8, 128), F32),
            pltpu.VMEM((9, 4, 512), BF16),
            pltpu.VMEM((1, 512), F32),
            pltpu.VMEM((9, 512, 512), BF16),
            pltpu.VMEM((1, 512), F32),
            pltpu.VMEM((1, 512), F32),
            pltpu.VMEM((24 * STRIDE, 128), F32),
            pltpu.VMEM((32, 16384), BF16),
            pltpu.VMEM((130 * 16, 128), F32),
            pltpu.VMEM((528, 128), F32),
            pltpu.VMEM((32, 128), F32),
            pltpu.VMEM((528, 128), BF16),
            pltpu.VMEM((N, 48, 128), BF16),
            pltpu.VMEM((48, 32), F32),
            pltpu.VMEM((32, 48), F32),
            pltpu.VMEM((48, 512), BF16),
            pltpu.VMEM((3, 56, 128), F32),
            pltpu.VMEM((12, 512, 512), BF16),
            pltpu.VMEM((16, 256, 512), BF16),
            pltpu.VMEM((10 * 128, 512), F32),
            pltpu.VMEM((16, 256, 512), BF16),
            pltpu.VMEM((10 * 128, 512), BF16),
            pltpu.VMEM((2, 16, 256, 512 // 2), F32),
            pltpu.VMEM((56, 128), F32),
            pltpu.VMEM((48, 128), BF16),
            pltpu.VMEM((N, 48, 128), BF16),
            pltpu.VMEM((3, 528, 128), F32),
            pltpu.VMEM((48, 16384), BF16),
            pltpu.VMEM((N, 8, 128), BF16),
            dma((10,)), dma((N,)), dma((N,)), dma((N,)), dma((N,)), dma((N,)), dma((N,)),
        ],
        compiler_params=pltpu.CompilerParams(collective_id=0, has_side_effects=True, vmem_limit_bytes=56 << 20),
        name="step",
    )(
        features, w_out, noisy_latent, timestep, jnp.asarray(noise_table()), w_in.transpose(0, 2, 1),
        b_in.reshape(1, 512), w_mid, b_mid.reshape(1, 512), reward_head.reshape(1, 512),
    )
    return pl.pallas_call(
        publish,
        out_shape=shapes,
        in_specs=[vmem, vmem],
        out_specs=(hbm, hbm),
        scratch_shapes=[dma((2,))],
        compiler_params=pltpu.CompilerParams(vmem_limit_bytes=1 << 20),
        name="publish",
    )(fg, wg)


def solution(mesh):
    in_specs = (
        P("dp", "mp", None, None), P("mp", None), P("dp", None, "mp", None), P("dp"), P(), P(), P(), P(), P(),
    )
    out_specs = (P("dp", "mp", None, None), P("mp", None))
    return jax.shard_map(body, mesh=mesh, in_specs=in_specs, out_specs=out_specs, check_vma=False)
```

```python
import jax
import jax.numpy as jnp
import numpy as np
from jax import lax
from jax.experimental import pallas as pl
from jax.experimental.pallas import tpu as pltpu
from jax.sharding import PartitionSpec as P

F32 = jnp.float32
BF16 = jnp.bfloat16
MESH = pl.DeviceIdType.MESH
N = 16
STRIDE = 136
CHUNK = 1024
NT = (((1,), (1,)), ((), ()))


MP_FAR = sorted(
    ((z, y, c) for z in range(2) for y in range(4) for c in range(2) if z or y or c),
    key=lambda d: -4 * (d[0] + min(d[1], 4 - d[1])) - d[2],
)
DP_FAR = sorted(
    ((x, z) for x in range(4) for z in range(4) if x or z),
    key=lambda d: -min(d[0], 4 - d[0]) - 2 * min(d[1], 4 - d[1]),
)


SLOT = {q: i for i, q in enumerate((a, b) for a in range(4) for b in range(4) if a % 3 or b % 3)}


def noise_table():
    betas = np.linspace(0.00085**0.5, 0.012**0.5, 1000, dtype=np.float32) ** 2
    table = np.cumprod((1.0 - betas).astype(np.float32), dtype=np.float32)
    return np.pad(table, (0, 24)).reshape(8, 128)


def iota(shape, dim):
    return lax.broadcasted_iota(jnp.int32, shape, dim)


def dot(a, b):
    return jnp.dot(a, b, preferred_element_type=F32)


def dot_nt(a, b):
    return lax.dot_general(a, b, NT, preferred_element_type=F32)


def right(v):
    return jnp.where(iota(v.shape, 1) == 0, 0.0, pltpu.roll(v, 1, 1))


def left(v):
    return jnp.where(iota(v.shape, 1) == 127, 0.0, pltpu.roll(v, 127, 1))


def rows(start, size):
    return pl.ds(pl.multiple_of(start, size), size)


def each(lo, hi, step, unroll=1):
    def run(j, c):
        step(j)
        return c

    lax.fori_loop(lo, hi, run, 0, unroll=unroll)


def kernel(
    feat, w_out, noisy, tstep, table, w_in, b_in, w_mid, b_mid, head,
    fg_out, wg_out,
    fbuf, wobuf, nbuf, tbuf, tabbuf, wibuf, bibuf, wmbuf, bmbuf, hbuf,
    stage, f2, rs, eacc, nz, eloc, recv, e48, e48t, w48, ls,
    upts, t3, s1, x3, gbuf, mm, lacc, ngblk, grecv, ns, im, wrecv,
    in_sem, send_sem, recv_sem, gsend_sem, grecv_sem, wsend_sem, wrecv_sem,
):
    me = lax.axis_index("mp")
    my_dp = lax.axis_index("dp")
    pairs = ((feat, fbuf), (w_out, wobuf), (noisy, nbuf), (tstep, tbuf), (table, tabbuf),
             (w_in, wibuf), (b_in, bibuf), (b_mid, bmbuf), (head, hbuf), (w_mid, wmbuf))
    mp_peers = [
        lax.rem(me // 8 + z, 2) * 8 + lax.rem(lax.rem(me // 2, 4) + y, 4) * 2 + lax.rem(lax.rem(me, 2) + c, 2)
        for z, y, c in MP_FAR
    ]
    dp_peers = [lax.rem(my_dp // 4 + x, 4) * 4 + lax.rem(lax.rem(my_dp, 4) + z, 4) for x, z in DP_FAR]
    loads = [pltpu.make_async_copy(src, dst, in_sem.at[i]) for i, (src, dst) in enumerate(pairs)]
    for copy in loads[:-1]:
        copy.start()
    barrier = pltpu.get_barrier_semaphore()

    for peer in dp_peers:
        pl.semaphore_signal(barrier, inc=1, device_id={"dp": peer}, device_id_type=MESH)
    for peer in mp_peers:
        pl.semaphore_signal(barrier, inc=1, device_id={"mp": peer}, device_id_type=MESH)

    for copy in loads[1:5]:
        copy.wait()
    level = jnp.sum(
        jnp.where(iota((8, 128), 0) * 128 + iota((8, 128), 1) == tbuf[0], tabbuf[...], 0.0), keepdims=True
    )
    root_a = jnp.sqrt(level)
    root_b = jnp.sqrt(1.0 - level)
    ratio = root_b / root_a

    def tap_column(b):
        j = lax.shift_right_logical(b, 2) & 3
        k = 3 * (2 - j) + lax.shift_right_logical(b, 4)
        return jnp.where(j < 3, 4 * k + (b & 3), -1)

    pick = jnp.where(iota((36, 48), 0) == tap_column(iota((36, 48), 1)), 1.0, 0.0).astype(BF16)
    pick_t = jnp.where(iota((48, 36), 1) == tap_column(iota((48, 36), 0)), 1.0, 0.0).astype(BF16)
    e48t[...] = jnp.zeros((32, 48), F32)
    e48t[0:20, :] = dot(wobuf[...], pick)
    e48[...] = jnp.zeros((48, 32), F32)
    e48[:, 0:20] = dot_nt(pick_t, wobuf[...])

    loads[0].wait()
    loads[-1].start()
    for c in range(20):
        stage[c * STRIDE : c * STRIDE + 128, :] = fbuf[0, c].astype(F32)
    for c in range(20, 24):
        stage[c * STRIDE : c * STRIDE + 128, :] = jnp.zeros((128, 128), F32)
    rs[0:16, :] = jnp.zeros((16, 128), F32)
    rs[129 * 16 : 130 * 16, :] = jnp.zeros((16, 128), F32)
    e_rows = e48[...].astype(BF16)

    def unet_rows(b):
        parts = []
        for i in range(CHUNK // 128):
            v = stage[pl.ds(b * (CHUNK // 128) + i, 24, stride=STRIDE), :]
            parts.append(jnp.concatenate([v, jnp.zeros((8, 128), F32)], axis=0).astype(BF16))
        block = jnp.concatenate(parts, axis=1)
        f2[:, rows(b * CHUNK, CHUNK)] = block
        p = dot(e_rows, block)
        for i in range(CHUNK // 128):
            q = p[:, i * 128 : (i + 1) * 128]
            y = b * (CHUNK // 128) + i
            rs[rows((y + 1) * 16, 16), :] = q[16:32] + right(q[0:16]) + left(q[32:48])

    each(0, 16384 // CHUNK, unet_rows, 4)

    for o in range(4):
        nz[pl.ds(o, 8, stride=4), :] = nbuf[0, o]
    eacc[0:8, :] = jnp.zeros((8, 128), F32)
    eacc[520:528, :] = jnp.zeros((8, 128), F32)
    low = iota((8, 128), 0) < 4

    def unet_pairs(b):
        def at(y, half):
            return rs[rows((y + 1) * 16 + 8 * half, 8), :]

        for i in range(4):
            y = 8 * b + 2 * i
            e = at(y + 1, 0)
            e += jnp.where(low, pltpu.roll(at(y, 0), 4, 0), pltpu.roll(at(y, 1), 4, 0))
            e += jnp.where(low, at(y - 1, 1), pltpu.roll(at(y + 2, 0), 4, 0))
            eacc[rows(8 + 4 * y, 8), :] = -ratio * e

    each(0, 16, unet_pairs)
    mine = pl.ds(pl.multiple_of(8 + 32 * me, 8), 32)
    eacc[mine, :] = eacc[mine, :] + nz[...] / root_a
    eloc[...] = eacc[...].astype(BF16)

    def lat_copy(dest, slot):
        return pltpu.make_async_remote_copy(
            src_ref=eloc.at[pl.ds(pl.multiple_of(32 * dest, 32), 48), :],
            dst_ref=recv.at[slot],
            send_sem=send_sem.at[slot],
            recv_sem=recv_sem.at[slot],
            device_id={"mp": dest},
            device_id_type=MESH,
        )

    pl.semaphore_wait(barrier, 2 * (N - 1))
    for j, peer in enumerate(mp_peers):
        lat_copy(peer, j + 1).start()

    loads[5].wait()
    loads[6].wait()
    w_rows = jnp.zeros((48, 512), F32)
    for k in range(9):
        ky, kx = divmod(k, 3)
        put = jnp.where(iota((48, 4), 0) == kx * 16 + ky * 4 + iota((48, 4), 1), 1.0, 0.0).astype(BF16)
        w_rows = w_rows + dot(put, wibuf[k])
    w48[...] = w_rows.astype(BF16)
    for copy in loads[7:]:
        copy.wait()

    def points(i):
        at = pl.ds(pl.multiple_of(i * 16, 16), 16)
        cols = []
        for kx in range(3):
            w0, w1, w2 = (wmbuf[3 * ky + kx, at, :].astype(F32) for ky in range(3))
            even, odd = 0.5 * (w0 + w2), 0.5 * w1
            cols.append((w0, even + odd, even - odd, w2))
        for qy in range(4):
            w0, w1, w2 = (col[qy] for col in cols)
            even, odd = 0.5 * (w0 + w2), 0.5 * w1
            for qx, u in enumerate((w0, even + odd, even - odd, w2)):
                if (qy, qx) in SLOT:
                    upts[SLOT[qy, qx], at, :] = u.astype(BF16)

    each(0, 32, points, 4)

    def taps(qy, qx, d, c):
        if (qy, qx) in SLOT:
            return upts[SLOT[qy, qx], d, c]
        return wmbuf[2 * qy + 2 * qx // 3, d, c]

    total = eacc[pl.ds(pl.multiple_of(32 * me, 32), 48), :]

    def lat_take(j, acc):
        lat_copy(lax.rem(me + j, N), j).wait_recv()
        return acc + recv[j].astype(F32)

    total = lax.fori_loop(1, N, lat_take, total)

    def column(b):
        return jnp.where(b < 64, 2 * b, 2 * b - 127)

    to_halves = jnp.where(iota((128, 128), 0) == column(iota((128, 128), 1)), 1.0, 0.0).astype(BF16)
    to_columns = jnp.where(iota((128, 128), 1) == column(iota((128, 128), 0)), 1.0, 0.0).astype(BF16)

    def from_right(v):
        lane = iota(v.shape, 1)
        v = jnp.where(lane < 64, pltpu.roll(v, 64, 1), pltpu.roll(v, 63, 1))
        return jnp.where(lane == 127, 0.0, v)

    def from_left(v):
        lane = iota(v.shape, 1)
        v = jnp.where(lane < 64, pltpu.roll(v, 65, 1), pltpu.roll(v, 64, 1))
        return jnp.where(lane == 0, 0.0, v)

    lat = dot(total.astype(BF16), to_halves)
    for i, t in enumerate((from_left(lat), lat, from_right(lat))):
        ls[i, 0:48, :] = t
        ls[i, 48:56, :] = jnp.zeros((8, 128), F32)

    def down(v):
        return jnp.where(iota(v.shape, 0) == 0, 0.0, pltpu.roll(v, 1, 0))

    def up(v):
        return jnp.where(iota(v.shape, 0) == 63, 0.0, pltpu.roll(v, 63, 0))

    def combine(m0, m1, m2, m3):
        return m0 + m1 + m2, m1 - m2 - m3

    def scatter(p0, p1, p2, p3):
        return p0, p1 - p2 - p3, p1 + p2 - p0, p3

    def hidden(r):
        at = slice(4 * r, 4 * r + 16)
        x48 = jnp.concatenate([ls[0, at, :], ls[1, at, :], ls[2, at, :]], axis=0)
        pre = dot(x48.T.astype(BF16), w48[...]) + bibuf[...]
        row = 8 * me - 1 + r
        half = jnp.where(jnp.logical_and(row >= 0, row < 128), 0.5, 0.0)
        sig = half * jnp.tanh(0.5 * pre) + half
        act = pre * sig
        s1[r * 128 : (r + 1) * 128, :] = sig + act * (1.0 - sig)
        return act

    acts = {}
    for p in range(4):
        for r in range(2 * p, 2 * p + 4):
            if r not in acts:
                acts[r] = hidden(r)
        d0, d1, d2, d3 = (acts[2 * p + i] for i in range(4))
        for qy, t in enumerate((d0 - d2, d1 + d2, d2 - d1, d1 - d3)):
            even, odd = t[0:64], t[64:128]
            for qx, u in enumerate((down(odd) - odd, even + odd, odd - even, even - up(even))):
                t3[4 * qy + qx, p * 64 : p * 64 + 64, :] = u.astype(BF16)

    HALF = 512 // 2

    def channels(n):
        return slice(n * HALF, (n + 1) * HALF)

    def forward(n, qy):
        for qx in range(4):
            mm[n % 2, 4 * qy + qx] = dot_nt(t3[4 * qy + qx], taps(qy, qx, channels(n), slice(None)))

    def mixed(n, p):
        at, ch = slice(p * 64, p * 64 + 64), channels(n)
        grads = []
        sums = [combine(*(mm[n % 2, 4 * qy + qx, at, :] for qx in range(4))) for qy in range(4)]
        for side in range(2):
            m0, m1, m2, m3 = (pair[side] for pair in sums)
            out = []
            for pre in combine(m0, m1 + bmbuf[:, ch], m2, m3):
                sig = 0.5 * jnp.tanh(0.5 * pre) + 0.5
                out.append(hbuf[:, ch] * (sig + (pre * sig) * (1.0 - sig)))
            g0, g1 = out
            grads.append((g0, g0 + g1, g0 - g1, g1))
        for qy in range(4):
            even, odd = grads[0][qy], grads[1][qy]
            for qx, u in enumerate((even, even + odd, even - odd, odd)):
                x3[4 * qy + qx, at, ch] = u.astype(BF16)

    for n in range(2):
        for qy in range(4):
            forward(n, qy)
            if n > 0:
                mixed(n - 1, qy)
    for p in range(4):
        mixed(2 - 1, p)

    lacc[...] = jnp.zeros((56, 128), F32)

    def latent_rows(n, r, val):
        at, ch = slice(r * 128, (r + 1) * 128), channels(n)
        gbuf[at, ch] = (val * s1[at, ch]).astype(BF16)

    def finish(n, r, p0, p1, p2, p3):
        c0, c1, c2, c3 = scatter(p0, p1, p2, p3)
        latent_rows(n, r, jnp.concatenate([c1 + down(c3), c2 + up(c0)], axis=0))

    def backward(n, qy):
        for qx in range(4):
            mm[n % 2, 4 * qy + qx] = dot(x3[4 * qy + qx], taps(qy, qx, slice(None), channels(n)))

    def give(n, p, carry):
        at = slice(p * 64, p * 64 + 64)
        given = [scatter(*(mm[n % 2, 4 * qy + qx, at, :] for qy in range(4))) for qx in range(4)]
        if carry is not None:
            given = [(g[0] + c[0], g[1] + c[1], g[2], g[3]) for g, c in zip(given, carry)]
        finish(n, 2 * p, *(g[0] for g in given))
        finish(n, 2 * p + 1, *(g[1] for g in given))
        carry = [(g[2], g[3]) for g in given]
        if p == 3:
            finish(n, 8, *(c[0] for c in carry))
            finish(n, 9, *(c[1] for c in carry))
        return carry

    carry = None
    for n in range(2):
        for qy in range(4):
            backward(n, qy)
            if n > 0:
                carry = give(n - 1, qy, carry)
        carry = None
    for p in range(4):
        carry = give(2 - 1, p, carry)
    lat_parts = dot_nt(w48[...], gbuf[...])
    for r in range(10):
        q = lat_parts[:, r * 128 : (r + 1) * 128]
        at = slice(4 * r, 4 * r + 16)
        lacc[at, :] = lacc[at, :] + (q[16:32] + from_right(q[0:16]) + from_left(q[32:48]))
    ngblk[...] = dot((-ratio * lacc[0:48, :]).astype(BF16), to_columns).astype(BF16)

    def ng_copy(peer, slot):
        return pltpu.make_async_remote_copy(
            src_ref=ngblk,
            dst_ref=grecv.at[slot],
            send_sem=gsend_sem.at[peer],
            recv_sem=grecv_sem.at[slot],
            device_id={"mp": peer},
            device_id_type=MESH,
        )

    def ng_take(j):
        peer = lax.rem(me + j, N)
        ng_copy(peer, peer).wait_recv()

    for peer in mp_peers:
        ng_copy(peer, me).start()
    grecv[me] = ngblk[...]
    ns[:, 0:8, :] = jnp.zeros((3, 8, 128), F32)
    ns[:, 512:528, :] = jnp.zeros((3, 16, 128), F32)
    each(1, N, ng_take)

    def shift(s, c):
        at = pl.ds(4 + 32 * s, 32)
        v = grecv[s].astype(F32)
        above = jnp.where(s > 0, grecv[jnp.maximum(s - 1, 0), 40 - 8 : 48].astype(F32)[8:16], 0.0)
        below = jnp.where(s < N - 1, grecv[jnp.minimum(s + 1, N - 1), 0:16].astype(F32)[0:8], 0.0)
        v = jnp.concatenate([v[8:16] + above, v[16:32], v[32:40] + below], axis=0)
        ns[0, at, :] = left(v)
        ns[1, at, :] = v
        ns[2, at, :] = right(v)
        return c

    lax.fori_loop(0, N, shift, 0, unroll=16)

    def columns(b, acc):
        parts = []
        for i in range(CHUNK // 128):
            at = pl.ds(4 * (b * (CHUNK // 128) + i), 16)
            parts.append(jnp.concatenate([ns[k, at, :].astype(BF16) for k in range(3)], axis=0))
        block = jnp.concatenate(parts, axis=1)
        at = rows(b * CHUNK, CHUNK)
        im[:, at] = block
        return acc + dot_nt(f2[:, at], block)

    wg = lax.fori_loop(0, 16384 // CHUNK, columns, jnp.zeros((32, 48), F32), unroll=8)
    wg = jnp.concatenate([wg[0:24], jnp.zeros((24, 80), F32)], axis=1)
    lane = iota((24, 128), 1)
    ordered = jnp.zeros((24, 128), F32)
    for k in range(9):
        ky, kx = divmod(k, 3)
        moved = pltpu.roll(wg, (4 * k - kx * 16 - (2 - ky) * 4) % 128, 1)
        ordered = jnp.where(jnp.logical_and(lane >= 4 * k, lane < 4 * k + 4), moved, ordered)
    wrecv[my_dp] = ordered[0:8] + pltpu.roll(ordered[8:16], 40, 1) + pltpu.roll(ordered[16:24], 80, 1)

    def wg_copy(peer, slot):
        return pltpu.make_async_remote_copy(
            src_ref=wrecv.at[my_dp],
            dst_ref=wrecv.at[slot],
            send_sem=wsend_sem.at[peer],
            recv_sem=wrecv_sem.at[slot],
            device_id={"dp": peer},
            device_id_type=MESH,
        )

    def wg_take(j):
        peer = lax.rem(my_dp + j, N)
        wg_copy(peer, peer).wait_recv()

    for peer in dp_peers:
        wg_copy(peer, my_dp).start()

    e_cols = e48t[...].astype(BF16)

    def feature(b):
        p = dot(e_cols, im[:, rows(b * CHUNK, CHUNK)])
        for i in range(CHUNK // 128):
            stage[pl.ds(b * (CHUNK // 128) + i, 24, stride=STRIDE), :] = p[0:24, i * 128 : (i + 1) * 128]

    each(0, 16384 // CHUNK, feature, 16)
    for c in range(20):
        fg_out[0, c] = stage[c * STRIDE : c * STRIDE + 128, :].astype(BF16)
    def sent(j):
        lat_copy(lax.rem(me + j, N), j).wait_send()
        ng_copy(lax.rem(me + j, N), me).wait_send()

    each(1, N, sent)
    each(1, N, wg_take)
    acc = wrecv[0]
    for s in range(1, N):
        acc = acc + wrecv[s]
    acc = acc * (1.0 / 16384.0)
    wg_out[0:8, :] = acc[:, 0:36]
    wg_out[8:16, :] = pltpu.roll(acc, 88, 1)[:, 0:36]
    wg_out[16:20, :] = pltpu.roll(acc, 48, 1)[0:4, 0:36]
    each(1, N, lambda j: wg_copy(lax.rem(my_dp + j, N), my_dp).wait_send())


def publish(fg, wg, fg_out, wg_out, sem):
    copies = [pltpu.make_async_copy(fg, fg_out, sem.at[0]), pltpu.make_async_copy(wg, wg_out, sem.at[1])]
    for copy in copies:
        copy.start()
    for copy in copies:
        copy.wait()


def body(features, w_out, noisy_latent, timestep, w_in, b_in, w_mid, b_mid, reward_head):
    hbm = pl.BlockSpec(memory_space=pltpu.HBM)
    vmem = pl.BlockSpec(memory_space=pltpu.VMEM)
    dma = pltpu.SemaphoreType.DMA
    shapes = (jax.ShapeDtypeStruct((1, 20, 128, 128), BF16), jax.ShapeDtypeStruct((20, 36), F32))
    fg, wg = pl.pallas_call(
        kernel,
        out_shape=(pltpu.VMEM(shapes[0].shape, BF16), pltpu.VMEM(shapes[1].shape, F32)),
        in_specs=[hbm] * 10,
        out_specs=(vmem, vmem),
        scratch_shapes=[
            pltpu.VMEM((1, 20, 128, 128), BF16),
            pltpu.VMEM((20, 36), BF16),
            pltpu.VMEM((1, 4, 8, 128), F32),
            pltpu.SMEM((1,), jnp.int32),
            pltpu.VMEM((8, 128), F32),
            pltpu.VMEM((9, 4, 512), BF16),
            pltpu.VMEM((1, 512), F32),
            pltpu.VMEM((9, 512, 512), BF16),
            pltpu.VMEM((1, 512), F32),
            pltpu.VMEM((1, 512), F32),
            pltpu.VMEM((24 * STRIDE, 128), F32),
            pltpu.VMEM((32, 16384), BF16),
            pltpu.VMEM((130 * 16, 128), F32),
            pltpu.VMEM((528, 128), F32),
            pltpu.VMEM((32, 128), F32),
            pltpu.VMEM((528, 128), BF16),
            pltpu.VMEM((N, 48, 128), BF16),
            pltpu.VMEM((48, 32), F32),
            pltpu.VMEM((32, 48), F32),
            pltpu.VMEM((48, 512), BF16),
            pltpu.VMEM((3, 56, 128), F32),
            pltpu.VMEM((12, 512, 512), BF16),
            pltpu.VMEM((16, 256, 512), BF16),
            pltpu.VMEM((10 * 128, 512), F32),
            pltpu.VMEM((16, 256, 512), BF16),
            pltpu.VMEM((10 * 128, 512), BF16),
            pltpu.VMEM((2, 16, 256, 512 // 2), F32),
            pltpu.VMEM((56, 128), F32),
            pltpu.VMEM((48, 128), BF16),
            pltpu.VMEM((N, 48, 128), BF16),
            pltpu.VMEM((3, 528, 128), F32),
            pltpu.VMEM((48, 16384), BF16),
            pltpu.VMEM((N, 8, 128), F32),
            dma((10,)), dma((N,)), dma((N,)), dma((N,)), dma((N,)), dma((N,)), dma((N,)),
        ],
        compiler_params=pltpu.CompilerParams(collective_id=0, has_side_effects=True, vmem_limit_bytes=56 << 20),
        name="step",
    )(
        features, w_out, noisy_latent, timestep, jnp.asarray(noise_table()), w_in.transpose(0, 2, 1),
        b_in.reshape(1, 512), w_mid, b_mid.reshape(1, 512), reward_head.reshape(1, 512),
    )
    return pl.pallas_call(
        publish,
        out_shape=shapes,
        in_specs=[vmem, vmem],
        out_specs=(hbm, hbm),
        scratch_shapes=[dma((2,))],
        compiler_params=pltpu.CompilerParams(vmem_limit_bytes=1 << 20),
        name="publish",
    )(fg, wg)


def solution(mesh):
    in_specs = (
        P("dp", "mp", None, None), P("mp", None), P("dp", None, "mp", None), P("dp"), P(), P(), P(), P(), P(),
    )
    out_specs = (P("dp", "mp", None, None), P("mp", None))
    return jax.shard_map(body, mesh=mesh, in_specs=in_specs, out_specs=out_specs, check_vma=False)
```
